32 devices in a mesh: dp: 16 (over z, x, core), fsdp: 2 (over y).
Axes of the slice: x: 2, y: 2, z: 4, core: 2. Of those that a mesh axis runs over, the one named last changes fastest.
Arguments:
- enc_tokens: bfloat16 [32768, 768], P(('dp', 'fsdp')), may hold values from -6 to 6
- dec_tokens: bfloat16 [8192, 768], P(('dp', 'fsdp')), may hold values from -6 to 6
- enc_segments: int32 [32768], P(('dp', 'fsdp')), may hold values from -1 to 15, as said below
- dec_segments: int32 [8192], P(('dp', 'fsdp')), may hold values from -1 to 15, as said below
- enc_upstream: bfloat16 [32768, 768], P(('dp', 'fsdp')), may hold values from -6 to 6
- dec_upstream: bfloat16 [8192, 768], P(('dp', 'fsdp')), may hold values from -6 to 6
- encoder_query: bfloat16 [768, 768], P('fsdp'), may hold values from -0.0546875 to 0.0546875
- encoder_keyval: bfloat16 [768, 1536], P('fsdp'), may hold values from -0.21875 to 0.21875
- encoder_proj: bfloat16 [768, 768], P('fsdp'), may hold values from -0.625 to 0.625
- encoder_inner: bfloat16 [768, 3072], P('fsdp'), may hold values from -0.21875 to 0.21875
- encoder_outer: bfloat16 [3072, 768], P('fsdp'), may hold values from -0.109375 to 0.109375
- encoder_gains: bfloat16 [768, 2], P('fsdp'), may hold values from 0.5 to 1.5
- encoder_table: bfloat16 [32, 12], P('fsdp'), may hold values from -4 to 4
- decoder_query: bfloat16 [768, 768], P('fsdp'), may hold values from -0.0546875 to 0.0546875
- decoder_keyval: bfloat16 [768, 1536], P('fsdp'), may hold values from -0.21875 to 0.21875
- decoder_proj: bfloat16 [768, 768], P('fsdp'), may hold values from -0.625 to 0.625
- cross_query: bfloat16 [768, 768], P('fsdp'), may hold values from -0.0390625 to 0.0390625
- cross_keyval: bfloat16 [768, 1536], P('fsdp'), may hold values from -0.21875 to 0.21875
- cross_proj: bfloat16 [768, 768], P('fsdp'), may hold values from -0.625 to 0.625
- decoder_inner: bfloat16 [768, 3072], P('fsdp'), may hold values from -0.21875 to 0.21875
- decoder_outer: bfloat16 [3072, 768], P('fsdp'), may hold values from -0.109375 to 0.109375
- decoder_gains: bfloat16 [768, 3], P('fsdp'), may hold values from 0.5 to 1.5
- decoder_table: bfloat16 [32, 12], P('fsdp'), may hold values from -4 to 4
Outputs:
- enc_result: bfloat16 [32768, 768], P(('dp', 'fsdp'))
- dec_result: bfloat16 [8192, 768], P(('dp', 'fsdp'))
- enc_tokens_grad: float32 [32768, 768], P(('dp', 'fsdp'))
- dec_tokens_grad: float32 [8192, 768], P(('dp', 'fsdp'))
- encoder_query_grad: float32 [768, 768], P(('dp', 'fsdp'))
- encoder_keyval_grad: float32 [768, 1536], P(('dp', 'fsdp'))
- encoder_proj_grad: float32 [768, 768], P(('dp', 'fsdp'))
- encoder_inner_grad: float32 [768, 3072], P(('dp', 'fsdp'))
- encoder_outer_grad: float32 [3072, 768], P(('dp', 'fsdp'))
- encoder_gains_grad: float32 [768, 2], P(('dp', 'fsdp'))
- encoder_table_grad: float32 [32, 12], replicated
- decoder_query_grad: float32 [768, 768], P(('dp', 'fsdp'))
- decoder_keyval_grad: float32 [768, 1536], P(('dp', 'fsdp'))
- decoder_proj_grad: float32 [768, 768], P(('dp', 'fsdp'))
- cross_query_grad: float32 [768, 768], P(('dp', 'fsdp'))
- cross_keyval_grad: float32 [768, 1536], P(('dp', 'fsdp'))
- cross_proj_grad: float32 [768, 768], P(('dp', 'fsdp'))
- decoder_inner_grad: float32 [768, 3072], P(('dp', 'fsdp'))
- decoder_outer_grad: float32 [3072, 768], P(('dp', 'fsdp'))
- decoder_gains_grad: float32 [768, 3], P(('dp', 'fsdp'))
- decoder_table_grad: float32 [32, 12], replicated
The draws below stay inside these ranges and needn't reach their ends.
Inputs may be any that keep to these rules, and one draw needn't show every extreme that they name: `enc_segments`: in each block of 1024 rows (the rows of one device) the sequences stand whole and back to back from the block's first row, numbered 0, 1, 2, ... in order, at most 16 of them, followed by padding rows marked -1; every block ends with at least one padding row. `dec_segments`: in each block of 256 rows the decoder targets of the same device's sequences stand back to back from the block's first row, with the same numbers in the same order, each sequence with one row or more, followed by padding rows marked -1.
All inputs are finite; a program needn't handle non-finite values.
Results may differ from the reference program's by a relative error of at most 0.025.
The reference program's roundings to bfloat16 on the way count: a program that leaves them out, or rounds other values in their place, can miss the bound.
Values may be sent and summed in bfloat16 or wider, within the bound.
A program may use at most 384 MiB of HBM per device.

```python
import math
import jax
import jax.numpy as jnp
from jax import lax

D = 768
H = 12
HD = 64
FF = 3072
NB = 32
SLOTS = 16
ENC_DEV = 1024
DEC_DEV = 256
GROUPS = 32
ENC_ROWS = 32768
DEC_ROWS = 8192


def seq_layout(key):
    folded = jax.random.fold_in(key, 7)
    first_key, second_key = jax.random.split(folded)
    offset = jax.random.randint(first_key, (), 0, 4)
    device = jnp.arange(GROUPS, dtype=jnp.int32)
    bucket_level = (device + offset) % 4
    seq_count = jnp.left_shift(jnp.int32(1), 4 - bucket_level)
    longest = ENC_DEV // seq_count
    random_bits = jax.random.randint(second_key, (GROUPS, SLOTS), 0, 1 << 20)
    shorten = 1 + random_bits % (longest[:, None] // 2)
    active = jnp.arange(SLOTS, dtype=jnp.int32)[None, :] < seq_count[:, None]
    enc_lengths = jnp.where(active, longest[:, None] - shorten, 0)
    dec_lengths = jnp.where(active, jnp.maximum(1, enc_lengths // 4), 0)
    return (enc_lengths, dec_lengths)


def segment_ids(lengths, row_count):
    finish = jnp.cumsum(lengths, axis=1)
    starts = finish - lengths
    position = jnp.arange(row_count, dtype=jnp.int32)
    inside = (position[None, None, :] >= starts[:, :, None]) & (position[None, None, :] < finish[:, :, None])
    number = jnp.arange(SLOTS, dtype=jnp.int32)[None, :, None] + 1
    labels = jnp.sum(jnp.where(inside, number, 0), axis=1) - 1
    return labels.reshape(-1).astype(jnp.int32)


def draw_enc_segments(key, part):
    enc_lengths, dec_lengths = seq_layout(key)
    return segment_ids(enc_lengths, ENC_DEV)


def draw_dec_segments(key, part):
    enc_lengths, dec_lengths = seq_layout(key)
    return segment_ids(dec_lengths, DEC_DEV)


def block_scale(stream_key, dims, pieces, smallest, top_value):
    level = 1.0
    for dim, shards_of in pieces:
        heights = jax.random.uniform(jax.random.fold_in(jax.random.fold_in(stream_key, 6), dim), (shards_of,), jnp.float32, smallest / len(pieces), top_value / len(pieces))
        level = level * jnp.repeat(jnp.exp(heights), dims[dim] // shards_of).reshape((-1,) + (1,) * (len(dims) - 1 - dim))
    return level


def bell_draw(stream_key, extent, deviation, most, pieces=(), held_as=jnp.bfloat16):
    entries = jax.random.normal(stream_key, extent, jnp.float32) * deviation
    if len(pieces) > 0:
        entries = block_scale(stream_key, extent, pieces, -0.22, 0.18) * entries
    return jnp.clip(entries, min=-most, max=most).astype(held_as)


def setup_inputs(seed: int = 0) -> dict:
    streams_of = jax.random.split(jax.random.key(seed), 24)
    enc_tokens = bell_draw(streams_of[0], (ENC_ROWS, D), 1.0, 6.0, ((0, 32),))
    dec_tokens = bell_draw(streams_of[1], (DEC_ROWS, D), 1.0, 6.0, ((0, 32),))
    enc_segments = draw_enc_segments(jax.random.fold_in(streams_of[23], 71), 0)
    dec_segments = draw_dec_segments(jax.random.fold_in(streams_of[23], 71), 0)
    enc_upstream = bell_draw(streams_of[4], (ENC_ROWS, D), 1.0, 6.0, ((0, 32),))
    dec_upstream = bell_draw(streams_of[5], (DEC_ROWS, D), 1.0, 6.0, ((0, 32),))
    encoder_query = bell_draw(streams_of[6], (D, D), (16 * D) ** -0.5, 0.0546875, ((0, 2),))
    encoder_keyval = bell_draw(streams_of[7], (D, 2 * D), D ** -0.5, 0.21875, ((0, 2),))
    encoder_proj = bell_draw(streams_of[8], (D, D), (D // 8) ** -0.5, 0.625, ((0, 2),))
    encoder_inner = bell_draw(streams_of[9], (D, FF), D ** -0.5, 0.21875, ((0, 2),))
    encoder_outer = bell_draw(streams_of[10], (FF, D), FF ** -0.5, 0.109375, ((0, 2),))
    encoder_gains = jnp.clip(1.0 + 0.1 * jax.random.normal(streams_of[11], (D, 2), jnp.float32), 0.5, 1.5).astype(jnp.bfloat16)
    encoder_table = bell_draw(streams_of[12], (NB, H), 1.0, 4.0, ((0, 2),))
    decoder_query = bell_draw(streams_of[13], (D, D), (16 * D) ** -0.5, 0.0546875, ((0, 2),))
    decoder_keyval = bell_draw(streams_of[14], (D, 2 * D), D ** -0.5, 0.21875, ((0, 2),))
    decoder_proj = bell_draw(streams_of[15], (D, D), (D // 8) ** -0.5, 0.625, ((0, 2),))
    cross_query = bell_draw(streams_of[16], (D, D), (32 * D) ** -0.5, 0.0390625, ((0, 2),))
    cross_keyval = bell_draw(streams_of[17], (D, 2 * D), D ** -0.5, 0.21875, ((0, 2),))
    cross_proj = bell_draw(streams_of[18], (D, D), (D // 8) ** -0.5, 0.625, ((0, 2),))
    decoder_inner = bell_draw(streams_of[19], (D, FF), D ** -0.5, 0.21875, ((0, 2),))
    decoder_outer = bell_draw(streams_of[20], (FF, D), FF ** -0.5, 0.109375, ((0, 2),))
    decoder_gains = jnp.clip(1.0 + 0.1 * jax.random.normal(streams_of[21], (D, 3), jnp.float32), 0.5, 1.5).astype(jnp.bfloat16)
    decoder_table = bell_draw(streams_of[22], (NB, H), 1.0, 4.0, ((0, 2),))
    return dict(enc_tokens=enc_tokens, dec_tokens=dec_tokens, enc_segments=enc_segments, dec_segments=dec_segments, enc_upstream=enc_upstream, dec_upstream=dec_upstream, encoder_query=encoder_query, encoder_keyval=encoder_keyval, encoder_proj=encoder_proj, encoder_inner=encoder_inner, encoder_outer=encoder_outer, encoder_gains=encoder_gains, encoder_table=encoder_table, decoder_query=decoder_query, decoder_keyval=decoder_keyval, decoder_proj=decoder_proj, cross_query=cross_query, cross_keyval=cross_keyval, cross_proj=cross_proj, decoder_inner=decoder_inner, decoder_outer=decoder_outer, decoder_gains=decoder_gains, decoder_table=decoder_table)


@jax.custom_vjp
def low(v):
    return lax.optimization_barrier(v.astype(jnp.bfloat16)).astype(jnp.float32)

@jax.custom_vjp
def low_back(v):
    return v

def low_keep(v):
    return (low(v), None)

def low_pass(kept, grad):
    return (grad,)

def back_keep(v):
    return (v, None)

def back_low(kept, grad):
    return (low(grad),)
low.defvjp(low_keep, low_pass)
low_back.defvjp(back_keep, back_low)
EPSILON = 1e-06
MASKED = -1e+30
ENC_EDGES = (12, 16, 23, 32, 46, 64, 91)
DEC_EDGES = tuple((math.ceil(16 * 2 ** (3 * power / 16)) for power in range(1, 16)))

def encoder_bucket(query_places, key_places):
    distance = query_places[:, None] - key_places[None, :]
    reach = jnp.abs(distance)
    farther = 8 + sum(((reach >= threshold).astype(jnp.int32) for threshold in ENC_EDGES))
    return jnp.where(reach < 8, reach, farther) + 16 * (distance < 0).astype(jnp.int32)

def decoder_bucket(query_places, key_places):
    ahead = jnp.maximum(query_places[:, None] - key_places[None, :], 0)
    farther = 16 + sum(((ahead >= threshold).astype(jnp.int32) for threshold in DEC_EDGES))
    return jnp.where(ahead < 16, ahead, farther)

def lowered(value):
    return low(low_back(value))

def matmul(former, latter):
    return jnp.dot(former, latter, precision=lax.Precision.HIGHEST)

def norm_rows(stream, norm_gain):
    return stream * lax.rsqrt(lax.optimization_barrier(jnp.mean(stream * stream, axis=-1, keepdims=True)) + EPSILON) * norm_gain

def split_heads(matrix):
    return matrix.reshape(matrix.shape[0], H, HD)

def attention(queries, key_heads, value_heads, bias, allowed):
    raw_scores = jnp.einsum('qhd,khd->hqk', queries, key_heads, precision=lax.Precision.HIGHEST)
    scores = low_back(raw_scores) + bias
    scores = jnp.where(allowed[None], scores, MASKED)
    weights = low(jax.nn.softmax(scores, axis=-1))
    return jnp.einsum('hqk,khd->qhd', weights, value_heads, precision=lax.Precision.HIGHEST)

def attention_sublayer(stream, norm_gain, wquery, wkeyval, wproj, bias, allowed, memory):
    normed = low(norm_rows(stream, norm_gain))
    source = normed if memory is None else memory
    queries = lowered(matmul(normed, wquery))
    keyval = lowered(matmul(source, wkeyval))
    features = wquery.shape[1]
    mixture = attention(split_heads(queries), split_heads(keyval[:, :features]), split_heads(keyval[:, features:]), bias, allowed)
    mixture = lowered(mixture.reshape(mixture.shape[0], features))
    return low_back(matmul(mixture, wproj))

def ffn_sublayer(stream, norm_gain, winner, wouter):
    normed = low(norm_rows(stream, norm_gain))
    before = low_back(matmul(normed, winner))
    hidden = low(jax.nn.gelu(before, approximate=True))
    return low_back(matmul(hidden, wouter))

def encoder_block(stream, labels, layer_weights):
    wquery, wkeyval, wproj, winner, wouter, gains, table = layer_weights
    places = jnp.arange(stream.shape[0], dtype=jnp.int32)
    bias = jnp.take(table.T, encoder_bucket(places, places), axis=1)
    allowed = labels[:, None] == labels[None, :]
    middle = stream + attention_sublayer(stream, gains[:, 0], wquery, wkeyval, wproj, bias, allowed, None)
    return middle + ffn_sublayer(middle, gains[:, 1], winner, wouter)

def decoder_block(stream, labels, memory, enc_labels, layer_weights):
    wquery, wkeyval, wproj, cquery, ckeyval, cproj, winner, wouter, gains, table = layer_weights
    places = jnp.arange(stream.shape[0], dtype=jnp.int32)
    bias = jnp.take(table.T, decoder_bucket(places, places), axis=1)
    allowed = (labels[:, None] == labels[None, :]) & (places[None, :] <= places[:, None])
    after_self = stream + attention_sublayer(stream, gains[:, 0], wquery, wkeyval, wproj, bias, allowed, None)
    cross_allowed = labels[:, None] == enc_labels[None, :]
    after_cross = after_self + attention_sublayer(after_self, gains[:, 1], cquery, ckeyval, cproj, 0.0, cross_allowed, memory)
    return after_cross + ffn_sublayer(after_cross, gains[:, 2], winner, wouter)

def reference(enc_tokens, dec_tokens, enc_segments, dec_segments, enc_upstream, dec_upstream, encoder_query, encoder_keyval, encoder_proj, encoder_inner, encoder_outer, encoder_gains, encoder_table, decoder_query, decoder_keyval, decoder_proj, cross_query, cross_keyval, cross_proj, decoder_inner, decoder_outer, decoder_gains, decoder_table):
    enc_params = tuple((weight.astype(jnp.float32) for weight in (encoder_query, encoder_keyval, encoder_proj, encoder_inner, encoder_outer, encoder_gains, encoder_table)))
    dec_params = tuple((weight.astype(jnp.float32) for weight in (decoder_query, decoder_keyval, decoder_proj, cross_query, cross_keyval, cross_proj, decoder_inner, decoder_outer, decoder_gains, decoder_table)))
    inputs = (enc_tokens.astype(jnp.float32).reshape(GROUPS, ENC_DEV, D), dec_tokens.astype(jnp.float32).reshape(GROUPS, DEC_DEV, D), enc_segments.reshape(GROUPS, ENC_DEV), dec_segments.reshape(GROUPS, DEC_DEV), enc_upstream.astype(jnp.float32).reshape(GROUPS, ENC_DEV, D), dec_upstream.astype(jnp.float32).reshape(GROUPS, DEC_DEV, D))

    def group_step(running, element):
        enc_stream, dec_stream, enc_labels, dec_labels, enc_arriving, dec_arriving = element

        def forward(enc_set, dec_set, enc_value, dec_value):
            enc_final = encoder_block(enc_value, enc_labels, enc_set)
            memory = low(enc_final)
            dec_final = decoder_block(dec_value, dec_labels, memory, enc_labels, dec_set)
            return (enc_final, dec_final)
        outputs, pullback = jax.vjp(forward, enc_params, dec_params, enc_stream, dec_stream)
        enc_live = (enc_labels >= 0).astype(jnp.float32)[:, None]
        dec_live = (dec_labels >= 0).astype(jnp.float32)[:, None]
        enc_back, dec_back, enc_grad, dec_grad = pullback((enc_arriving * enc_live, dec_arriving * dec_live))
        running = jax.tree.map(jnp.add, running, (enc_back, dec_back))
        return (running, (outputs[0].astype(jnp.bfloat16), outputs[1].astype(jnp.bfloat16), enc_grad, dec_grad))
    initial = jax.tree.map(jnp.zeros_like, (enc_params, dec_params))
    (enc_sums, dec_sums), stacked = lax.scan(group_step, initial, inputs)
    enc_result = stacked[0].reshape(ENC_ROWS, D)
    dec_result = stacked[1].reshape(DEC_ROWS, D)
    enc_grad = stacked[2].reshape(ENC_ROWS, D)
    dec_grad = stacked[3].reshape(DEC_ROWS, D)
    return (enc_result, dec_result, enc_grad, dec_grad, enc_sums[0], enc_sums[1], enc_sums[2], enc_sums[3], enc_sums[4], enc_sums[5], enc_sums[6], dec_sums[0], dec_sums[1], dec_sums[2], dec_sums[3], dec_sums[4], dec_sums[5], dec_sums[6], dec_sums[7], dec_sums[8], dec_sums[9])
```

```python
import functools
import math

import jax
import jax.numpy as jnp
from jax import lax
from jax.experimental import pallas as pl
from jax.experimental.pallas import tpu as pltpu
from jax.sharding import PartitionSpec as P

H = 12
HD = 64
NB = 32
TILE = 128
BAND = 5
EPSILON = 1e-06
MASKED = -1e30
ENC_EDGES = (12, 16, 23, 32, 46, 64, 91)
DEC_EDGES = tuple((math.ceil(16 * 2 ** (3 * power / 16)) for power in range(1, 16)))
PADDING_LABEL = 1 << 20


def encoder_bucket(distance):
    reach = jnp.abs(distance)
    farther = 8 + sum(((reach >= threshold).astype(jnp.int32) for threshold in ENC_EDGES))
    return jnp.where(reach < 8, reach, farther) + 16 * (distance < 0).astype(jnp.int32)


def decoder_bucket(distance):
    ahead = jnp.maximum(distance, 0)
    farther = 16 + sum(((ahead >= threshold).astype(jnp.int32) for threshold in DEC_EDGES))
    return jnp.where(ahead < 16, ahead, farther)


def band_onehot(bucket_of):
    shape = (NB, BAND, TILE, TILE)
    step = lax.broadcasted_iota(jnp.int32, shape, 1) - 2
    key = lax.broadcasted_iota(jnp.int32, shape, 2)
    query = lax.broadcasted_iota(jnp.int32, shape, 3)
    bucket = bucket_of(step * TILE + query - key)
    return (bucket == lax.broadcasted_iota(jnp.int32, shape, 0)).reshape(NB, BAND * TILE * TILE)


def band_bias(table, bucket_of):
    onehot = band_onehot(bucket_of).astype(jnp.bfloat16)
    flat = lax.dot_general(
        table, onehot, (((0,), (0,)), ((), ())), preferred_element_type=jnp.float32
    )
    return flat.reshape(H, BAND, TILE, TILE)


def band_table_grad(band, bucket_of):
    onehot = band_onehot(bucket_of).astype(jnp.float32)
    return lax.dot_general(
        onehot,
        band.reshape(H, BAND * TILE * TILE),
        (((1,), (1,)), ((), ())),
        precision=lax.Precision.HIGHEST,
        preferred_element_type=jnp.float32,
    )


def key_bounds(query_labels, key_labels, query_rows, key_rows):
    queries = jnp.where(query_labels < 0, PADDING_LABEL, query_labels).reshape(-1, query_rows)
    keys = jnp.where(key_labels < 0, PADDING_LABEL, key_labels)
    first = jnp.sum((keys[None, :] < queries[:, :1]).astype(jnp.int32), axis=1)
    last = jnp.sum((keys[None, :] <= queries[:, -1:]).astype(jnp.int32), axis=1)
    return jnp.stack([first // key_rows, (last + key_rows - 1) // key_rows])


def fold_rows(value, combine):
    rows = value.shape[0]
    while rows > 8:
        rows //= 2
        value = combine(value[:rows], value[rows:])
    return value


def head_parts(block):
    lane = lax.broadcasted_iota(jnp.int32, block.shape, 1)
    zero = jnp.zeros_like(block)
    return (jnp.where(lane < HD, block, zero), jnp.where(lane < HD, zero, block))


def flip(value):
    return value.astype(jnp.float32).T


def band_index(query_tile, key_tile):
    return jnp.clip(query_tile - key_tile, -2, 2) + 2


def tile_mask(spec, key_tile, query_block, segk_ref, segq_ref):
    rows, lanes = spec["kb"], spec["qb"]
    start = pl.multiple_of(key_tile * rows, rows)
    labels = segk_ref[pl.ds(start, rows), :]
    labels = jnp.concatenate([labels] * (lanes // TILE), axis=1)
    mask = labels == segq_ref[...]
    if spec["causal"]:
        key = lax.broadcasted_iota(jnp.int32, (rows, lanes), 0) + key_tile * rows
        query = lax.broadcasted_iota(jnp.int32, (rows, lanes), 1) + query_block * lanes
        mask = mask & (key <= query)
    return mask


def tile_bias(spec, head, key_tile, query_block, bias_ref):
    rows, lanes = spec["kb"] // TILE, spec["qb"] // TILE
    return jnp.concatenate(
        [
            jnp.concatenate(
                [
                    bias_ref[
                        head, band_index(query_block * lanes + lane, key_tile * rows + row)
                    ]
                    for lane in range(lanes)
                ],
                axis=1,
            )
            for row in range(rows)
        ],
        axis=0,
    )


def dot_rows(former, latter):
    return lax.dot_general(
        former, latter, (((1,), (1,)), ((), ())), preferred_element_type=jnp.float32
    )


def dot_plain(former, latter):
    return jnp.dot(former, latter, preferred_element_type=jnp.float32)


def forward_kernel(spec, bounds_ref, q_ref, k_ref, v_ref, segq_ref, segk_ref, *rest):
    bias_ref, rest = (rest[0], rest[1:]) if spec["bias"] else (None, rest)
    o_ref, lse_ref, score_ref, vt_ref = rest
    kb, qb = spec["kb"], spec["qb"]
    block = pl.program_id(1)

    @pl.when(block == 0)
    def _():
        vt_ref[...] = flip(v_ref[...]).astype(jnp.bfloat16)

    parts = head_parts(q_ref[...])
    first, last = bounds_ref[0, block], bounds_ref[1, block]

    def score(tile, highest):
        start = pl.multiple_of(tile * kb, kb)
        keys = k_ref[pl.ds(start, kb), :]
        mask = tile_mask(spec, tile, block, segk_ref, segq_ref)
        fresh = []
        for head in range(2):
            s = dot_rows(keys, parts[head])
            if spec["bias"]:
                s = s + tile_bias(spec, head, tile, block, bias_ref)
            s = jnp.where(mask, s, MASKED)
            score_ref[head, pl.ds(start, kb), :] = s
            fresh.append(jnp.maximum(highest[head], fold_rows(s, jnp.maximum)))
        return tuple(fresh)

    low = jnp.full((8, qb), MASKED, jnp.float32)
    highest = lax.fori_loop(first, last, score, (low, low))
    top = [jnp.max(value, axis=0, keepdims=True) for value in highest]

    def exponent(tile, summed):
        start = pl.multiple_of(tile * kb, kb)
        fresh = []
        for head in range(2):
            e = jnp.exp(score_ref[head, pl.ds(start, kb), :] - top[head])
            score_ref[head, pl.ds(start, kb), :] = e
            fresh.append(summed[head] + fold_rows(e, jnp.add))
        return tuple(fresh)

    none = jnp.zeros((8, qb), jnp.float32)
    summed = lax.fori_loop(first, last, exponent, (none, none))
    total = [jnp.sum(value, axis=0, keepdims=True) for value in summed]
    scale = [1.0 / value for value in total]

    def mix(tile, mixed):
        start = pl.multiple_of(tile * kb, kb)
        fresh = []
        for head in range(2):
            weights = (score_ref[head, pl.ds(start, kb), :] * scale[head]).astype(jnp.bfloat16)
            values = vt_ref[pl.ds(head * HD, HD), pl.ds(start, kb)]
            fresh.append(mixed[head] + dot_plain(values, weights))
        return tuple(fresh)

    nothing = jnp.zeros((HD, qb), jnp.float32)
    mixed = lax.fori_loop(first, last, mix, (nothing, nothing))
    o_ref[...] = flip(jnp.concatenate(mixed, axis=0)).astype(jnp.bfloat16)
    lse_ref[0] = jnp.concatenate(
        [top[head] + jnp.log(total[head]) for head in range(2)], axis=0
    )


def backward_kernel(
    spec, bounds_ref, q_ref, k_ref, v_ref, do_ref, lse_ref, segq_ref, segk_ref, *rest
):
    bias_ref, rest = (rest[0], rest[1:]) if spec["bias"] else (None, rest)
    dq_ref, dkv_ref, rest = rest[0], rest[1], rest[2:]
    band_ref, rest = (rest[0], rest[1:]) if spec["bias"] else (None, rest)
    p_ref, dp_ref, dk_ref, dv_ref, kt_ref = rest
    kb, qb = spec["kb"], spec["qb"]
    pair, block = pl.program_id(0), pl.program_id(1)

    @pl.when(block == 0)
    def _():
        kt_ref[...] = flip(k_ref[...]).astype(jnp.bfloat16)
        dk_ref[...] = jnp.zeros_like(dk_ref)
        dv_ref[...] = jnp.zeros_like(dv_ref)
        if spec["bias"]:
            band_ref[...] = jnp.zeros_like(band_ref)

    parts = head_parts(q_ref[...])
    dparts = head_parts(do_ref[...])
    lse = lse_ref[0]
    first, last = bounds_ref[0, block], bounds_ref[1, block]

    def weigh(tile, delta):
        start = pl.multiple_of(tile * kb, kb)
        keys = k_ref[pl.ds(start, kb), :]
        values = v_ref[pl.ds(start, kb), :]
        mask = tile_mask(spec, tile, block, segk_ref, segq_ref)
        fresh = []
        dvalues = dv_ref[pl.ds(start, kb), :]
        for head in range(2):
            s = dot_rows(keys, parts[head])
            if spec["bias"]:
                s = s + tile_bias(spec, head, tile, block, bias_ref)
            p = jnp.exp(jnp.where(mask, s, MASKED) - lse[head : head + 1])
            dp = dot_rows(values, dparts[head])
            p_ref[head, pl.ds(start, kb), :] = p
            dp_ref[head, pl.ds(start, kb), :] = dp
            fresh.append(delta[head] + fold_rows(p * dp, jnp.add))
            dvalues = dvalues + dot_plain(p.astype(jnp.bfloat16), dparts[head])
        dv_ref[pl.ds(start, kb), :] = dvalues
        return tuple(fresh)

    none = jnp.zeros((8, qb), jnp.float32)
    delta = lax.fori_loop(first, last, weigh, (none, none))
    delta = [jnp.sum(value, axis=0, keepdims=True) for value in delta]

    def pull(tile, dquery):
        start = pl.multiple_of(tile * kb, kb)
        fresh = []
        dkeys = dk_ref[pl.ds(start, kb), :]
        for head in range(2):
            ds = p_ref[head, pl.ds(start, kb), :] * (
                dp_ref[head, pl.ds(start, kb), :] - delta[head]
            )
            if spec["bias"]:
                rows, lanes = kb // TILE, qb // TILE
                for row in range(rows):
                    for lane in range(lanes):
                        index = band_index(block * lanes + lane, tile * rows + row)
                        band_ref[head, index] += ds[
                            row * TILE : (row + 1) * TILE, lane * TILE : (lane + 1) * TILE
                        ]
            low = ds.astype(jnp.bfloat16)
            dkeys = dkeys + dot_plain(low, parts[head])
            kt = kt_ref[pl.ds(head * HD, HD), pl.ds(start, kb)]
            fresh.append(dquery[head] + dot_plain(kt, low))
        dk_ref[pl.ds(start, kb), :] = dkeys
        return tuple(fresh)

    nothing = jnp.zeros((HD, qb), jnp.float32)
    dquery = lax.fori_loop(first, last, pull, (nothing, nothing))
    dq_ref[...] = flip(jnp.concatenate(dquery, axis=0)).astype(jnp.bfloat16)

    @pl.when(block == pl.num_programs(1) - 1)
    def _():
        column = pl.multiple_of(pair * 2 * HD, 2 * HD)
        dkv_ref[:, pl.ds(column, 2 * HD)] = dk_ref[...].astype(jnp.bfloat16)
        column = pl.multiple_of((pl.num_programs(0) + pair) * 2 * HD, 2 * HD)
        dkv_ref[:, pl.ds(column, 2 * HD)] = dv_ref[...].astype(jnp.bfloat16)


def attention_setup(queries, keyval, query_labels, key_labels, bias, causal):
    rows, keys = queries.shape[0], keyval.shape[0]
    qb, kb = min(256, rows), min(256, keys)
    spec = dict(qb=qb, kb=kb, causal=causal, bias=bias is not None)
    bounds = key_bounds(query_labels, key_labels, qb, kb)
    segq = query_labels[None, :]
    segk = jnp.broadcast_to(key_labels[:, None], (keys, TILE))
    pairs = H // 2
    in_specs = dict(
        q=pl.BlockSpec((qb, 2 * HD), lambda pair, block, bounds: (block, pair)),
        k=pl.BlockSpec((keys, 2 * HD), lambda pair, block, bounds: (0, pair)),
        v=pl.BlockSpec((keys, 2 * HD), lambda pair, block, bounds: (0, pairs + pair)),
        segq=pl.BlockSpec((1, qb), lambda pair, block, bounds: (0, block)),
        segk=pl.BlockSpec((keys, TILE), lambda pair, block, bounds: (0, 0)),
        lse=pl.BlockSpec((1, 2, qb), lambda pair, block, bounds: (pair, 0, block)),
        band=pl.BlockSpec(
            (2, BAND, TILE, TILE), lambda pair, block, bounds: (pair, 0, 0, 0)
        ),
        whole=pl.BlockSpec((keys, 4 * pairs * HD), lambda pair, block, bounds: (0, 0)),
    )
    return spec, bounds, segq, segk, in_specs, (pairs, rows // qb)


def attend_forward(queries, keyval, query_labels, key_labels, bias, causal):
    spec, bounds, segq, segk, specs, grid = attention_setup(
        queries, keyval, query_labels, key_labels, bias, causal
    )
    rows, keys = queries.shape[0], keyval.shape[0]
    work = H * rows * keys
    extra = ([specs["band"]], [bias]) if bias is not None else ([], [])
    return pl.pallas_call(
        functools.partial(forward_kernel, spec),
        out_shape=(
            jax.ShapeDtypeStruct((rows, H * HD), jnp.bfloat16),
            jax.ShapeDtypeStruct((H // 2, 2, rows), jnp.float32),
        ),
        grid_spec=pltpu.PrefetchScalarGridSpec(
            num_scalar_prefetch=1,
            grid=grid,
            in_specs=[specs["q"], specs["k"], specs["v"], specs["segq"], specs["segk"]]
            + extra[0],
            out_specs=[specs["q"], specs["lse"]],
            scratch_shapes=[
                pltpu.VMEM((2, keys, spec["qb"]), jnp.float32),
                pltpu.VMEM((2 * HD, keys), jnp.bfloat16),
            ],
        ),
        compiler_params=pltpu.CompilerParams(vmem_limit_bytes=40 << 20),
        cost_estimate=pl.CostEstimate(
            flops=16 * HD * work, transcendentals=work, bytes_accessed=8 << 20
        ),
    )(bounds, queries, keyval, keyval, segq, segk, *extra[1])


def attend_backward(queries, keyval, query_labels, key_labels, bias, causal, lse, dmixture):
    spec, bounds, segq, segk, specs, grid = attention_setup(
        queries, keyval, query_labels, key_labels, bias, causal
    )
    rows, keys = queries.shape[0], keyval.shape[0]
    work = H * rows * keys
    extra = ([specs["band"]], [bias]) if bias is not None else ([], [])
    band = (
        [jax.ShapeDtypeStruct((H, BAND, TILE, TILE), jnp.float32)] if bias is not None else []
    )
    out = pl.pallas_call(
        functools.partial(backward_kernel, spec),
        out_shape=[
            jax.ShapeDtypeStruct((rows, H * HD), jnp.bfloat16),
            jax.ShapeDtypeStruct((keys, 2 * H * HD), jnp.bfloat16),
        ]
        + band,
        grid_spec=pltpu.PrefetchScalarGridSpec(
            num_scalar_prefetch=1,
            grid=grid,
            in_specs=[
                specs["q"],
                specs["k"],
                specs["v"],
                specs["q"],
                specs["lse"],
                specs["segq"],
                specs["segk"],
            ]
            + extra[0],
            out_specs=[specs["q"], specs["whole"]] + extra[0],
            scratch_shapes=[
                pltpu.VMEM((2, keys, spec["qb"]), jnp.float32),
                pltpu.VMEM((2, keys, spec["qb"]), jnp.float32),
                pltpu.VMEM((keys, 2 * HD), jnp.float32),
                pltpu.VMEM((keys, 2 * HD), jnp.float32),
                pltpu.VMEM((2 * HD, keys), jnp.bfloat16),
            ],
        ),
        compiler_params=pltpu.CompilerParams(vmem_limit_bytes=48 << 20),
        cost_estimate=pl.CostEstimate(
            flops=40 * HD * work, transcendentals=work, bytes_accessed=16 << 20
        ),
    )(bounds, queries, keyval, keyval, dmixture, lse, segq, segk, *extra[1])
    return (out[0], out[1], out[2] if bias is not None else None)


def product(former, latter):
    return jnp.dot(former, latter, preferred_element_type=jnp.float32)


def transpose_product(former, latter):
    return lax.dot_general(
        former, latter, (((0,), (0,)), ((), ())), preferred_element_type=jnp.float32
    )


def product_transposed(former, latter):
    return lax.dot_general(
        former, latter, (((1,), (1,)), ((), ())), preferred_element_type=jnp.float32
    )


def smooth_gate(value):
    return jax.nn.gelu(value, approximate=True)


def norm_forward(stream, norm_gain):
    return (
        stream * lax.rsqrt(jnp.mean(stream * stream, axis=-1, keepdims=True) + EPSILON) * norm_gain
    )


def norm_backward(stream, norm_gain, gradient):
    outcome, pullback = jax.vjp(norm_forward, stream, norm_gain)
    return pullback(gradient)


def attention_forward(stream, norm_gain, wquery, wkeyval, wproj, layout, memory):
    normed = norm_forward(stream, norm_gain).astype(jnp.bfloat16)
    queries = product(normed, wquery).astype(jnp.bfloat16)
    source = normed if memory is None else memory
    keyval = product(source, wkeyval).astype(jnp.bfloat16)
    mixture, logsum = attend_forward(queries, keyval, *layout)
    return (stream + product(mixture, wproj), (normed, queries, keyval, mixture, logsum))


def attention_backward(stream, norm_gain, wquery, wkeyval, wproj, layout, memory, stored, gradient):
    normed, queries, keyval, mixture, logsum = stored
    gradient_low = gradient.astype(jnp.bfloat16)
    project_grad = transpose_product(mixture, gradient_low)
    dmixture = product_transposed(gradient_low, wproj).astype(jnp.bfloat16)
    dquery_low, dkeyval_low, band = attend_backward(queries, keyval, *layout, logsum, dmixture)
    source = normed if memory is None else memory
    query_grad = transpose_product(normed, dquery_low)
    keyval_grad = transpose_product(source, dkeyval_low)
    dnormed = product_transposed(dquery_low, wquery)
    dsource = product_transposed(dkeyval_low, wkeyval)
    if memory is None:
        dnormed = dnormed + dsource
        dsource = None
    dstream, dgain = norm_backward(stream, norm_gain, dnormed)
    return (gradient + dstream, dgain, query_grad, keyval_grad, project_grad, band, dsource)


def feed_forward(stream, norm_gain, winner, wouter):
    normed = norm_forward(stream, norm_gain).astype(jnp.bfloat16)
    before = product(normed, winner)
    hidden = smooth_gate(before).astype(jnp.bfloat16)
    return (stream + product(hidden, wouter), (normed, before, hidden))


def feed_backward(stream, norm_gain, winner, wouter, stored, gradient):
    normed, before, hidden = stored
    gradient_low = gradient.astype(jnp.bfloat16)
    outer_grad = transpose_product(hidden, gradient_low)
    dhidden = product_transposed(gradient_low, wouter)
    gate_value, gate_pullback = jax.vjp(smooth_gate, before)
    dbefore = gate_pullback(dhidden)[0].astype(jnp.bfloat16)
    inner_grad = transpose_product(normed, dbefore)
    dnormed = product_transposed(dbefore, winner)
    dstream, dgain = norm_backward(stream, norm_gain, dnormed)
    return (gradient + dstream, dgain, inner_grad, outer_grad)


def index_bits(devices):
    return devices.bit_length() - 1


def swap_pairs(devices, bit):
    return [(place, place ^ (1 << bit)) for place in range(devices)]


class Links:
    def __init__(self, mesh):
        self.sizes = dict(mesh.shape)
        self.bits = [("fsdp", bit) for bit in range(index_bits(self.sizes["fsdp"]))]
        self.bits += [("dp", bit) for bit in range(index_bits(self.sizes["dp"]))]

    def side(self, axis, bit):
        return (lax.axis_index(axis) >> bit) & 1

    def swap(self, value, axis, bit):
        return lax.ppermute(value, axis, swap_pairs(self.sizes[axis], bit))

    def gather(self, shard):
        rows, columns = shard.shape
        half = rows // 2
        core, place = self.side("dp", 0), lax.axis_index("fsdp")
        part = lax.dynamic_slice_in_dim(shard, core * half, half, 0)
        theirs = self.swap(part, "fsdp", 0)
        mate = self.swap(theirs, "dp", 0)
        whole = jnp.zeros((2 * rows, columns), shard.dtype)
        other = (1 - place) * rows
        whole = lax.dynamic_update_slice_in_dim(whole, shard, place * rows, 0)
        whole = lax.dynamic_update_slice_in_dim(whole, theirs, other + core * half, 0)
        return lax.dynamic_update_slice_in_dim(whole, mate, other + (1 - core) * half, 0)

    def gather_small(self, shard):
        other = self.swap(shard, "fsdp", 0)
        first = lax.axis_index("fsdp") == 0
        return jnp.concatenate(
            [jnp.where(first, shard, other), jnp.where(first, other, shard)], axis=0
        )

    def scatter(self, value, order, kept=jnp.bfloat16):
        rows, columns = value.shape
        shape = (2,) * len(self.bits) + (rows >> len(self.bits), columns)
        current = value.astype(kept).reshape(shape)
        left = list(reversed(self.bits))
        for step, key in enumerate(order):
            spot = left.index(key)
            side = self.side(*key)
            send = lax.dynamic_index_in_dim(current, 1 - side, spot, keepdims=False)
            mine = lax.dynamic_index_in_dim(current, side, spot, keepdims=False)
            arrived = self.swap(send, *key)
            current = mine.astype(jnp.float32) + arrived.astype(jnp.float32)
            if step < len(order) - 1:
                current = current.astype(kept)
            left.remove(key)
        return current

    def orders(self):
        core, row = ("dp", 0), ("fsdp", 0)
        rest = [key for key in self.bits if key not in (core, row)]
        across = rest[:1]
        return ([core] + across + [row] + rest[1:], [core, row] + rest)


def body(
    links,
    enc_tokens,
    dec_tokens,
    enc_segments,
    dec_segments,
    enc_upstream,
    dec_upstream,
    encoder_query,
    encoder_keyval,
    encoder_proj,
    encoder_inner,
    encoder_outer,
    encoder_gains,
    encoder_table,
    decoder_query,
    decoder_keyval,
    decoder_proj,
    cross_query,
    cross_keyval,
    cross_proj,
    decoder_inner,
    decoder_outer,
    decoder_gains,
    decoder_table,
):
    small = jnp.concatenate(
        [encoder_gains, decoder_gains]
        + [
            jnp.concatenate([encoder_table, decoder_table], axis=0).reshape(
                encoder_gains.shape[0], -1
            )
        ],
        axis=1,
    )
    small = links.gather_small(small)
    enc_gains = small[:, 0:2].astype(jnp.float32)
    dec_gains = small[:, 2:5].astype(jnp.float32)
    tables = small[:, 5:].reshape(2, 2, NB // 2, H)
    enc_bias = band_bias(tables[:, 0].reshape(NB, H), encoder_bucket)
    dec_bias = band_bias(tables[:, 1].reshape(NB, H), decoder_bucket)

    equery, ekeyval, eproj = (
        links.gather(w) for w in (encoder_query, encoder_keyval, encoder_proj)
    )
    einner, eouter = (links.gather(w) for w in (encoder_inner, encoder_outer))
    dquery, dkeyval, dproj = (
        links.gather(w) for w in (decoder_query, decoder_keyval, decoder_proj)
    )
    cquery, ckeyval, cproj = (links.gather(w) for w in (cross_query, cross_keyval, cross_proj))
    dinner, douter = (links.gather(w) for w in (decoder_inner, decoder_outer))

    enc_layout = (enc_segments, enc_segments, enc_bias, False)
    dec_layout = (dec_segments, dec_segments, dec_bias, True)
    cross_layout = (dec_segments, enc_segments, None, False)

    enc_stream = enc_tokens.astype(jnp.float32)
    enc_middle, enc_self = attention_forward(
        enc_stream, enc_gains[:, 0], equery, ekeyval, eproj, enc_layout, None
    )
    enc_final, enc_ffn = feed_forward(enc_middle, enc_gains[:, 1], einner, eouter)
    memory = enc_final.astype(jnp.bfloat16)

    dec_stream = dec_tokens.astype(jnp.float32)
    after_self, dec_self = attention_forward(
        dec_stream, dec_gains[:, 0], dquery, dkeyval, dproj, dec_layout, None
    )
    after_cross, dec_cross = attention_forward(
        after_self, dec_gains[:, 1], cquery, ckeyval, cproj, cross_layout, memory
    )
    dec_final, dec_ffn = feed_forward(after_cross, dec_gains[:, 2], dinner, douter)

    first, second = links.orders()

    dec_live = (dec_segments >= 0).astype(jnp.float32)[:, None]
    gradient = dec_upstream.astype(jnp.float32) * dec_live
    gradient, dgain_ffn, dinner_grad, douter_grad = feed_backward(
        after_cross, dec_gains[:, 2], dinner, douter, dec_ffn, gradient
    )
    dinner_share = links.scatter(dinner_grad, first)
    douter_share = links.scatter(douter_grad, second)
    gradient, dgain_cross, cquery_grad, ckeyval_grad, cproj_grad, _, memory_grad = (
        attention_backward(
            after_self,
            dec_gains[:, 1],
            cquery,
            ckeyval,
            cproj,
            cross_layout,
            memory,
            dec_cross,
            gradient,
        )
    )
    cproj_share = links.scatter(cproj_grad, first)
    cquery_share = links.scatter(cquery_grad, first)
    ckeyval_share = links.scatter(ckeyval_grad, second)
    dec_gradient, dgain_self, dquery_grad, dkeyval_grad, dproj_grad, dec_band, _ = (
        attention_backward(
            dec_stream,
            dec_gains[:, 0],
            dquery,
            dkeyval,
            dproj,
            dec_layout,
            None,
            dec_self,
            gradient,
        )
    )
    dproj_share = links.scatter(dproj_grad, first)
    dquery_share = links.scatter(dquery_grad, first)
    dkeyval_share = links.scatter(dkeyval_grad, second)

    enc_live = (enc_segments >= 0).astype(jnp.float32)[:, None]
    gradient = enc_upstream.astype(jnp.float32) * enc_live + memory_grad
    gradient, egain_ffn, einner_grad, eouter_grad = feed_backward(
        enc_middle, enc_gains[:, 1], einner, eouter, enc_ffn, gradient
    )
    einner_share = links.scatter(einner_grad, first)
    eouter_share = links.scatter(eouter_grad, second)
    enc_gradient, egain_self, equery_grad, ekeyval_grad, eproj_grad, enc_band, _ = (
        attention_backward(
            enc_stream,
            enc_gains[:, 0],
            equery,
            ekeyval,
            eproj,
            enc_layout,
            None,
            enc_self,
            gradient,
        )
    )
    eproj_share = links.scatter(eproj_grad, first)
    equery_share = links.scatter(equery_grad, first)
    ekeyval_share = links.scatter(ekeyval_grad, second)

    table_grads = jnp.concatenate(
        [
            band_table_grad(enc_band, encoder_bucket),
            band_table_grad(dec_band, decoder_bucket),
        ],
        axis=0,
    )
    columns = jnp.stack([egain_self, egain_ffn, dgain_self, dgain_cross, dgain_ffn], axis=1)
    wide = columns.shape[0]
    packed = jnp.concatenate(
        [columns, table_grads.reshape(wide, -1)], axis=1
    )
    packed = jnp.pad(packed, ((0, 0), (0, TILE - packed.shape[1])))
    small_share = links.scatter(packed, second, jnp.float32)
    tables_grad = lax.all_gather(small_share[:, 5:6], ("dp", "fsdp"), axis=0, tiled=True)
    tables_grad = tables_grad.reshape(2, NB, H)
    return (
        memory,
        dec_final.astype(jnp.bfloat16),
        enc_gradient,
        dec_gradient,
        equery_share,
        ekeyval_share,
        eproj_share,
        einner_share,
        eouter_share,
        small_share[:, 0:2],
        tables_grad[0],
        dquery_share,
        dkeyval_share,
        dproj_share,
        cquery_share,
        ckeyval_share,
        cproj_share,
        dinner_share,
        douter_share,
        small_share[:, 2:5],
        tables_grad[1],
    )


def solution(mesh):
    in_specs = (
        P(("dp", "fsdp"), None),
        P(("dp", "fsdp"), None),
        P(("dp", "fsdp")),
        P(("dp", "fsdp")),
        P(("dp", "fsdp"), None),
        P(("dp", "fsdp"), None),
        P("fsdp", None),
        P("fsdp", None),
        P("fsdp", None),
        P("fsdp", None),
        P("fsdp", None),
        P("fsdp", None),
        P("fsdp", None),
        P("fsdp", None),
        P("fsdp", None),
        P("fsdp", None),
        P("fsdp", None),
        P("fsdp", None),
        P("fsdp", None),
        P("fsdp", None),
        P("fsdp", None),
        P("fsdp", None),
        P("fsdp", None),
    )
    out_specs = (
        P(("dp", "fsdp"), None),
        P(("dp", "fsdp"), None),
        P(("dp", "fsdp"), None),
        P(("dp", "fsdp"), None),
        P(("dp", "fsdp"), None),
        P(("dp", "fsdp"), None),
        P(("dp", "fsdp"), None),
        P(("dp", "fsdp"), None),
        P(("dp", "fsdp"), None),
        P(("dp", "fsdp"), None),
        P(),
        P(("dp", "fsdp"), None),
        P(("dp", "fsdp"), None),
        P(("dp", "fsdp"), None),
        P(("dp", "fsdp"), None),
        P(("dp", "fsdp"), None),
        P(("dp", "fsdp"), None),
        P(("dp", "fsdp"), None),
        P(("dp", "fsdp"), None),
        P(("dp", "fsdp"), None),
        P(),
    )
    return jax.shard_map(
        functools.partial(body, Links(mesh)), mesh=mesh, in_specs=in_specs, out_specs=out_specs, check_vma=False)
```

```python
import functools
import math

import jax
import jax.numpy as jnp
from jax import lax
from jax.experimental import pallas as pl
from jax.experimental.pallas import tpu as pltpu
from jax.sharding import PartitionSpec as P

H = 12
HD = 64
NB = 32
TILE = 128
BAND = 5
EPSILON = 1e-06
MASKED = -1e30
ENC_EDGES = (12, 16, 23, 32, 46, 64, 91)
DEC_EDGES = tuple((math.ceil(16 * 2 ** (3 * power / 16)) for power in range(1, 16)))
PADDING_LABEL = 1 << 20


def encoder_bucket(distance):
    reach = jnp.abs(distance)
    farther = 8 + sum(((reach >= threshold).astype(jnp.int32) for threshold in ENC_EDGES))
    return jnp.where(reach < 8, reach, farther) + 16 * (distance < 0).astype(jnp.int32)


def decoder_bucket(distance):
    ahead = jnp.maximum(distance, 0)
    farther = 16 + sum(((ahead >= threshold).astype(jnp.int32) for threshold in DEC_EDGES))
    return jnp.where(ahead < 16, ahead, farther)


def band_onehot(bucket_of):
    shape = (NB, BAND, TILE, TILE)
    step = lax.broadcasted_iota(jnp.int32, shape, 1) - 2
    key = lax.broadcasted_iota(jnp.int32, shape, 2)
    query = lax.broadcasted_iota(jnp.int32, shape, 3)
    bucket = bucket_of(step * TILE + query - key)
    return (bucket == lax.broadcasted_iota(jnp.int32, shape, 0)).reshape(NB, BAND * TILE * TILE)


def band_bias(table, bucket_of):
    onehot = band_onehot(bucket_of).astype(jnp.bfloat16)
    flat = lax.dot_general(
        table, onehot, (((0,), (0,)), ((), ())), preferred_element_type=jnp.float32
    )
    return flat.reshape(H, BAND, TILE, TILE)


def band_table_grad(band, bucket_of):
    onehot = band_onehot(bucket_of).astype(jnp.float32)
    return lax.dot_general(
        onehot,
        band.reshape(H, BAND * TILE * TILE),
        (((1,), (1,)), ((), ())),
        precision=lax.Precision.HIGHEST,
        preferred_element_type=jnp.float32,
    )


def key_bounds(query_labels, key_labels, query_rows, key_rows):
    queries = jnp.where(query_labels < 0, PADDING_LABEL, query_labels).reshape(-1, query_rows)
    keys = jnp.where(key_labels < 0, PADDING_LABEL, key_labels)
    first = jnp.sum((keys[None, :] < queries[:, :1]).astype(jnp.int32), axis=1)
    last = jnp.sum((keys[None, :] <= queries[:, -1:]).astype(jnp.int32), axis=1)
    return jnp.stack([first // key_rows, (last + key_rows - 1) // key_rows])


def fold_rows(value, combine):
    rows = value.shape[0]
    while rows > 8:
        rows //= 2
        value = combine(value[:rows], value[rows:])
    return value


def head_parts(block):
    lane = lax.broadcasted_iota(jnp.int32, block.shape, 1)
    zero = jnp.zeros_like(block)
    return (jnp.where(lane < HD, block, zero), jnp.where(lane < HD, zero, block))


def flip(value):
    return value.astype(jnp.float32).T


def band_index(query_tile, key_tile):
    return jnp.clip(query_tile - key_tile, -2, 2) + 2


def tile_mask(spec, key_tile, query_block, segk_ref, segq_ref):
    rows, lanes = spec["kb"], spec["qb"]
    start = pl.multiple_of(key_tile * rows, rows) if spec["skip"] else key_tile * rows
    labels = segk_ref[pl.ds(start, rows), :]
    labels = jnp.concatenate([labels] * (lanes // TILE), axis=1)
    mask = labels == segq_ref[...]
    if spec["causal"]:
        key = lax.broadcasted_iota(jnp.int32, (rows, lanes), 0) + key_tile * rows
        query = lax.broadcasted_iota(jnp.int32, (rows, lanes), 1) + query_block * lanes
        mask = mask & (key <= query)
    return mask


def tile_bias(spec, head, key_tile, query_block, bias_ref):
    rows, lanes = spec["kb"] // TILE, spec["qb"] // TILE
    return jnp.concatenate(
        [
            jnp.concatenate(
                [
                    bias_ref[
                        head, band_index(query_block * lanes + lane, key_tile * rows + row)
                    ]
                    for lane in range(lanes)
                ],
                axis=1,
            )
            for row in range(rows)
        ],
        axis=0,
    )


def dot_rows(former, latter):
    return lax.dot_general(
        former, latter, (((1,), (1,)), ((), ())), preferred_element_type=jnp.float32
    )


def dot_plain(former, latter):
    return jnp.dot(former, latter, preferred_element_type=jnp.float32)


def for_counts(spec, first, last, run):
    if not spec["skip"]:
        run(0, spec["tiles"])
        return
    for count in range(1, spec["tiles"] + 1):
        pl.when(last - first == count)(functools.partial(run, first, count))


def forward_kernel(spec, bounds_ref, q_ref, k_ref, v_ref, segq_ref, segk_ref, *rest):
    bias_ref, rest = (rest[0], rest[1:]) if spec["bias"] else (None, rest)
    o_ref, lse_ref, score_ref, vt_ref = rest
    kb, qb, pairs = spec["kb"], spec["qb"], spec["pairs"]
    block = pl.program_id(1)

    @pl.when(block == 0)
    def _():
        for pair in range(pairs):
            span = slice(pair * 2 * HD, (pair + 1) * 2 * HD)
            vt_ref[span, :] = flip(v_ref[:, span]).astype(jnp.bfloat16)

    def run(first, count):
        starts = [(first + tile) * kb for tile in range(count)]
        if spec["skip"]:
            starts = [pl.multiple_of(start, kb) for start in starts]
        for pair in range(pairs):
            span = slice(pair * 2 * HD, (pair + 1) * 2 * HD)
            parts = head_parts(q_ref[:, span])
            mixed, logsum = [], []
            for head in range(2):
                number = 2 * pair + head
                top = None
                for tile in range(count):
                    s = dot_rows(k_ref[pl.ds(starts[tile], kb), span], parts[head])
                    if spec["bias"]:
                        s = s + tile_bias(spec, number, first + tile, block, bias_ref)
                    mask = tile_mask(spec, first + tile, block, segk_ref, segq_ref)
                    s = jnp.where(mask, s, MASKED)
                    score_ref[number, tile] = s
                    peak = fold_rows(s, jnp.maximum)
                    top = peak if top is None else jnp.maximum(top, peak)
                top = jnp.max(top, axis=0, keepdims=True)
                total = None
                for tile in range(count):
                    e = jnp.exp(score_ref[number, tile] - top)
                    score_ref[number, tile] = e
                    part = fold_rows(e, jnp.add)
                    total = part if total is None else total + part
                total = jnp.sum(total, axis=0, keepdims=True)
                scale = 1.0 / total
                mix = None
                for tile in range(count):
                    weights = (score_ref[number, tile] * scale).astype(jnp.bfloat16)
                    rows = slice(number * HD, (number + 1) * HD)
                    part = dot_plain(vt_ref[rows, pl.ds(starts[tile], kb)], weights)
                    mix = part if mix is None else mix + part
                mixed.append(mix)
                logsum.append(top + jnp.log(total))
            o_ref[:, span] = flip(jnp.concatenate(mixed, axis=0)).astype(jnp.bfloat16)
            lse_ref[pair] = jnp.concatenate(logsum, axis=0)

    for_counts(spec, bounds_ref[0, block], bounds_ref[1, block], run)


def backward_kernel(
    spec, bounds_ref, q_ref, k_ref, v_ref, do_ref, lse_ref, segq_ref, segk_ref, *rest
):
    bias_ref, rest = (rest[0], rest[1:]) if spec["bias"] else (None, rest)
    dq_ref, dkv_ref, rest = rest[0], rest[1], rest[2:]
    band_ref, rest = (rest[0], rest[1:]) if spec["bias"] else (None, rest)
    p_ref, dp_ref, dk_ref, dv_ref, kt_ref = rest
    kb, qb, pairs = spec["kb"], spec["qb"], spec["pairs"]
    group, block = pl.program_id(0), pl.program_id(1)

    @pl.when(block == 0)
    def _():
        for pair in range(pairs):
            span = slice(pair * 2 * HD, (pair + 1) * 2 * HD)
            kt_ref[span, :] = flip(k_ref[:, span]).astype(jnp.bfloat16)
        dk_ref[...] = jnp.zeros_like(dk_ref)
        dv_ref[...] = jnp.zeros_like(dv_ref)
        if spec["bias"]:
            band_ref[...] = jnp.zeros_like(band_ref)

    def run(first, count):
        starts = [(first + tile) * kb for tile in range(count)]
        if spec["skip"]:
            starts = [pl.multiple_of(start, kb) for start in starts]
        for pair in range(pairs):
            span = slice(pair * 2 * HD, (pair + 1) * 2 * HD)
            parts = head_parts(q_ref[:, span])
            dparts = head_parts(do_ref[:, span])
            lse = lse_ref[pair]
            dquery = []
            for head in range(2):
                number = 2 * pair + head
                delta = None
                for tile in range(count):
                    here = pl.ds(starts[tile], kb)
                    s = dot_rows(k_ref[here, span], parts[head])
                    if spec["bias"]:
                        s = s + tile_bias(spec, number, first + tile, block, bias_ref)
                    mask = tile_mask(spec, first + tile, block, segk_ref, segq_ref)
                    p = jnp.exp(jnp.where(mask, s, MASKED) - lse[head : head + 1])
                    dp = dot_rows(v_ref[here, span], dparts[head])
                    p_ref[number, tile] = p
                    dp_ref[number, tile] = dp
                    part = fold_rows(p * dp, jnp.add)
                    delta = part if delta is None else delta + part
                    dv_ref[here, span] += dot_plain(p.astype(jnp.bfloat16), dparts[head])
                delta = jnp.sum(delta, axis=0, keepdims=True)
                mix = None
                for tile in range(count):
                    here = pl.ds(starts[tile], kb)
                    ds = p_ref[number, tile] * (dp_ref[number, tile] - delta)
                    if spec["bias"]:
                        rows, lanes = kb // TILE, qb // TILE
                        for row in range(rows):
                            for lane in range(lanes):
                                index = band_index(
                                    block * lanes + lane, (first + tile) * rows + row
                                )
                                band_ref[number, index] += ds[
                                    row * TILE : (row + 1) * TILE,
                                    lane * TILE : (lane + 1) * TILE,
                                ]
                    low = ds.astype(jnp.bfloat16)
                    dk_ref[here, span] += dot_plain(low, parts[head])
                    rows = slice(number * HD, (number + 1) * HD)
                    part = dot_plain(kt_ref[rows, here], low)
                    mix = part if mix is None else mix + part
                dquery.append(mix)
            dq_ref[:, span] = flip(jnp.concatenate(dquery, axis=0)).astype(jnp.bfloat16)

    for_counts(spec, bounds_ref[0, block], bounds_ref[1, block], run)

    @pl.when(block == pl.num_programs(1) - 1)
    def _():
        width = pairs * 2 * HD
        column = pl.multiple_of(group * width, width)
        dkv_ref[:, pl.ds(column, width)] = dk_ref[...].astype(jnp.bfloat16)
        column = pl.multiple_of((pl.num_programs(0) + group) * width, width)
        dkv_ref[:, pl.ds(column, width)] = dv_ref[...].astype(jnp.bfloat16)


def attention_setup(queries, keyval, query_labels, key_labels, bias, causal):
    rows, keys = queries.shape[0], keyval.shape[0]
    qb, kb = min(256, rows), min(256, keys)
    skip = rows > qb
    pairs = 1 if skip else 3
    spec = dict(
        qb=qb,
        kb=kb,
        causal=causal,
        bias=bias is not None,
        pairs=pairs,
        tiles=keys // kb,
        skip=skip,
    )
    bounds = key_bounds(query_labels, key_labels, qb, kb)
    segq = query_labels[None, :]
    segk = jnp.broadcast_to(key_labels[:, None], (keys, TILE))
    groups = H // 2 // pairs
    width = 2 * HD * pairs
    specs = dict(
        q=pl.BlockSpec((qb, width), lambda group, block, bounds: (block, group)),
        k=pl.BlockSpec((keys, width), lambda group, block, bounds: (0, group)),
        v=pl.BlockSpec((keys, width), lambda group, block, bounds: (0, groups + group)),
        segq=pl.BlockSpec((1, qb), lambda group, block, bounds: (0, block)),
        segk=pl.BlockSpec((keys, TILE), lambda group, block, bounds: (0, 0)),
        lse=pl.BlockSpec((pairs, 2, qb), lambda group, block, bounds: (group, 0, block)),
        band=pl.BlockSpec(
            (2 * pairs, BAND, TILE, TILE), lambda group, block, bounds: (group, 0, 0, 0)
        ),
        whole=pl.BlockSpec((keys, 2 * H * HD), lambda group, block, bounds: (0, 0)),
    )
    scores = pltpu.VMEM((2 * pairs, keys // kb, kb, qb), jnp.float32)
    return spec, bounds, segq, segk, specs, (groups, rows // qb), scores


def attend_forward(queries, keyval, query_labels, key_labels, bias, causal):
    spec, bounds, segq, segk, specs, grid, scores = attention_setup(
        queries, keyval, query_labels, key_labels, bias, causal
    )
    rows, keys = queries.shape[0], keyval.shape[0]
    work = H * rows * keys
    extra = ([specs["band"]], [bias]) if bias is not None else ([], [])
    return pl.pallas_call(
        functools.partial(forward_kernel, spec),
        out_shape=(
            jax.ShapeDtypeStruct((rows, H * HD), jnp.bfloat16),
            jax.ShapeDtypeStruct((H // 2, 2, rows), jnp.float32),
        ),
        grid_spec=pltpu.PrefetchScalarGridSpec(
            num_scalar_prefetch=1,
            grid=grid,
            in_specs=[specs["q"], specs["k"], specs["v"], specs["segq"], specs["segk"]]
            + extra[0],
            out_specs=[specs["q"], specs["lse"]],
            scratch_shapes=[
                scores,
                pltpu.VMEM((2 * HD * spec["pairs"], keys), jnp.bfloat16),
            ],
        ),
        compiler_params=pltpu.CompilerParams(vmem_limit_bytes=40 << 20),
        cost_estimate=pl.CostEstimate(
            flops=16 * HD * work, transcendentals=work, bytes_accessed=8 << 20
        ),
    )(bounds, queries, keyval, keyval, segq, segk, *extra[1])


def attend_backward(queries, keyval, query_labels, key_labels, bias, causal, lse, dmixture):
    spec, bounds, segq, segk, specs, grid, scores = attention_setup(
        queries, keyval, query_labels, key_labels, bias, causal
    )
    rows, keys = queries.shape[0], keyval.shape[0]
    work = H * rows * keys
    extra = ([specs["band"]], [bias]) if bias is not None else ([], [])
    band = (
        [jax.ShapeDtypeStruct((H, BAND, TILE, TILE), jnp.float32)] if bias is not None else []
    )
    out = pl.pallas_call(
        functools.partial(backward_kernel, spec),
        out_shape=[
            jax.ShapeDtypeStruct((rows, H * HD), jnp.bfloat16),
            jax.ShapeDtypeStruct((keys, 2 * H * HD), jnp.bfloat16),
        ]
        + band,
        grid_spec=pltpu.PrefetchScalarGridSpec(
            num_scalar_prefetch=1,
            grid=grid,
            in_specs=[
                specs["q"],
                specs["k"],
                specs["v"],
                specs["q"],
                specs["lse"],
                specs["segq"],
                specs["segk"],
            ]
            + extra[0],
            out_specs=[specs["q"], specs["whole"]] + extra[0],
            scratch_shapes=[
                scores,
                scores,
                pltpu.VMEM((keys, 2 * HD * spec["pairs"]), jnp.float32),
                pltpu.VMEM((keys, 2 * HD * spec["pairs"]), jnp.float32),
                pltpu.VMEM((2 * HD * spec["pairs"], keys), jnp.bfloat16),
            ],
        ),
        compiler_params=pltpu.CompilerParams(vmem_limit_bytes=48 << 20),
        cost_estimate=pl.CostEstimate(
            flops=40 * HD * work, transcendentals=work, bytes_accessed=16 << 20
        ),
    )(bounds, queries, keyval, keyval, dmixture, lse, segq, segk, *extra[1])
    return (out[0], out[1], out[2] if bias is not None else None)


def product(former, latter):
    return jnp.dot(former, latter, preferred_element_type=jnp.float32)


def transpose_product(former, latter):
    return lax.dot_general(
        former, latter, (((0,), (0,)), ((), ())), preferred_element_type=jnp.float32
    )


def product_transposed(former, latter):
    return lax.dot_general(
        former, latter, (((1,), (1,)), ((), ())), preferred_element_type=jnp.float32
    )


def smooth_gate(value):
    return jax.nn.gelu(value, approximate=True)


def norm_forward(stream, norm_gain):
    return (
        stream * lax.rsqrt(jnp.mean(stream * stream, axis=-1, keepdims=True) + EPSILON) * norm_gain
    )


def norm_backward(stream, norm_gain, gradient):
    outcome, pullback = jax.vjp(norm_forward, stream, norm_gain)
    return pullback(gradient)


def attention_forward(stream, norm_gain, wquery, wkeyval, wproj, layout, memory):
    normed = norm_forward(stream, norm_gain).astype(jnp.bfloat16)
    queries = product(normed, wquery).astype(jnp.bfloat16)
    source = normed if memory is None else memory
    keyval = product(source, wkeyval).astype(jnp.bfloat16)
    mixture, logsum = attend_forward(queries, keyval, *layout)
    return (stream + product(mixture, wproj), (normed, queries, keyval, mixture, logsum))


def attention_backward(stream, norm_gain, wquery, wkeyval, wproj, layout, memory, stored, gradient):
    normed, queries, keyval, mixture, logsum = stored
    gradient_low = gradient.astype(jnp.bfloat16)
    project_grad = transpose_product(mixture, gradient_low)
    dmixture = product_transposed(gradient_low, wproj).astype(jnp.bfloat16)
    dquery_low, dkeyval_low, band = attend_backward(queries, keyval, *layout, logsum, dmixture)
    source = normed if memory is None else memory
    query_grad = transpose_product(normed, dquery_low)
    keyval_grad = transpose_product(source, dkeyval_low)
    dnormed = product_transposed(dquery_low, wquery)
    dsource = product_transposed(dkeyval_low, wkeyval)
    if memory is None:
        dnormed = dnormed + dsource
        dsource = None
    dstream, dgain = norm_backward(stream, norm_gain, dnormed)
    return (gradient + dstream, dgain, query_grad, keyval_grad, project_grad, band, dsource)


def feed_forward(stream, norm_gain, winner, wouter):
    normed = norm_forward(stream, norm_gain).astype(jnp.bfloat16)
    before = product(normed, winner)
    hidden = smooth_gate(before).astype(jnp.bfloat16)
    return (stream + product(hidden, wouter), (normed, before, hidden))


def feed_backward(stream, norm_gain, winner, wouter, stored, gradient):
    normed, before, hidden = stored
    gradient_low = gradient.astype(jnp.bfloat16)
    outer_grad = transpose_product(hidden, gradient_low)
    dhidden = product_transposed(gradient_low, wouter)
    gate_value, gate_pullback = jax.vjp(smooth_gate, before)
    dbefore = gate_pullback(dhidden)[0].astype(jnp.bfloat16)
    inner_grad = transpose_product(normed, dbefore)
    dnormed = product_transposed(dbefore, winner)
    dstream, dgain = norm_backward(stream, norm_gain, dnormed)
    return (gradient + dstream, dgain, inner_grad, outer_grad)


def index_bits(devices):
    return devices.bit_length() - 1


class Links:
    def __init__(self, mesh):
        self.sizes = dict(mesh.shape)
        self.bits = [("fsdp", bit) for bit in range(index_bits(self.sizes["fsdp"]))]
        self.bits += [("dp", bit) for bit in range(index_bits(self.sizes["dp"]))]

    def side(self, axis, bit):
        return lax.rem(lax.axis_index(axis) // (1 << bit), 2)

    def partner(self, axis, bit):
        return {axis: lax.axis_index(axis) + (1 - 2 * self.side(axis, bit)) * (1 << bit)}

    def orders(self):
        core, row = ("dp", 0), ("fsdp", 0)
        rest = [key for key in self.bits if key not in (core, row)]
        return ([core] + rest[:1] + [row] + rest[1:], [core, row] + rest)

    def swap(self, value, axis, bit):
        pairs = [(place, place ^ (1 << bit)) for place in range(self.sizes[axis])]
        return lax.ppermute(value, axis, pairs)

    def total(self, value):
        for key in self.bits:
            value = value + self.swap(value, *key)
        return value

    def gather(self, shard):
        rows, columns = shard.shape
        half = rows // 2
        core, place = self.side("dp", 0), lax.axis_index("fsdp")
        part = lax.dynamic_slice_in_dim(shard, core * half, half, 0)
        theirs = self.swap(part, "fsdp", 0)
        mate = self.swap(theirs, "dp", 0)
        whole = jnp.zeros((2 * rows, columns), shard.dtype)
        other = (1 - place) * rows
        whole = lax.dynamic_update_slice_in_dim(whole, shard, place * rows, 0)
        whole = lax.dynamic_update_slice_in_dim(whole, theirs, other + core * half, 0)
        return lax.dynamic_update_slice_in_dim(whole, mate, other + (1 - core) * half, 0)

    def gather_small(self, shard):
        other = self.swap(shard, "fsdp", 0)
        first = lax.axis_index("fsdp") == 0
        return jnp.concatenate(
            [jnp.where(first, shard, other), jnp.where(first, other, shard)], axis=0
        )

    def devices(self):
        return self.sizes["dp"] * self.sizes["fsdp"]

    def place(self):
        return lax.axis_index("dp") * self.sizes["fsdp"] + lax.axis_index("fsdp")


def pick(ref, lead, spot, count, side):
    return ref.at[(lead,) + (slice(None),) * spot + (side,) + (slice(None),) * (count - spot - 1)]


def reduce_kernel(links, pairs, g_ref, out_ref, own_ref, *rest):
    stages = len(links.bits)
    sums, (send_sem, recv_sem, own_sem) = rest[:stages], rest[stages:]
    plans = []
    for order in links.orders():
        left = list(reversed(links.bits))
        plan = []
        for key in order:
            plan.append((key, left.index(key), len(left)))
            left.remove(key)
        plans.append(plan)

    barrier = pltpu.get_barrier_semaphore()
    for key in links.bits:
        pl.semaphore_signal(
            barrier,
            inc=1,
            device_id=links.partner(*key),
            device_id_type=pl.DeviceIdType.MESH,
        )
    pl.semaphore_wait(barrier, stages)

    def source(stage, chunk, parity, away):
        key, spot, count = plans[parity][stage]
        side = links.side(*key)
        ref = g_ref if stage == 0 else sums[stage - 1]
        return pick(ref, chunk, spot, count, 1 - side if away else side)

    def send(stage, chunk, parity):
        key, _, _ = plans[parity][stage]
        return pltpu.make_async_remote_copy(
            src_ref=source(stage, chunk, parity, True),
            dst_ref=sums[stage].at[chunk],
            send_sem=send_sem.at[stage, chunk],
            recv_sem=recv_sem.at[stage, chunk],
            device_id=links.partner(*key),
            device_id_type=pl.DeviceIdType.MESH,
        )

    def fetch(pair, parity):
        slot = lax.rem(pair, 2)
        return pltpu.make_async_copy(
            source(0, 2 * pair + parity, parity, False),
            own_ref.at[slot, parity],
            own_sem.at[slot, parity],
        )

    def step(slot, carry):
        @pl.when(slot < pairs)
        def _():
            for parity in range(2):
                send(0, 2 * slot + parity, parity).start()
                fetch(slot, parity).start()

        for stage in range(stages):
            pair = slot - 1 - stage

            @pl.when((pair >= 0) & (pair < pairs))
            def _():
                for parity in range(2):
                    chunk = 2 * pair + parity
                    send(stage, chunk, parity).wait()
                    if stage == 0:
                        fetch(pair, parity).wait()
                        mine = own_ref[lax.rem(pair, 2), parity]
                    else:
                        mine = source(stage, chunk, parity, False)[...]
                    if stage < stages - 1:
                        sums[stage][chunk] = sums[stage][chunk] + mine
                        send(stage + 1, chunk, parity).start()
                    else:
                        out_ref[chunk] = sums[stage][chunk].astype(jnp.float32) + mine.astype(
                            jnp.float32
                        )

        return carry

    lax.fori_loop(0, pairs + stages, step, 0)


def reduce_chunks(links, grads, collective_id):
    chunks, _, rows, columns = grads.shape
    stages = len(links.bits)
    sums = [
        pltpu.VMEM((chunks,) + (2,) * (stages - 1 - stage) + (rows, columns), jnp.bfloat16)
        for stage in range(stages)
    ]
    return pl.pallas_call(
        functools.partial(reduce_kernel, links, chunks // 2),
        out_shape=jax.ShapeDtypeStruct((chunks, rows, columns), jnp.float32),
        in_specs=[pl.BlockSpec(memory_space=pl.ANY)],
        out_specs=pl.BlockSpec(memory_space=pltpu.VMEM),
        scratch_shapes=[
            pltpu.VMEM((2, 2) + (2,) * (stages - 1) + (rows, columns), jnp.bfloat16)
        ]
        + sums
        + [
            pltpu.SemaphoreType.DMA((stages, chunks)),
            pltpu.SemaphoreType.DMA((stages, chunks)),
            pltpu.SemaphoreType.DMA((2, 2)),
        ],
        compiler_params=pltpu.CompilerParams(
            collective_id=collective_id, has_side_effects=True, vmem_limit_bytes=58 << 20
        ),
    )(grads.reshape((chunks,) + (2,) * stages + (rows, columns)))


def fold_grad(grad, devices, width):
    rows, columns = grad.shape
    deep, wide = rows // width, columns // width
    r = rows // devices // deep
    grad = grad.astype(jnp.bfloat16).reshape(devices, deep, r, wide, 2, width // 2)
    return grad.transpose(1, 3, 0, 4, 2, 5).reshape(deep * wide, devices, 2 * r, width // 2)


def unfold_share(chunks, rows, columns):
    count, folded, half = chunks.shape
    deep, wide = rows * 2 // folded, columns // (2 * half)
    chunks = chunks.reshape(deep, wide, 2, folded // 2, half)
    return chunks.transpose(0, 3, 1, 2, 4).reshape(rows, columns)


def reduce_grads(links, grads, collective_id):
    devices = links.devices()
    width = min(grad.shape[0] for grad in grads)
    folded = [fold_grad(grad, devices, width) for grad in grads]
    counts = [piece.shape[0] for piece in folded]
    shares = reduce_chunks(links, jnp.concatenate(folded, axis=0), collective_id)
    result, start = [], 0
    for grad, count in zip(grads, counts):
        rows, columns = grad.shape
        result.append(unfold_share(shares[start : start + count], rows // devices, columns))
        start += count
    return result


def body(
    links,
    enc_tokens,
    dec_tokens,
    enc_segments,
    dec_segments,
    enc_upstream,
    dec_upstream,
    encoder_query,
    encoder_keyval,
    encoder_proj,
    encoder_inner,
    encoder_outer,
    encoder_gains,
    encoder_table,
    decoder_query,
    decoder_keyval,
    decoder_proj,
    cross_query,
    cross_keyval,
    cross_proj,
    decoder_inner,
    decoder_outer,
    decoder_gains,
    decoder_table,
):
    small = jnp.concatenate(
        [encoder_gains, decoder_gains]
        + [
            jnp.concatenate([encoder_table, decoder_table], axis=0).reshape(
                encoder_gains.shape[0], -1
            )
        ],
        axis=1,
    )
    small = links.gather_small(small)
    enc_gains = small[:, 0:2].astype(jnp.float32)
    dec_gains = small[:, 2:5].astype(jnp.float32)
    tables = small[:, 5:].reshape(2, 2, NB // 2, H)
    enc_bias = band_bias(tables[:, 0].reshape(NB, H), encoder_bucket)
    dec_bias = band_bias(tables[:, 1].reshape(NB, H), decoder_bucket)

    equery, ekeyval, eproj = (
        links.gather(w) for w in (encoder_query, encoder_keyval, encoder_proj)
    )
    einner, eouter = (links.gather(w) for w in (encoder_inner, encoder_outer))
    dquery, dkeyval, dproj = (
        links.gather(w) for w in (decoder_query, decoder_keyval, decoder_proj)
    )
    cquery, ckeyval, cproj = (links.gather(w) for w in (cross_query, cross_keyval, cross_proj))
    dinner, douter = (links.gather(w) for w in (decoder_inner, decoder_outer))

    enc_layout = (enc_segments, enc_segments, enc_bias, False)
    dec_layout = (dec_segments, dec_segments, dec_bias, True)
    cross_layout = (dec_segments, enc_segments, None, False)

    enc_stream = enc_tokens.astype(jnp.float32)
    enc_middle, enc_self = attention_forward(
        enc_stream, enc_gains[:, 0], equery, ekeyval, eproj, enc_layout, None
    )
    enc_final, enc_ffn = feed_forward(enc_middle, enc_gains[:, 1], einner, eouter)
    memory = enc_final.astype(jnp.bfloat16)

    dec_stream = dec_tokens.astype(jnp.float32)
    after_self, dec_self = attention_forward(
        dec_stream, dec_gains[:, 0], dquery, dkeyval, dproj, dec_layout, None
    )
    after_cross, dec_cross = attention_forward(
        after_self, dec_gains[:, 1], cquery, ckeyval, cproj, cross_layout, memory
    )
    dec_final, dec_ffn = feed_forward(after_cross, dec_gains[:, 2], dinner, douter)


    dec_live = (dec_segments >= 0).astype(jnp.float32)[:, None]
    gradient = dec_upstream.astype(jnp.float32) * dec_live
    gradient, dgain_ffn, dinner_grad, douter_grad = feed_backward(
        after_cross, dec_gains[:, 2], dinner, douter, dec_ffn, gradient
    )
    gradient, dgain_cross, cquery_grad, ckeyval_grad, cproj_grad, _, memory_grad = (
        attention_backward(
            after_self,
            dec_gains[:, 1],
            cquery,
            ckeyval,
            cproj,
            cross_layout,
            memory,
            dec_cross,
            gradient,
        )
    )
    dec_gradient, dgain_self, dquery_grad, dkeyval_grad, dproj_grad, dec_band, _ = (
        attention_backward(
            dec_stream,
            dec_gains[:, 0],
            dquery,
            dkeyval,
            dproj,
            dec_layout,
            None,
            dec_self,
            gradient,
        )
    )

    enc_live = (enc_segments >= 0).astype(jnp.float32)[:, None]
    gradient = enc_upstream.astype(jnp.float32) * enc_live + memory_grad
    gradient, egain_ffn, einner_grad, eouter_grad = feed_backward(
        enc_middle, enc_gains[:, 1], einner, eouter, enc_ffn, gradient
    )
    enc_gradient, egain_self, equery_grad, ekeyval_grad, eproj_grad, enc_band, _ = (
        attention_backward(
            enc_stream,
            enc_gains[:, 0],
            equery,
            ekeyval,
            eproj,
            enc_layout,
            None,
            enc_self,
            gradient,
        )
    )

    table_grads = [
        band_table_grad(enc_band, encoder_bucket),
        band_table_grad(dec_band, decoder_bucket),
    ]
    gain_grads = jnp.stack([egain_self, egain_ffn, dgain_self, dgain_cross, dgain_ffn])
    flat = jnp.concatenate([gain_grads.reshape(-1)] + [grad.reshape(-1) for grad in table_grads])
    flat = links.total(flat.reshape(-1, TILE)).reshape(-1)
    width = gain_grads.shape[1]
    tables_grad = flat[5 * width :].reshape(2, NB, H)
    own = width // links.devices()
    gains_share = lax.dynamic_slice_in_dim(
        flat[: 5 * width].reshape(5, width), links.place() * own, own, 1
    ).T
    (
        equery_share,
        ekeyval_share,
        eproj_share,
        einner_share,
        eouter_share,
        dquery_share,
        dkeyval_share,
        dproj_share,
        cquery_share,
        ckeyval_share,
        cproj_share,
        dinner_share,
        douter_share,
    ) = reduce_grads(
        links,
        [
            equery_grad,
            ekeyval_grad,
            eproj_grad,
            einner_grad,
            eouter_grad,
            dquery_grad,
            dkeyval_grad,
            dproj_grad,
            cquery_grad,
            ckeyval_grad,
            cproj_grad,
            dinner_grad,
            douter_grad,
        ],
        0,
    )
    return (
        memory,
        dec_final.astype(jnp.bfloat16),
        enc_gradient,
        dec_gradient,
        equery_share,
        ekeyval_share,
        eproj_share,
        einner_share,
        eouter_share,
        gains_share[:, 0:2],
        tables_grad[0],
        dquery_share,
        dkeyval_share,
        dproj_share,
        cquery_share,
        ckeyval_share,
        cproj_share,
        dinner_share,
        douter_share,
        gains_share[:, 2:5],
        tables_grad[1],
    )


def solution(mesh):
    in_specs = (
        P(("dp", "fsdp"), None),
        P(("dp", "fsdp"), None),
        P(("dp", "fsdp")),
        P(("dp", "fsdp")),
        P(("dp", "fsdp"), None),
        P(("dp", "fsdp"), None),
        P("fsdp", None),
        P("fsdp", None),
        P("fsdp", None),
        P("fsdp", None),
        P("fsdp", None),
        P("fsdp", None),
        P("fsdp", None),
        P("fsdp", None),
        P("fsdp", None),
        P("fsdp", None),
        P("fsdp", None),
        P("fsdp", None),
        P("fsdp", None),
        P("fsdp", None),
        P("fsdp", None),
        P("fsdp", None),
        P("fsdp", None),
    )
    out_specs = (
        P(("dp", "fsdp"), None),
        P(("dp", "fsdp"), None),
        P(("dp", "fsdp"), None),
        P(("dp", "fsdp"), None),
        P(("dp", "fsdp"), None),
        P(("dp", "fsdp"), None),
        P(("dp", "fsdp"), None),
        P(("dp", "fsdp"), None),
        P(("dp", "fsdp"), None),
        P(("dp", "fsdp"), None),
        P(),
        P(("dp", "fsdp"), None),
        P(("dp", "fsdp"), None),
        P(("dp", "fsdp"), None),
        P(("dp", "fsdp"), None),
        P(("dp", "fsdp"), None),
        P(("dp", "fsdp"), None),
        P(("dp", "fsdp"), None),
        P(("dp", "fsdp"), None),
        P(("dp", "fsdp"), None),
        P(),
    )
    return jax.shard_map(
        functools.partial(body, Links(mesh)), mesh=mesh, in_specs=in_specs, out_specs=out_specs, check_vma=False)
```

```python
import functools
import math

import jax
import jax.numpy as jnp
import numpy as np
from jax import lax
from jax.experimental import pallas as pl
from jax.experimental.pallas import tpu as pltpu
from jax.sharding import PartitionSpec as P

H = 12
HD = 64
NB = 32
TILE = 128
BAND = 5
EPSILON = 1e-06
MASKED = -1e30
ENC_EDGES = (12, 16, 23, 32, 46, 64, 91)
DEC_EDGES = tuple((math.ceil(16 * 2 ** (3 * power / 16)) for power in range(1, 16)))
PADDING_LABEL = 1 << 20
SPAN = 2 * TILE
FOLD = 8
LAG = 2
DELAY = 2
HOLD = DELAY + 1
OFFLOADED = ("dinner", "douter")
NAMES = (
    "equery",
    "ekeyval",
    "eproj",
    "einner",
    "eouter",
    "dquery",
    "dkeyval",
    "dproj",
    "cquery",
    "ckeyval",
    "cproj",
    "dinner",
    "douter",
)


def encoder_bucket(distance):
    reach = np.abs(distance)
    farther = 8 + sum((reach >= threshold).astype(np.int32) for threshold in ENC_EDGES)
    return np.where(reach < 8, reach, farther) + 16 * (distance < 0).astype(np.int32)


def decoder_bucket(distance):
    ahead = np.maximum(distance, 0)
    farther = 16 + sum((ahead >= threshold).astype(np.int32) for threshold in DEC_EDGES)
    return np.where(ahead < 16, ahead, farther)


def band_distances(rows):
    step = np.arange(BAND)[:, None, None] - 2
    row = np.arange(rows)[None, :, None]
    lane = np.arange(SPAN)[None, None, :]
    lane = np.where(lane < TILE, lane, lane - SPAN)
    return step * TILE + lane - row


def bucket_onehot(bucket_of, rows, dtype):
    bucket = jnp.asarray(bucket_of(band_distances(rows)).reshape(1, -1), jnp.int32)
    return (bucket == lax.broadcasted_iota(jnp.int32, (NB, 1), 0)).astype(dtype)


def band_bias(table, bucket_of):
    onehot = bucket_onehot(bucket_of, 1, jnp.bfloat16)
    flat = lax.dot_general(
        table, onehot, (((0,), (0,)), ((), ())), preferred_element_type=jnp.float32
    )
    return flat.reshape(H, BAND, SPAN)


def band_table_grad(band, bucket_of):
    return lax.dot_general(
        bucket_onehot(bucket_of, FOLD, jnp.float32),
        band.reshape(H, BAND * FOLD * SPAN),
        (((1,), (1,)), ((), ())),
        precision=lax.Precision.HIGHEST,
        preferred_element_type=jnp.float32,
    )


def key_bounds(query_labels, key_labels, query_rows, key_rows):
    queries = jnp.where(query_labels < 0, PADDING_LABEL, query_labels).reshape(-1, query_rows)
    keys = jnp.where(key_labels < 0, PADDING_LABEL, key_labels)
    first = jnp.sum((keys[None, :] < queries[:, :1]).astype(jnp.int32), axis=1)
    last = jnp.sum((keys[None, :] <= queries[:, -1:]).astype(jnp.int32), axis=1)
    return jnp.stack([first // key_rows, (last + key_rows - 1) // key_rows])


def fold_rows(value, combine):
    rows = value.shape[0]
    while rows > 8:
        rows //= 2
        value = combine(value[:rows], value[rows:])
    return value


def head_parts(block):
    lane = lax.broadcasted_iota(jnp.int32, block.shape, 1)
    zero = jnp.zeros_like(block)
    return (jnp.where(lane < HD, block, zero), jnp.where(lane < HD, zero, block))


def flip(value):
    return value.astype(jnp.float32).T


def band_index(query_tile, key_tile):
    return jnp.clip(query_tile - key_tile, -2, 2) + 2


def spread_bias(bias_ref, tiles_ref):
    for head in range(tiles_ref.shape[0]):
        for step in range(BAND):
            row = bias_ref[head, step : step + 1, :]
            if step in (0, BAND - 1):
                tiles_ref[head, step] = jnp.broadcast_to(row[:, :TILE], (TILE, TILE))
            else:
                wide = jnp.broadcast_to(row, (TILE, SPAN))
                wide = pltpu.roll(wide, 0, 1, stride=1, stride_axis=0)
                tiles_ref[head, step] = wide[:, :TILE]


def gather_diagonals(tiles_ref, band_ref):
    for head in range(tiles_ref.shape[0]):
        for step in range(BAND):
            tile = tiles_ref[head, step]
            tile = jnp.concatenate([tile, jnp.zeros_like(tile)], axis=1)
            rows = TILE
            while rows > FOLD:
                rows //= 2
                tile = tile[:rows] + pltpu.roll(tile[rows:], SPAN - rows, 1)
            band_ref[head, step] = tile


def tile_mask(spec, key_tile, query_block, segk_ref, segq_ref):
    rows, lanes = spec["kb"], spec["qb"]
    start = pl.multiple_of(key_tile * rows, rows) if spec["skip"] else key_tile * rows
    labels = segk_ref[pl.ds(start, rows), :]
    labels = jnp.concatenate([labels] * (lanes // TILE), axis=1)
    mask = labels == segq_ref[...]
    if spec["causal"]:
        key = lax.broadcasted_iota(jnp.int32, (rows, lanes), 0) + key_tile * rows
        query = lax.broadcasted_iota(jnp.int32, (rows, lanes), 1) + query_block * lanes
        mask = mask & (key <= query)
    return mask


def tile_bias(spec, head, key_tile, query_block, bias_ref):
    rows, lanes = spec["kb"] // TILE, spec["qb"] // TILE
    return jnp.concatenate(
        [
            jnp.concatenate(
                [
                    bias_ref[
                        head, band_index(query_block * lanes + lane, key_tile * rows + row)
                    ]
                    for lane in range(lanes)
                ],
                axis=1,
            )
            for row in range(rows)
        ],
        axis=0,
    )


def dot_rows(former, latter):
    return lax.dot_general(
        former, latter, (((1,), (1,)), ((), ())), preferred_element_type=jnp.float32
    )


def dot_plain(former, latter):
    return jnp.dot(former, latter, preferred_element_type=jnp.float32)


def for_counts(spec, first, last, run):
    if not spec["skip"]:
        run(0, spec["tiles"])
        return
    for count in range(1, spec["tiles"] + 1):
        pl.when(last - first == count)(functools.partial(run, first, count))


def forward_kernel(spec, bounds_ref, q_ref, k_ref, v_ref, segq_ref, segk_ref, *rest):
    bias_ref, rest = (rest[0], rest[1:]) if spec["bias"] else (None, rest)
    o_ref, lse_ref, score_ref, vt_ref, rest = *rest[:4], rest[4:]
    tiles_ref = rest[0] if spec["bias"] else None
    kb, qb, pairs = spec["kb"], spec["qb"], spec["pairs"]
    block = pl.program_id(1)

    @pl.when(block == 0)
    def _():
        for pair in range(pairs):
            span = slice(pair * 2 * HD, (pair + 1) * 2 * HD)
            vt_ref[span, :] = flip(v_ref[:, span]).astype(jnp.bfloat16)
        if spec["bias"]:
            spread_bias(bias_ref, tiles_ref)

    def run(first, count):
        starts = [(first + tile) * kb for tile in range(count)]
        if spec["skip"]:
            starts = [pl.multiple_of(start, kb) for start in starts]
        for pair in range(pairs):
            span = slice(pair * 2 * HD, (pair + 1) * 2 * HD)
            parts = head_parts(q_ref[:, span])
            mixed, logsum = [], []
            for head in range(2):
                number = 2 * pair + head
                top = None
                for tile in range(count):
                    s = dot_rows(k_ref[pl.ds(starts[tile], kb), span], parts[head])
                    if spec["bias"]:
                        s = s + tile_bias(spec, number, first + tile, block, tiles_ref)
                    mask = tile_mask(spec, first + tile, block, segk_ref, segq_ref)
                    s = jnp.where(mask, s, MASKED)
                    score_ref[number, tile] = s
                    peak = fold_rows(s, jnp.maximum)
                    top = peak if top is None else jnp.maximum(top, peak)
                top = jnp.max(top, axis=0, keepdims=True)
                total = None
                for tile in range(count):
                    e = jnp.exp(score_ref[number, tile] - top)
                    score_ref[number, tile] = e
                    part = fold_rows(e, jnp.add)
                    total = part if total is None else total + part
                total = jnp.sum(total, axis=0, keepdims=True)
                scale = 1.0 / total
                mix = None
                for tile in range(count):
                    weights = (score_ref[number, tile] * scale).astype(jnp.bfloat16)
                    rows = slice(number * HD, (number + 1) * HD)
                    part = dot_plain(vt_ref[rows, pl.ds(starts[tile], kb)], weights)
                    mix = part if mix is None else mix + part
                mixed.append(mix)
                logsum.append(top + jnp.log(total))
            o_ref[:, span] = flip(jnp.concatenate(mixed, axis=0)).astype(jnp.bfloat16)
            lse_ref[pair] = jnp.concatenate(logsum, axis=0)

    for_counts(spec, bounds_ref[0, block], bounds_ref[1, block], run)


def backward_kernel(
    spec, bounds_ref, q_ref, k_ref, v_ref, do_ref, lse_ref, segq_ref, segk_ref, *rest
):
    bias_ref, rest = (rest[0], rest[1:]) if spec["bias"] else (None, rest)
    dq_ref, dkv_ref, rest = rest[0], rest[1], rest[2:]
    band_ref, rest = (rest[0], rest[1:]) if spec["bias"] else (None, rest)
    p_ref, dp_ref, dk_ref, dv_ref, kt_ref, rest = *rest[:5], rest[5:]
    tiles_ref, dtiles_ref = rest if spec["bias"] else (None, None)
    kb, qb, pairs = spec["kb"], spec["qb"], spec["pairs"]
    group, block = pl.program_id(0), pl.program_id(1)

    @pl.when(block == 0)
    def _():
        for pair in range(pairs):
            span = slice(pair * 2 * HD, (pair + 1) * 2 * HD)
            kt_ref[span, :] = flip(k_ref[:, span]).astype(jnp.bfloat16)
        dk_ref[...] = jnp.zeros_like(dk_ref)
        dv_ref[...] = jnp.zeros_like(dv_ref)
        if spec["bias"]:
            spread_bias(bias_ref, tiles_ref)
            dtiles_ref[...] = jnp.zeros_like(dtiles_ref)

    def run(first, count):
        starts = [(first + tile) * kb for tile in range(count)]
        if spec["skip"]:
            starts = [pl.multiple_of(start, kb) for start in starts]
        for pair in range(pairs):
            span = slice(pair * 2 * HD, (pair + 1) * 2 * HD)
            parts = head_parts(q_ref[:, span])
            dparts = head_parts(do_ref[:, span])
            lse = lse_ref[pair]
            stacked = jnp.concatenate(parts, axis=0)
            dstacked = jnp.concatenate(dparts, axis=0)
            deltas = []
            for head in range(2):
                number = 2 * pair + head
                delta = None
                for tile in range(count):
                    here = pl.ds(starts[tile], kb)
                    s = dot_rows(k_ref[here, span], parts[head])
                    if spec["bias"]:
                        s = s + tile_bias(spec, number, first + tile, block, tiles_ref)
                    mask = tile_mask(spec, first + tile, block, segk_ref, segq_ref)
                    p = jnp.exp(jnp.where(mask, s, MASKED) - lse[head : head + 1])
                    dp = dot_rows(v_ref[here, span], dparts[head])
                    p_ref[number, tile] = p
                    dp_ref[number, tile] = dp
                    part = fold_rows(p * dp, jnp.add)
                    delta = part if delta is None else delta + part
                deltas.append(jnp.sum(delta, axis=0, keepdims=True))
            dquery = [None, None]
            for tile in range(count):
                here = pl.ds(starts[tile], kb)
                weights, lows = [], []
                for head in range(2):
                    number = 2 * pair + head
                    p = p_ref[number, tile]
                    ds = p * (dp_ref[number, tile] - deltas[head])
                    if spec["bias"]:
                        rows, lanes = kb // TILE, qb // TILE
                        for row in range(rows):
                            for lane in range(lanes):
                                index = band_index(
                                    block * lanes + lane, (first + tile) * rows + row
                                )
                                dtiles_ref[number, index] += ds[
                                    row * TILE : (row + 1) * TILE,
                                    lane * TILE : (lane + 1) * TILE,
                                ]
                    low = ds.astype(jnp.bfloat16)
                    weights.append(p.astype(jnp.bfloat16))
                    lows.append(low)
                    rows = slice(number * HD, (number + 1) * HD)
                    part = dot_plain(kt_ref[rows, here], low)
                    dquery[head] = part if tile == 0 else dquery[head] + part
                dv_ref[here, span] += dot_plain(jnp.concatenate(weights, axis=1), dstacked)
                dk_ref[here, span] += dot_plain(jnp.concatenate(lows, axis=1), stacked)
            dq_ref[:, span] = flip(jnp.concatenate(dquery, axis=0)).astype(jnp.bfloat16)

    for_counts(spec, bounds_ref[0, block], bounds_ref[1, block], run)

    @pl.when(block == pl.num_programs(1) - 1)
    def _():
        width = pairs * 2 * HD
        column = pl.multiple_of(group * width, width)
        dkv_ref[:, pl.ds(column, width)] = dk_ref[...].astype(jnp.bfloat16)
        column = pl.multiple_of((pl.num_programs(0) + group) * width, width)
        dkv_ref[:, pl.ds(column, width)] = dv_ref[...].astype(jnp.bfloat16)
        if spec["bias"]:
            gather_diagonals(dtiles_ref, band_ref)


def attention_setup(queries, keyval, query_labels, key_labels, bias, causal, pairs):
    rows, keys = queries.shape[0], keyval.shape[0]
    qb, kb = min(256, rows), min(256, keys)
    skip = rows > qb
    pairs = pairs if skip else 3
    spec = dict(
        qb=qb,
        kb=kb,
        causal=causal,
        bias=bias is not None,
        pairs=pairs,
        tiles=keys // kb,
        skip=skip,
    )
    bounds = jnp.zeros((2, 1), jnp.int32)
    if skip:
        bounds = key_bounds(query_labels, key_labels, qb, kb)
    segq = query_labels[None, :]
    segk = jnp.broadcast_to(key_labels[:, None], (keys, TILE))
    groups = H // 2 // pairs
    width = 2 * HD * pairs
    specs = dict(
        q=pl.BlockSpec((qb, width), lambda group, block, bounds: (block, group)),
        k=pl.BlockSpec((keys, width), lambda group, block, bounds: (0, group)),
        v=pl.BlockSpec((keys, width), lambda group, block, bounds: (0, groups + group)),
        segq=pl.BlockSpec((1, qb), lambda group, block, bounds: (0, block)),
        segk=pl.BlockSpec((keys, TILE), lambda group, block, bounds: (0, 0)),
        lse=pl.BlockSpec((pairs, 2, qb), lambda group, block, bounds: (group, 0, block)),
        bias=pl.BlockSpec((2 * pairs, BAND, SPAN), lambda group, block, bounds: (group, 0, 0)),
        band=pl.BlockSpec(
            (2 * pairs, BAND, FOLD, SPAN), lambda group, block, bounds: (group, 0, 0, 0)
        ),
        whole=pl.BlockSpec((keys, 2 * H * HD), lambda group, block, bounds: (0, 0)),
    )
    scores = pltpu.VMEM((2 * pairs, keys // kb, kb, qb), jnp.float32)
    return spec, bounds, segq, segk, specs, (groups, rows // qb), scores


def attend_forward(queries, keyval, query_labels, key_labels, bias, causal):
    spec, bounds, segq, segk, specs, grid, scores = attention_setup(
        queries, keyval, query_labels, key_labels, bias, causal, 2
    )
    rows, keys = queries.shape[0], keyval.shape[0]
    work = H * rows * keys
    extra = ([specs["bias"]], [bias]) if bias is not None else ([], [])
    tiles = [pltpu.VMEM((2 * spec["pairs"], BAND, TILE, TILE), jnp.float32)] * len(extra[0])
    return pl.pallas_call(
        functools.partial(forward_kernel, spec),
        out_shape=(
            jax.ShapeDtypeStruct((rows, H * HD), jnp.bfloat16),
            jax.ShapeDtypeStruct((H // 2, 2, rows), jnp.float32),
        ),
        grid_spec=pltpu.PrefetchScalarGridSpec(
            num_scalar_prefetch=1,
            grid=grid,
            in_specs=[specs["q"], specs["k"], specs["v"], specs["segq"], specs["segk"]]
            + extra[0],
            out_specs=[specs["q"], specs["lse"]],
            scratch_shapes=[
                scores,
                pltpu.VMEM((2 * HD * spec["pairs"], keys), jnp.bfloat16),
            ]
            + tiles,
        ),
        compiler_params=pltpu.CompilerParams(vmem_limit_bytes=40 << 20),
        cost_estimate=pl.CostEstimate(
            flops=16 * HD * work, transcendentals=work, bytes_accessed=8 << 20
        ),
    )(bounds, queries, keyval, keyval, segq, segk, *extra[1])


def attend_backward(queries, keyval, query_labels, key_labels, bias, causal, lse, dmixture):
    spec, bounds, segq, segk, specs, grid, scores = attention_setup(
        queries, keyval, query_labels, key_labels, bias, causal, 1
    )
    rows, keys = queries.shape[0], keyval.shape[0]
    work = H * rows * keys
    extra = ([specs["bias"]], [bias]) if bias is not None else ([], [])
    tiles = [pltpu.VMEM((2 * spec["pairs"], BAND, TILE, TILE), jnp.float32)] * len(extra[0])
    band = (
        [jax.ShapeDtypeStruct((H, BAND, FOLD, SPAN), jnp.float32)] if bias is not None else []
    )
    out = pl.pallas_call(
        functools.partial(backward_kernel, spec),
        out_shape=[
            jax.ShapeDtypeStruct((rows, H * HD), jnp.bfloat16),
            jax.ShapeDtypeStruct((keys, 2 * H * HD), jnp.bfloat16),
        ]
        + band,
        grid_spec=pltpu.PrefetchScalarGridSpec(
            num_scalar_prefetch=1,
            grid=grid,
            in_specs=[
                specs["q"],
                specs["k"],
                specs["v"],
                specs["q"],
                specs["lse"],
                specs["segq"],
                specs["segk"],
            ]
            + extra[0],
            out_specs=[specs["q"], specs["whole"]] + [specs["band"]] * len(band),
            scratch_shapes=[
                scores,
                scores,
                pltpu.VMEM((keys, 2 * HD * spec["pairs"]), jnp.float32),
                pltpu.VMEM((keys, 2 * HD * spec["pairs"]), jnp.float32),
                pltpu.VMEM((2 * HD * spec["pairs"], keys), jnp.bfloat16),
            ]
            + tiles
            + tiles,
        ),
        compiler_params=pltpu.CompilerParams(vmem_limit_bytes=48 << 20),
        cost_estimate=pl.CostEstimate(
            flops=40 * HD * work, transcendentals=work, bytes_accessed=16 << 20
        ),
    )(bounds, queries, keyval, keyval, dmixture, lse, segq, segk, *extra[1])
    return (out[0], out[1], out[2] if bias is not None else None)


def product(former, latter):
    return jnp.dot(former, latter, preferred_element_type=jnp.float32)


def transpose_product(former, latter):
    return lax.dot_general(
        former, latter, (((0,), (0,)), ((), ())), preferred_element_type=jnp.float32
    )


def product_transposed(former, latter):
    return lax.dot_general(
        former, latter, (((1,), (1,)), ((), ())), preferred_element_type=jnp.float32
    )


def smooth_gate(value):
    return jax.nn.gelu(value, approximate=True)


def norm_forward(stream, norm_gain):
    return (
        stream * lax.rsqrt(jnp.mean(stream * stream, axis=-1, keepdims=True) + EPSILON) * norm_gain
    )


def norm_backward(stream, norm_gain, gradient):
    outcome, pullback = jax.vjp(norm_forward, stream, norm_gain)
    return pullback(gradient)


def attention_forward(stream, norm_gain, wquery, wkeyval, wproj, layout, memory):
    normed = norm_forward(stream, norm_gain).astype(jnp.bfloat16)
    queries = product(normed, wquery).astype(jnp.bfloat16)
    source = normed if memory is None else memory
    keyval = product(source, wkeyval).astype(jnp.bfloat16)
    mixture, logsum = attend_forward(queries, keyval, *layout)
    return (stream + product(mixture, wproj), (normed, queries, keyval, mixture, logsum))


def attention_backward(
    grads, names, stream, norm_gain, wquery, wkeyval, wproj, layout, memory, stored, gradient
):
    normed, queries, keyval, mixture, logsum = stored
    gradient_low = gradient.astype(jnp.bfloat16)
    grads.add(names[2], mixture, gradient_low)
    dmixture = product_transposed(gradient_low, wproj).astype(jnp.bfloat16)
    dquery_low, dkeyval_low, band = attend_backward(queries, keyval, *layout, logsum, dmixture)
    source = normed if memory is None else memory
    grads.add(names[0], normed, dquery_low)
    grads.add(names[1], source, dkeyval_low)
    dnormed = product_transposed(dquery_low, wquery)
    dsource = product_transposed(dkeyval_low, wkeyval)
    if memory is None:
        dnormed = dnormed + dsource
        dsource = None
    dstream, dgain = norm_backward(stream, norm_gain, dnormed)
    return (gradient + dstream, dgain, band, dsource)


def feed_forward(stream, norm_gain, winner, wouter):
    normed = norm_forward(stream, norm_gain).astype(jnp.bfloat16)
    before = product(normed, winner)
    hidden = smooth_gate(before).astype(jnp.bfloat16)
    return (stream + product(hidden, wouter), (normed, before, hidden))


def feed_backward(grads, names, stream, norm_gain, winner, wouter, stored, gradient):
    normed, before, hidden = stored
    gradient_low = gradient.astype(jnp.bfloat16)
    grads.add(names[1], hidden, gradient_low)
    dhidden = product_transposed(gradient_low, wouter)
    gate_value, gate_pullback = jax.vjp(smooth_gate, before)
    dbefore = gate_pullback(dhidden)[0].astype(jnp.bfloat16)
    grads.add(names[0], normed, dbefore)
    dnormed = product_transposed(dbefore, winner)
    dstream, dgain = norm_backward(stream, norm_gain, dnormed)
    return (gradient + dstream, dgain)


def index_bits(devices):
    return devices.bit_length() - 1


class Links:
    def __init__(self, mesh):
        self.sizes = dict(mesh.shape)
        self.bits = [("fsdp", bit) for bit in range(index_bits(self.sizes["fsdp"]))]
        self.bits += [("dp", bit) for bit in range(index_bits(self.sizes["dp"]))]

    def side(self, axis, bit):
        return lax.rem(lax.axis_index(axis) // (1 << bit), 2)

    def partner(self, axis, bit):
        return {axis: lax.axis_index(axis) + (1 - 2 * self.side(axis, bit)) * (1 << bit)}

    def orders(self):
        core, row = ("dp", 0), ("fsdp", 0)
        rest = [key for key in self.bits if key not in (core, row)]
        third = [core] + rest[1:2] + rest[:1] + [row] + rest[2:]
        return ([core] + rest[:1] + [row] + rest[1:], [core, row] + rest, third)

    def swap(self, value, axis, bit):
        pairs = [(place, place ^ (1 << bit)) for place in range(self.sizes[axis])]
        return lax.ppermute(value, axis, pairs)

    def total(self, value):
        for key in self.bits:
            value = value + self.swap(value, *key)
        return value

    def gather_small(self, shard):
        other = self.swap(shard, "fsdp", 0)
        first = lax.axis_index("fsdp") == 0
        return jnp.concatenate(
            [jnp.where(first, shard, other), jnp.where(first, other, shard)], axis=0
        )

    def devices(self):
        return self.sizes["dp"] * self.sizes["fsdp"]

    def place(self):
        return lax.axis_index("dp") * self.sizes["fsdp"] + lax.axis_index("fsdp")


def pick(ref, lead, spot, count, side):
    return ref.at[(lead,) + (slice(None),) * spot + (side,) + (slice(None),) * (count - spot - 1)]


def reduce_kernel(links, chunks, g_ref, out_ref, own_ref, *rest):
    stages = len(links.bits)
    sums, (send_sem, recv_sem, own_sem) = rest[:stages], rest[stages:]
    plans = []
    for order in links.orders():
        left = list(reversed(links.bits))
        plan = []
        for key in order:
            plan.append((key, left.index(key), len(left)))
            left.remove(key)
        plans.append(plan)
    kinds = len(plans)

    barrier = pltpu.get_barrier_semaphore()
    for key in links.bits:
        pl.semaphore_signal(
            barrier,
            inc=1,
            device_id=links.partner(*key),
            device_id_type=pl.DeviceIdType.MESH,
        )
    pl.semaphore_wait(barrier, stages)

    def source(stage, chunk, kind, away):
        key, spot, count = plans[kind][stage]
        side = links.side(*key)
        ref = g_ref if stage == 0 else sums[stage - 1]
        return pick(ref, chunk, spot, count, 1 - side if away else side)

    def send(stage, chunk, kind):
        key, _, _ = plans[kind][stage]
        return pltpu.make_async_remote_copy(
            src_ref=source(stage, chunk, kind, True),
            dst_ref=sums[stage].at[chunk],
            send_sem=send_sem.at[stage, chunk],
            recv_sem=recv_sem.at[stage, chunk],
            device_id=links.partner(*key),
            device_id_type=pl.DeviceIdType.MESH,
        )

    def fetch(chunk, kind):
        slot = lax.rem(chunk, HOLD)
        return pltpu.make_async_copy(
            source(0, chunk, kind, False), own_ref.at[slot], own_sem.at[slot]
        )

    def step(group, carry):
        for turn in range(kinds):
            now = group * kinds + turn

            @pl.when(now < chunks)
            def _():
                send(0, now, turn).start()
                fetch(now, turn).start()

            for stage in range(stages):
                chunk = now - DELAY * (stage + 1)
                kind = (turn - DELAY * (stage + 1)) % kinds

                @pl.when((chunk >= 0) & (chunk < chunks))
                def _():
                    send(stage, chunk, kind).wait()
                    if stage == 0:
                        fetch(chunk, kind).wait()
                        mine = own_ref[lax.rem(chunk, HOLD)]
                    else:
                        mine = source(stage, chunk, kind, False)[...]
                    if stage < stages - 1:
                        sums[stage][chunk] = sums[stage][chunk] + mine
                        send(stage + 1, chunk, kind).start()
                    else:
                        out_ref[chunk] = sums[stage][chunk].astype(jnp.float32) + mine.astype(
                            jnp.float32
                        )

        return carry

    slots = chunks + DELAY * stages
    lax.fori_loop(0, (slots + kinds - 1) // kinds, step, 0)


def reduce_chunks(links, grads, collective_id):
    chunks, _, rows, columns = grads.shape
    stages = len(links.bits)
    sums = [
        pltpu.VMEM((chunks,) + (2,) * (stages - 1 - stage) + (rows, columns), jnp.bfloat16)
        for stage in range(stages)
    ]
    return pl.pallas_call(
        functools.partial(reduce_kernel, links, chunks),
        out_shape=jax.ShapeDtypeStruct((chunks, rows, columns), jnp.float32),
        in_specs=[pl.BlockSpec(memory_space=pltpu.HBM)],
        out_specs=pl.BlockSpec(memory_space=pltpu.VMEM),
        scratch_shapes=[
            pltpu.VMEM((HOLD,) + (2,) * (stages - 1) + (rows, columns), jnp.bfloat16)
        ]
        + sums
        + [
            pltpu.SemaphoreType.DMA((stages, chunks)),
            pltpu.SemaphoreType.DMA((stages, chunks)),
            pltpu.SemaphoreType.DMA((HOLD,)),
        ],
        compiler_params=pltpu.CompilerParams(
            collective_id=collective_id, has_side_effects=True, vmem_limit_bytes=58 << 20
        ),
    )(grads.reshape((chunks,) + (2,) * stages + (rows, columns)))


def fold_grad(grad, devices, width):
    rows, columns = grad.shape
    deep, wide = rows // width, columns // width
    r = rows // devices // deep
    grad = grad.astype(jnp.bfloat16).reshape(devices, deep, r, wide, 2, width // 2)
    return grad.transpose(1, 3, 0, 4, 2, 5).reshape(deep * wide, devices, 2 * r, width // 2)


def unfold_share(chunks, rows, columns):
    count, folded, half = chunks.shape
    deep, wide = rows * 2 // folded, columns // (2 * half)
    chunks = chunks.reshape(deep, wide, 2, folded // 2, half)
    return chunks.transpose(0, 3, 1, 2, 4).reshape(rows, columns)


def gather_kernel(links, units, count, *refs):
    shards, wholes, held = refs[:count], refs[count : 2 * count], refs[2 * count : 3 * count]
    send_sem, recv_sem, local_sem = refs[3 * count :]
    core, mesh_id = ("dp", 0), pl.DeviceIdType.MESH
    keys = [("dp", 1), ("dp", 2), core]
    orders = [[keys[0], keys[1], core], [keys[1], keys[0], core]]
    row = ("fsdp", 0)
    place = lax.axis_index("fsdp")

    barrier = pltpu.get_barrier_semaphore()
    for key in [row] + keys:
        pl.semaphore_signal(
            barrier, inc=1, device_id=links.partner(*key), device_id_type=mesh_id
        )
    pl.semaphore_wait(barrier, 1 + len(keys))

    def piece(known):
        return tuple(slice(None) if key in known else links.side(*key) for key in keys)

    def send(stage, unit):
        order = orders[unit % 2]
        number, rows, columns = units[unit]
        if stage == 0:
            key, where = row, piece([])
            src = shards[number].at[where + (rows, columns)]
        else:
            key, where = order[stage - 1], piece(order[: stage - 1])
            src = wholes[number].at[(1 - place,) + where + (rows, columns)]
        dst = wholes[number].at[
            (place if stage == 0 else 1 - place,) + where + (rows, columns)
        ]
        return pltpu.make_async_remote_copy(
            src_ref=src,
            dst_ref=dst,
            send_sem=send_sem.at[stage, unit],
            recv_sem=recv_sem.at[stage, unit],
            device_id=links.partner(*key),
            device_id_type=mesh_id,
        )

    def load(number):
        return pltpu.make_async_copy(shards[number], held[number], local_sem.at[0, number])

    def keep(number):
        return pltpu.make_async_copy(
            held[number], wholes[number].at[place], local_sem.at[1, number]
        )

    stages = 1 + len(keys)
    for unit in range(len(units)):
        send(0, unit).start()
    for number in range(count):
        load(number).start()
    for slot in range(len(units) + LAG * (stages - 1)):
        for stage in range(stages):
            unit = slot - LAG * stage
            if 0 <= unit < len(units):
                send(stage, unit).wait()
                if stage + 1 < stages:
                    send(stage + 1, unit).start()
        if slot < count:
            load(slot).wait()
            keep(slot).start()
    for number in range(count):
        keep(number).wait()


def gather_units(shards, width):
    least = min(shard.shape[0] for shard in shards)
    units = []
    for number, shard in enumerate(shards):
        deep, wide = shard.shape[0] // least, shard.shape[1] // width
        rows = shard.shape[0] // 8 // deep
        for part in range(deep):
            for column in range(wide):
                units.append(
                    (
                        number,
                        slice(part * rows, (part + 1) * rows),
                        slice(column * width, (column + 1) * width),
                    )
                )
    return units


def gather_weights(links, shards, collective_id):
    count = len(shards)
    units = gather_units(shards, shards[0].shape[1])
    split = [
        shard.reshape(2, 2, 2, shard.shape[0] // 8, shard.shape[1]) for shard in shards
    ]
    wholes = pl.pallas_call(
        functools.partial(gather_kernel, links, units, count),
        out_shape=[jax.ShapeDtypeStruct((2,) + piece.shape, piece.dtype) for piece in split],
        in_specs=[pl.BlockSpec(memory_space=pltpu.HBM)] * count,
        out_specs=[pl.BlockSpec(memory_space=pltpu.HBM)] * count,
        scratch_shapes=[pltpu.VMEM(piece.shape, piece.dtype) for piece in split]
        + [
            pltpu.SemaphoreType.DMA((4, len(units))),
            pltpu.SemaphoreType.DMA((4, len(units))),
            pltpu.SemaphoreType.DMA((2, count)),
        ],
        compiler_params=pltpu.CompilerParams(
            collective_id=collective_id, has_side_effects=True, vmem_limit_bytes=60 << 20
        ),
    )(*split)
    return [
        whole.reshape(2 * shard.shape[0], shard.shape[1]) for whole, shard in zip(wholes, shards)
    ]


def weight_kernel(deep, x_ref, dy_ref, *rest):
    out_ref = rest[-1]
    total = lax.dot_general(
        x_ref[...], dy_ref[...], (((0,), (0,)), ((), ())), preferred_element_type=jnp.float32
    )
    half = total.shape[1] // 2
    rows = out_ref.shape[2] // 2
    total = total.reshape(out_ref.shape[1], deep, rows, 2 * half)
    for part in range(deep):
        piece = total[:, part]
        piece = jnp.concatenate([piece[:, :, :half], piece[:, :, half:]], axis=1)
        out_ref[part] = piece.astype(jnp.bfloat16)


def weight_chunks(x, dy, chunks, start, count, devices, width):
    rows, deep, wide = x.shape[0], x.shape[1] // width, dy.shape[1] // width
    r = width // devices
    if deep == 1:
        specs = [
            pl.BlockSpec((rows, width), lambda w: (0, 0)),
            pl.BlockSpec((rows, width), lambda w: (0, w)),
        ]
        out_spec = pl.BlockSpec((1, devices, 2 * r, width // 2), lambda w: (start + w, 0, 0, 0))
    else:
        specs = [
            pl.BlockSpec((rows, width), lambda w: (0, w)),
            pl.BlockSpec((rows, width), lambda w: (0, 0)),
        ]
        out_spec = pl.BlockSpec(
            (deep, devices // deep, 2 * r, width // 2), lambda w: (start // deep, w, 0, 0)
        )
    extra = [] if chunks is None else [chunks]
    return pl.pallas_call(
        functools.partial(weight_kernel, deep),
        out_shape=jax.ShapeDtypeStruct((count, devices, 2 * r, width // 2), jnp.bfloat16),
        grid=(max(deep, wide),),
        in_specs=specs + [pl.BlockSpec(memory_space=pltpu.HBM)] * len(extra),
        out_specs=out_spec,
        input_output_aliases={2: 0} if extra else {},
        compiler_params=pltpu.CompilerParams(vmem_limit_bytes=40 << 20),
        cost_estimate=pl.CostEstimate(
            flops=2 * rows * x.shape[1] * dy.shape[1],
            transcendentals=0,
            bytes_accessed=2 * (x.size + dy.size + x.shape[1] * dy.shape[1]),
        ),
    )(x, dy, *extra)


class Gradients:
    def __init__(self, links, width, shapes):
        self.links, self.width, self.shapes = links, width, shapes
        self.starts, self.count, self.scattered = {}, 0, {}
        for name, (rows, columns) in shapes.items():
            self.starts[name] = self.count
            self.count += rows // width * (columns // width)
        self.chunks = None

    def scatter(self, name, x, dy):
        grad = transpose_product(x, dy).astype(jnp.bfloat16)
        share = lax.psum_scatter(grad, ("dp", "fsdp"), scatter_dimension=0, tiled=True)
        self.scattered[name] = share.astype(jnp.float32)

    def add(self, name, x, dy):
        if name in OFFLOADED:
            self.scatter(name, x, dy)
            return
        devices, start = self.links.devices(), self.starts[name]
        if self.width // devices % 8 == 0:
            self.chunks = weight_chunks(
                x, dy, self.chunks, start, self.count, devices, self.width
            )
            return
        fresh = fold_grad(transpose_product(x, dy), devices, self.width)
        if self.chunks is None:
            self.chunks = jnp.zeros((self.count,) + fresh.shape[1:], fresh.dtype)
        self.chunks = lax.dynamic_update_slice_in_dim(self.chunks, fresh, start, 0)

    def shares(self, collective_id):
        shares = reduce_chunks(self.links, self.chunks, collective_id)
        devices = self.links.devices()
        shapes = [(rows // devices, columns) for rows, columns in self.shapes.values()]
        if self.width // devices % 8 == 0:
            result = pl.pallas_call(
                functools.partial(unfold_kernel, self.width),
                out_shape=[jax.ShapeDtypeStruct(shape, jnp.float32) for shape in shapes],
            )(shares)
            return dict(zip(self.shapes, result)) | self.scattered
        result = dict(self.scattered)
        for (name, (rows, columns)), shape in zip(self.shapes.items(), shapes):
            start = self.starts[name]
            count = rows // self.width * (columns // self.width)
            result[name] = unfold_share(shares[start : start + count], *shape)
        return result


def unfold_kernel(width, shares_ref, *out_refs):
    chunk, r, half = 0, shares_ref.shape[1] // 2, width // 2
    for out_ref in out_refs:
        for row in range(0, out_ref.shape[0], r):
            for column in range(0, out_ref.shape[1], width):
                for part in range(2):
                    out_ref[
                        row : row + r, column + part * half : column + (part + 1) * half
                    ] = shares_ref[chunk, part * r : (part + 1) * r, :]
                chunk += 1


def body(
    links,
    enc_tokens,
    dec_tokens,
    enc_segments,
    dec_segments,
    enc_upstream,
    dec_upstream,
    encoder_query,
    encoder_keyval,
    encoder_proj,
    encoder_inner,
    encoder_outer,
    encoder_gains,
    encoder_table,
    decoder_query,
    decoder_keyval,
    decoder_proj,
    cross_query,
    cross_keyval,
    cross_proj,
    decoder_inner,
    decoder_outer,
    decoder_gains,
    decoder_table,
):
    small = jnp.concatenate(
        [encoder_gains, decoder_gains]
        + [
            jnp.concatenate([encoder_table, decoder_table], axis=0).reshape(
                encoder_gains.shape[0], -1
            )
        ],
        axis=1,
    )
    small = links.gather_small(small)
    enc_gains = small[:, 0:2].astype(jnp.float32)
    dec_gains = small[:, 2:5].astype(jnp.float32)
    tables = small[:, 5:].reshape(2, 2, NB // 2, H)
    enc_bias = band_bias(tables[:, 0].reshape(NB, H), encoder_bucket)
    dec_bias = band_bias(tables[:, 1].reshape(NB, H), decoder_bucket)

    shards = [
        encoder_query,
        encoder_keyval,
        encoder_proj,
        encoder_inner,
        encoder_outer,
        decoder_query,
        decoder_keyval,
        decoder_proj,
        cross_query,
        cross_keyval,
        cross_proj,
        decoder_inner,
        decoder_outer,
    ]
    shards = dict(zip(NAMES, shards))
    later = [shards.pop(name) for name in OFFLOADED]
    weights = dict(zip(shards, gather_weights(links, list(shards.values()), 1)))
    weights["equery"], *later = lax.optimization_barrier((weights["equery"], *later))
    for name, shard in zip(OFFLOADED, later):
        weights[name] = lax.all_gather(shard, "fsdp", axis=0, tiled=True)
    order = [
        "dinner",
        "douter",
        "einner",
        "eouter",
        "cproj",
        "cquery",
        "ckeyval",
        "dproj",
        "dquery",
        "dkeyval",
        "eproj",
        "equery",
        "ekeyval",
    ]
    grads = Gradients(
        links,
        encoder_query.shape[1],
        {name: weights[name].shape for name in order if name not in OFFLOADED},
    )

    enc_layout = (enc_segments, enc_segments, enc_bias, False)
    dec_layout = (dec_segments, dec_segments, dec_bias, True)
    cross_layout = (dec_segments, enc_segments, None, False)

    enc_stream = enc_tokens.astype(jnp.float32)
    enc_middle, enc_self = attention_forward(
        enc_stream, enc_gains[:, 0], weights["equery"], weights["ekeyval"], weights["eproj"], enc_layout, None
    )
    enc_final, enc_ffn = feed_forward(enc_middle, enc_gains[:, 1], weights["einner"], weights["eouter"])
    memory = enc_final.astype(jnp.bfloat16)

    dec_stream = dec_tokens.astype(jnp.float32)
    after_self, dec_self = attention_forward(
        dec_stream, dec_gains[:, 0], weights["dquery"], weights["dkeyval"], weights["dproj"], dec_layout, None
    )
    after_cross, dec_cross = attention_forward(
        after_self, dec_gains[:, 1], weights["cquery"], weights["ckeyval"], weights["cproj"], cross_layout, memory
    )
    dec_final, dec_ffn = feed_forward(after_cross, dec_gains[:, 2], weights["dinner"], weights["douter"])


    dec_live = (dec_segments >= 0).astype(jnp.float32)[:, None]
    gradient = dec_upstream.astype(jnp.float32) * dec_live
    gradient, dgain_ffn = feed_backward(
        grads, ("dinner", "douter"), after_cross, dec_gains[:, 2], weights["dinner"], weights["douter"], dec_ffn, gradient
    )
    gradient, dgain_cross, _, memory_grad = (
        attention_backward(
            grads,
            ("cquery", "ckeyval", "cproj"),
            after_self,
            dec_gains[:, 1],
            weights["cquery"],
            weights["ckeyval"],
            weights["cproj"],
            cross_layout,
            memory,
            dec_cross,
            gradient,
        )
    )
    dec_gradient, dgain_self, dec_band, _ = (
        attention_backward(
            grads,
            ("dquery", "dkeyval", "dproj"),
            dec_stream,
            dec_gains[:, 0],
            weights["dquery"],
            weights["dkeyval"],
            weights["dproj"],
            dec_layout,
            None,
            dec_self,
            gradient,
        )
    )

    enc_live = (enc_segments >= 0).astype(jnp.float32)[:, None]
    gradient = enc_upstream.astype(jnp.float32) * enc_live + memory_grad
    gradient, egain_ffn = feed_backward(
        grads, ("einner", "eouter"), enc_middle, enc_gains[:, 1], weights["einner"], weights["eouter"], enc_ffn, gradient
    )
    enc_gradient, egain_self, enc_band, _ = (
        attention_backward(
            grads,
            ("equery", "ekeyval", "eproj"),
            enc_stream,
            enc_gains[:, 0],
            weights["equery"],
            weights["ekeyval"],
            weights["eproj"],
            enc_layout,
            None,
            enc_self,
            gradient,
        )
    )

    table_grads = [
        band_table_grad(enc_band, encoder_bucket),
        band_table_grad(dec_band, decoder_bucket),
    ]
    gain_grads = jnp.stack([egain_self, egain_ffn, dgain_self, dgain_cross, dgain_ffn])
    flat = jnp.concatenate([gain_grads.reshape(-1)] + [grad.reshape(-1) for grad in table_grads])
    flat = links.total(flat.reshape(-1, TILE)).reshape(-1)
    width = gain_grads.shape[1]
    flat, grads.chunks = lax.optimization_barrier((flat, grads.chunks))
    tables_grad = flat[5 * width :].reshape(2, NB, H)
    own = width // links.devices()
    gains_share = lax.dynamic_slice_in_dim(
        flat[: 5 * width].reshape(5, width), links.place() * own, own, 1
    ).T
    shares = grads.shares(0)
    return (
        memory,
        dec_final.astype(jnp.bfloat16),
        enc_gradient,
        dec_gradient,
        shares["equery"],
        shares["ekeyval"],
        shares["eproj"],
        shares["einner"],
        shares["eouter"],
        gains_share[:, 0:2],
        tables_grad[0],
        shares["dquery"],
        shares["dkeyval"],
        shares["dproj"],
        shares["cquery"],
        shares["ckeyval"],
        shares["cproj"],
        shares["dinner"],
        shares["douter"],
        gains_share[:, 2:5],
        tables_grad[1],
    )


def solution(mesh):
    in_specs = (
        P(("dp", "fsdp"), None),
        P(("dp", "fsdp"), None),
        P(("dp", "fsdp")),
        P(("dp", "fsdp")),
        P(("dp", "fsdp"), None),
        P(("dp", "fsdp"), None),
        P("fsdp", None),
        P("fsdp", None),
        P("fsdp", None),
        P("fsdp", None),
        P("fsdp", None),
        P("fsdp", None),
        P("fsdp", None),
        P("fsdp", None),
        P("fsdp", None),
        P("fsdp", None),
        P("fsdp", None),
        P("fsdp", None),
        P("fsdp", None),
        P("fsdp", None),
        P("fsdp", None),
        P("fsdp", None),
        P("fsdp", None),
    )
    out_specs = (
        P(("dp", "fsdp"), None),
        P(("dp", "fsdp"), None),
        P(("dp", "fsdp"), None),
        P(("dp", "fsdp"), None),
        P(("dp", "fsdp"), None),
        P(("dp", "fsdp"), None),
        P(("dp", "fsdp"), None),
        P(("dp", "fsdp"), None),
        P(("dp", "fsdp"), None),
        P(("dp", "fsdp"), None),
        P(),
        P(("dp", "fsdp"), None),
        P(("dp", "fsdp"), None),
        P(("dp", "fsdp"), None),
        P(("dp", "fsdp"), None),
        P(("dp", "fsdp"), None),
        P(("dp", "fsdp"), None),
        P(("dp", "fsdp"), None),
        P(("dp", "fsdp"), None),
        P(("dp", "fsdp"), None),
        P(),
    )
    return jax.shard_map(
        functools.partial(body, Links(mesh)), mesh=mesh, in_specs=in_specs, out_specs=out_specs, check_vma=False)
```

```python
import functools
import math

import jax
import jax.numpy as jnp
import numpy as np
from jax import lax
from jax.experimental import pallas as pl
from jax.experimental.pallas import tpu as pltpu
from jax.sharding import PartitionSpec as P

H = 12
HD = 64
NB = 32
TILE = 128
BAND = 5
EPSILON = 1e-06
MASKED = -1e30
ENC_EDGES = (12, 16, 23, 32, 46, 64, 91)
DEC_EDGES = tuple((math.ceil(16 * 2 ** (3 * power / 16)) for power in range(1, 16)))
PADDING_LABEL = 1 << 20
SPAN = 2 * TILE
FOLD = 8
LAG = 3
DELAY = 2
HOLD = DELAY + 1
OFFLOADED = ("dinner", "douter")
LATER = ("dinner",)
NAMES = (
    "equery",
    "ekeyval",
    "eproj",
    "einner",
    "eouter",
    "dquery",
    "dkeyval",
    "dproj",
    "cquery",
    "ckeyval",
    "cproj",
    "dinner",
    "douter",
)


def encoder_bucket(distance):
    reach = np.abs(distance)
    farther = 8 + sum((reach >= threshold).astype(np.int32) for threshold in ENC_EDGES)
    return np.where(reach < 8, reach, farther) + 16 * (distance < 0).astype(np.int32)


def decoder_bucket(distance):
    ahead = np.maximum(distance, 0)
    farther = 16 + sum((ahead >= threshold).astype(np.int32) for threshold in DEC_EDGES)
    return np.where(ahead < 16, ahead, farther)


def band_distances(rows):
    step = np.arange(BAND)[:, None, None] - 2
    row = np.arange(rows)[None, :, None]
    lane = np.arange(SPAN)[None, None, :]
    lane = np.where(lane < TILE, lane, lane - SPAN)
    return step * TILE + lane - row


def bucket_onehot(bucket_of, rows, dtype):
    bucket = jnp.asarray(bucket_of(band_distances(rows)).reshape(1, -1), jnp.int32)
    return (bucket == lax.broadcasted_iota(jnp.int32, (NB, 1), 0)).astype(dtype)


def band_bias(table, bucket_of):
    onehot = bucket_onehot(bucket_of, 1, jnp.bfloat16)
    flat = lax.dot_general(
        table, onehot, (((0,), (0,)), ((), ())), preferred_element_type=jnp.float32
    )
    return flat.reshape(H, BAND, SPAN)


def band_table_grad(band, bucket_of):
    return lax.dot_general(
        bucket_onehot(bucket_of, FOLD, jnp.float32),
        band.reshape(H, BAND * FOLD * SPAN),
        (((1,), (1,)), ((), ())),
        precision=lax.Precision.HIGHEST,
        preferred_element_type=jnp.float32,
    )


def key_bounds(query_labels, key_labels, query_rows, key_rows):
    queries = jnp.where(query_labels < 0, PADDING_LABEL, query_labels).reshape(-1, query_rows)
    keys = jnp.where(key_labels < 0, PADDING_LABEL, key_labels)
    first = jnp.sum((keys[None, :] < queries[:, :1]).astype(jnp.int32), axis=1)
    last = jnp.sum((keys[None, :] <= queries[:, -1:]).astype(jnp.int32), axis=1)
    return jnp.stack([first // key_rows, (last + key_rows - 1) // key_rows])


def fold_rows(value, combine):
    rows = value.shape[0]
    while rows > 8:
        rows //= 2
        value = combine(value[:rows], value[rows:])
    return value


def head_parts(block):
    lane = lax.broadcasted_iota(jnp.int32, block.shape, 1)
    zero = jnp.zeros_like(block)
    return (jnp.where(lane < HD, block, zero), jnp.where(lane < HD, zero, block))


def flip(value):
    return value.astype(jnp.float32).T


def band_index(query_tile, key_tile):
    return jnp.clip(query_tile - key_tile, -2, 2) + 2


def spread_bias(bias_ref, tiles_ref):
    for head in range(tiles_ref.shape[0]):
        for step in range(BAND):
            row = bias_ref[head, step : step + 1, :]
            if step in (0, BAND - 1):
                tiles_ref[head, step] = jnp.broadcast_to(row[:, :TILE], (TILE, TILE))
            else:
                wide = jnp.broadcast_to(row, (TILE, SPAN))
                wide = pltpu.roll(wide, 0, 1, stride=1, stride_axis=0)
                tiles_ref[head, step] = wide[:, :TILE]


def gather_diagonals(tiles_ref, band_ref):
    for head in range(tiles_ref.shape[0]):
        for step in range(BAND):
            tile = tiles_ref[head, step]
            tile = jnp.concatenate([tile, jnp.zeros_like(tile)], axis=1)
            rows = TILE
            while rows > FOLD:
                rows //= 2
                tile = tile[:rows] + pltpu.roll(tile[rows:], SPAN - rows, 1)
            band_ref[head, step] = tile


def tile_mask(spec, key_tile, query_block, segk_ref, segq_ref):
    rows, lanes = spec["kb"], spec["qb"]
    start = pl.multiple_of(key_tile * rows, rows) if spec["skip"] else key_tile * rows
    labels = segk_ref[pl.ds(start, rows), :]
    labels = jnp.concatenate([labels] * (lanes // TILE), axis=1)
    mask = labels == segq_ref[...]
    if spec["causal"]:
        key = lax.broadcasted_iota(jnp.int32, (rows, lanes), 0) + key_tile * rows
        query = lax.broadcasted_iota(jnp.int32, (rows, lanes), 1) + query_block * lanes
        mask = mask & (key <= query)
    return mask


def tile_bias(spec, head, key_tile, query_block, bias_ref):
    rows, lanes = spec["kb"] // TILE, spec["qb"] // TILE
    return jnp.concatenate(
        [
            jnp.concatenate(
                [
                    bias_ref[
                        head, band_index(query_block * lanes + lane, key_tile * rows + row)
                    ]
                    for lane in range(lanes)
                ],
                axis=1,
            )
            for row in range(rows)
        ],
        axis=0,
    )


def dot_rows(former, latter):
    return lax.dot_general(
        former, latter, (((1,), (1,)), ((), ())), preferred_element_type=jnp.float32
    )


def dot_plain(former, latter):
    return jnp.dot(former, latter, preferred_element_type=jnp.float32)


def for_counts(spec, first, last, run):
    if not spec["skip"]:
        run(0, spec["tiles"])
        return
    for count in range(1, spec["tiles"] + 1):
        pl.when(last - first == count)(functools.partial(run, first, count))


def forward_kernel(spec, bounds_ref, q_ref, k_ref, v_ref, segq_ref, segk_ref, *rest):
    bias_ref, rest = (rest[0], rest[1:]) if spec["bias"] else (None, rest)
    o_ref, lse_ref, score_ref, vt_ref, rest = *rest[:4], rest[4:]
    tiles_ref = rest[0] if spec["bias"] else None
    kb, qb, pairs = spec["kb"], spec["qb"], spec["pairs"]
    block = pl.program_id(1)

    @pl.when(block == 0)
    def _():
        for pair in range(pairs):
            span = slice(pair * 2 * HD, (pair + 1) * 2 * HD)
            vt_ref[span, :] = flip(v_ref[:, span]).astype(jnp.bfloat16)
        if spec["bias"]:
            spread_bias(bias_ref, tiles_ref)

    def run(first, count):
        starts = [(first + tile) * kb for tile in range(count)]
        if spec["skip"]:
            starts = [pl.multiple_of(start, kb) for start in starts]
        for pair in range(pairs):
            span = slice(pair * 2 * HD, (pair + 1) * 2 * HD)
            parts = head_parts(q_ref[:, span])
            mixed, logsum = [], []
            for head in range(2):
                number = 2 * pair + head
                top = None
                for tile in range(count):
                    s = dot_rows(k_ref[pl.ds(starts[tile], kb), span], parts[head])
                    if spec["bias"]:
                        s = s + tile_bias(spec, number, first + tile, block, tiles_ref)
                    mask = tile_mask(spec, first + tile, block, segk_ref, segq_ref)
                    s = jnp.where(mask, s, MASKED)
                    score_ref[number, tile] = s
                    peak = fold_rows(s, jnp.maximum)
                    top = peak if top is None else jnp.maximum(top, peak)
                top = jnp.max(top, axis=0, keepdims=True)
                total = None
                for tile in range(count):
                    e = jnp.exp(score_ref[number, tile] - top)
                    score_ref[number, tile] = e
                    part = fold_rows(e, jnp.add)
                    total = part if total is None else total + part
                total = jnp.sum(total, axis=0, keepdims=True)
                scale = 1.0 / total
                mix = None
                for tile in range(count):
                    weights = (score_ref[number, tile] * scale).astype(jnp.bfloat16)
                    rows = slice(number * HD, (number + 1) * HD)
                    part = dot_plain(vt_ref[rows, pl.ds(starts[tile], kb)], weights)
                    mix = part if mix is None else mix + part
                mixed.append(mix)
                logsum.append(top + jnp.log(total))
            o_ref[:, span] = flip(jnp.concatenate(mixed, axis=0)).astype(jnp.bfloat16)
            lse_ref[pair] = jnp.concatenate(logsum, axis=0)

    for_counts(spec, bounds_ref[0, block], bounds_ref[1, block], run)


def backward_kernel(
    spec, bounds_ref, q_ref, k_ref, v_ref, do_ref, lse_ref, segq_ref, segk_ref, *rest
):
    bias_ref, rest = (rest[0], rest[1:]) if spec["bias"] else (None, rest)
    dq_ref, dkv_ref, rest = rest[0], rest[1], rest[2:]
    band_ref, rest = (rest[0], rest[1:]) if spec["bias"] else (None, rest)
    p_ref, dp_ref, dk_ref, dv_ref, kt_ref, rest = *rest[:5], rest[5:]
    tiles_ref, dtiles_ref = rest if spec["bias"] else (None, None)
    kb, qb, pairs = spec["kb"], spec["qb"], spec["pairs"]
    group, block = pl.program_id(0), pl.program_id(1)

    @pl.when(block == 0)
    def _():
        for pair in range(pairs):
            span = slice(pair * 2 * HD, (pair + 1) * 2 * HD)
            kt_ref[span, :] = flip(k_ref[:, span]).astype(jnp.bfloat16)
        dk_ref[...] = jnp.zeros_like(dk_ref)
        dv_ref[...] = jnp.zeros_like(dv_ref)
        if spec["bias"]:
            spread_bias(bias_ref, tiles_ref)
            dtiles_ref[...] = jnp.zeros_like(dtiles_ref)

    def run(first, count):
        starts = [(first + tile) * kb for tile in range(count)]
        if spec["skip"]:
            starts = [pl.multiple_of(start, kb) for start in starts]
        for pair in range(pairs):
            span = slice(pair * 2 * HD, (pair + 1) * 2 * HD)
            parts = head_parts(q_ref[:, span])
            dparts = head_parts(do_ref[:, span])
            lse = lse_ref[pair]
            stacked = jnp.concatenate(parts, axis=0)
            dstacked = jnp.concatenate(dparts, axis=0)
            deltas = []
            for head in range(2):
                number = 2 * pair + head
                delta = None
                for tile in range(count):
                    here = pl.ds(starts[tile], kb)
                    s = dot_rows(k_ref[here, span], parts[head])
                    if spec["bias"]:
                        s = s + tile_bias(spec, number, first + tile, block, tiles_ref)
                    mask = tile_mask(spec, first + tile, block, segk_ref, segq_ref)
                    p = jnp.exp(jnp.where(mask, s, MASKED) - lse[head : head + 1])
                    dp = dot_rows(v_ref[here, span], dparts[head])
                    p_ref[number, tile] = p
                    dp_ref[number, tile] = dp
                    part = fold_rows(p * dp, jnp.add)
                    delta = part if delta is None else delta + part
                deltas.append(jnp.sum(delta, axis=0, keepdims=True))
            dquery = [None, None]
            for tile in range(count):
                here = pl.ds(starts[tile], kb)
                weights, lows = [], []
                for head in range(2):
                    number = 2 * pair + head
                    p = p_ref[number, tile]
                    ds = p * (dp_ref[number, tile] - deltas[head])
                    if spec["bias"]:
                        rows, lanes = kb // TILE, qb // TILE
                        for row in range(rows):
                            for lane in range(lanes):
                                index = band_index(
                                    block * lanes + lane, (first + tile) * rows + row
                                )
                                dtiles_ref[number, index] += ds[
                                    row * TILE : (row + 1) * TILE,
                                    lane * TILE : (lane + 1) * TILE,
                                ]
                    low = ds.astype(jnp.bfloat16)
                    weights.append(p.astype(jnp.bfloat16))
                    lows.append(low)
                    rows = slice(number * HD, (number + 1) * HD)
                    part = dot_plain(kt_ref[rows, here], low)
                    dquery[head] = part if tile == 0 else dquery[head] + part
                dv_ref[here, span] += dot_plain(jnp.concatenate(weights, axis=1), dstacked)
                dk_ref[here, span] += dot_plain(jnp.concatenate(lows, axis=1), stacked)
            dq_ref[:, span] = flip(jnp.concatenate(dquery, axis=0)).astype(jnp.bfloat16)

    for_counts(spec, bounds_ref[0, block], bounds_ref[1, block], run)

    @pl.when(block == pl.num_programs(1) - 1)
    def _():
        width = pairs * 2 * HD
        column = pl.multiple_of(group * width, width)
        dkv_ref[:, pl.ds(column, width)] = dk_ref[...].astype(jnp.bfloat16)
        column = pl.multiple_of((pl.num_programs(0) + group) * width, width)
        dkv_ref[:, pl.ds(column, width)] = dv_ref[...].astype(jnp.bfloat16)
        if spec["bias"]:
            gather_diagonals(dtiles_ref, band_ref)


def attention_setup(queries, keyval, query_labels, key_labels, bias, causal, pairs):
    rows, keys = queries.shape[0], keyval.shape[0]
    qb, kb = min(256, rows), min(256, keys)
    skip = rows > qb
    kb = TILE if skip else kb
    pairs = pairs if skip else 2
    spec = dict(
        qb=qb,
        kb=kb,
        causal=causal,
        bias=bias is not None,
        pairs=pairs,
        tiles=keys // kb,
        skip=skip,
    )
    bounds = jnp.zeros((2, 1), jnp.int32)
    if skip:
        bounds = key_bounds(query_labels, key_labels, qb, kb)
    segq = query_labels[None, :]
    segk = jnp.broadcast_to(key_labels[:, None], (keys, TILE))
    groups = H // 2 // pairs
    width = 2 * HD * pairs
    specs = dict(
        q=pl.BlockSpec((qb, width), lambda group, block, bounds: (block, group)),
        k=pl.BlockSpec((keys, width), lambda group, block, bounds: (0, group)),
        v=pl.BlockSpec((keys, width), lambda group, block, bounds: (0, groups + group)),
        segq=pl.BlockSpec((1, qb), lambda group, block, bounds: (0, block)),
        segk=pl.BlockSpec((keys, TILE), lambda group, block, bounds: (0, 0)),
        lse=pl.BlockSpec((pairs, 2, qb), lambda group, block, bounds: (group, 0, block)),
        bias=pl.BlockSpec((2 * pairs, BAND, SPAN), lambda group, block, bounds: (group, 0, 0)),
        band=pl.BlockSpec(
            (2 * pairs, BAND, FOLD, SPAN), lambda group, block, bounds: (group, 0, 0, 0)
        ),
        whole=pl.BlockSpec((keys, 2 * H * HD), lambda group, block, bounds: (0, 0)),
    )
    scores = pltpu.VMEM((2 * pairs, keys // kb, kb, qb), jnp.float32)
    return spec, bounds, segq, segk, specs, (groups, rows // qb), scores


def attend_forward(queries, keyval, query_labels, key_labels, bias, causal):
    spec, bounds, segq, segk, specs, grid, scores = attention_setup(
        queries, keyval, query_labels, key_labels, bias, causal, 2
    )
    rows, keys = queries.shape[0], keyval.shape[0]
    work = H * rows * keys
    extra = ([specs["bias"]], [bias]) if bias is not None else ([], [])
    tiles = [pltpu.VMEM((2 * spec["pairs"], BAND, TILE, TILE), jnp.float32)] * len(extra[0])
    return pl.pallas_call(
        functools.partial(forward_kernel, spec),
        out_shape=(
            jax.ShapeDtypeStruct((rows, H * HD), jnp.bfloat16),
            jax.ShapeDtypeStruct((H // 2, 2, rows), jnp.float32),
        ),
        grid_spec=pltpu.PrefetchScalarGridSpec(
            num_scalar_prefetch=1,
            grid=grid,
            in_specs=[specs["q"], specs["k"], specs["v"], specs["segq"], specs["segk"]]
            + extra[0],
            out_specs=[specs["q"], specs["lse"]],
            scratch_shapes=[
                scores,
                pltpu.VMEM((2 * HD * spec["pairs"], keys), jnp.bfloat16),
            ]
            + tiles,
        ),
        compiler_params=pltpu.CompilerParams(vmem_limit_bytes=40 << 20),
        cost_estimate=pl.CostEstimate(
            flops=16 * HD * work, transcendentals=work, bytes_accessed=8 << 20
        ),
    )(bounds, queries, keyval, keyval, segq, segk, *extra[1])


def attend_backward(queries, keyval, query_labels, key_labels, bias, causal, lse, dmixture):
    spec, bounds, segq, segk, specs, grid, scores = attention_setup(
        queries, keyval, query_labels, key_labels, bias, causal, 1
    )
    rows, keys = queries.shape[0], keyval.shape[0]
    work = H * rows * keys
    extra = ([specs["bias"]], [bias]) if bias is not None else ([], [])
    tiles = [pltpu.VMEM((2 * spec["pairs"], BAND, TILE, TILE), jnp.float32)] * len(extra[0])
    band = (
        [jax.ShapeDtypeStruct((H, BAND, FOLD, SPAN), jnp.float32)] if bias is not None else []
    )
    out = pl.pallas_call(
        functools.partial(backward_kernel, spec),
        out_shape=[
            jax.ShapeDtypeStruct((rows, H * HD), jnp.bfloat16),
            jax.ShapeDtypeStruct((keys, 2 * H * HD), jnp.bfloat16),
        ]
        + band,
        grid_spec=pltpu.PrefetchScalarGridSpec(
            num_scalar_prefetch=1,
            grid=grid,
            in_specs=[
                specs["q"],
                specs["k"],
                specs["v"],
                specs["q"],
                specs["lse"],
                specs["segq"],
                specs["segk"],
            ]
            + extra[0],
            out_specs=[specs["q"], specs["whole"]] + [specs["band"]] * len(band),
            scratch_shapes=[
                scores,
                scores,
                pltpu.VMEM((keys, 2 * HD * spec["pairs"]), jnp.float32),
                pltpu.VMEM((keys, 2 * HD * spec["pairs"]), jnp.float32),
                pltpu.VMEM((2 * HD * spec["pairs"], keys), jnp.bfloat16),
            ]
            + tiles
            + tiles,
        ),
        compiler_params=pltpu.CompilerParams(vmem_limit_bytes=48 << 20),
        cost_estimate=pl.CostEstimate(
            flops=40 * HD * work, transcendentals=work, bytes_accessed=16 << 20
        ),
    )(bounds, queries, keyval, keyval, dmixture, lse, segq, segk, *extra[1])
    return (out[0], out[1], out[2] if bias is not None else None)


def product(former, latter):
    return jnp.dot(former, latter, preferred_element_type=jnp.float32)


def transpose_product(former, latter):
    return lax.dot_general(
        former, latter, (((0,), (0,)), ((), ())), preferred_element_type=jnp.float32
    )


def product_transposed(former, latter):
    return lax.dot_general(
        former, latter, (((1,), (1,)), ((), ())), preferred_element_type=jnp.float32
    )


def smooth_gate(value):
    return jax.nn.gelu(value, approximate=True)


def norm_forward(stream, norm_gain):
    return (
        stream * lax.rsqrt(jnp.mean(stream * stream, axis=-1, keepdims=True) + EPSILON) * norm_gain
    )


def norm_backward(stream, norm_gain, gradient):
    outcome, pullback = jax.vjp(norm_forward, stream, norm_gain)
    return pullback(gradient)


def attention_forward(stream, norm_gain, wquery, wkeyval, wproj, layout, memory):
    normed = norm_forward(stream, norm_gain).astype(jnp.bfloat16)
    queries = product(normed, wquery).astype(jnp.bfloat16)
    source = normed if memory is None else memory
    keyval = product(source, wkeyval).astype(jnp.bfloat16)
    mixture, logsum = attend_forward(queries, keyval, *layout)
    return (stream + product(mixture, wproj), (normed, queries, keyval, mixture, logsum))


def attention_backward(
    grads, names, stream, norm_gain, wquery, wkeyval, wproj, layout, memory, stored, gradient
):
    normed, queries, keyval, mixture, logsum = stored
    gradient_low = gradient.astype(jnp.bfloat16)
    grads.add(names[2], mixture, gradient_low)
    dmixture = product_transposed(gradient_low, wproj).astype(jnp.bfloat16)
    dquery_low, dkeyval_low, band = attend_backward(queries, keyval, *layout, logsum, dmixture)
    source = normed if memory is None else memory
    grads.add(names[0], normed, dquery_low)
    grads.add(names[1], source, dkeyval_low)
    dnormed = product_transposed(dquery_low, wquery)
    dsource = product_transposed(dkeyval_low, wkeyval)
    if memory is None:
        dnormed = dnormed + dsource
        dsource = None
    dstream, dgain = norm_backward(stream, norm_gain, dnormed)
    return (gradient + dstream, dgain, band, dsource)


def feed_forward(stream, norm_gain, winner, wouter):
    normed = norm_forward(stream, norm_gain).astype(jnp.bfloat16)
    before = product(normed, winner)
    hidden = smooth_gate(before).astype(jnp.bfloat16)
    return (stream + product(hidden, wouter), (normed, before, hidden))


def feed_backward(grads, names, stream, norm_gain, winner, wouter, stored, gradient):
    normed, before, hidden = stored
    gradient_low = gradient.astype(jnp.bfloat16)
    grads.add(names[1], hidden, gradient_low)
    dhidden = product_transposed(gradient_low, wouter)
    gate_value, gate_pullback = jax.vjp(smooth_gate, before)
    dbefore = gate_pullback(dhidden)[0].astype(jnp.bfloat16)
    grads.add(names[0], normed, dbefore)
    dnormed = product_transposed(dbefore, winner)
    dstream, dgain = norm_backward(stream, norm_gain, dnormed)
    return (gradient + dstream, dgain)


def index_bits(devices):
    return devices.bit_length() - 1


class Links:
    def __init__(self, mesh):
        self.sizes = dict(mesh.shape)
        self.bits = [("fsdp", bit) for bit in range(index_bits(self.sizes["fsdp"]))]
        self.bits += [("dp", bit) for bit in range(index_bits(self.sizes["dp"]))]

    def side(self, axis, bit):
        return lax.rem(lax.axis_index(axis) // (1 << bit), 2)

    def partner(self, axis, bit):
        return {axis: lax.axis_index(axis) + (1 - 2 * self.side(axis, bit)) * (1 << bit)}

    def orders(self):
        core, row = ("dp", 0), ("fsdp", 0)
        rest = [key for key in self.bits if key not in (core, row)]
        third = [core] + rest[1:2] + rest[:1] + [row] + rest[2:]
        return ([core] + rest[:1] + [row] + rest[1:], [core, row] + rest, third)

    def swap(self, value, axis, bit):
        pairs = [(place, place ^ (1 << bit)) for place in range(self.sizes[axis])]
        return lax.ppermute(value, axis, pairs)

    def total(self, value):
        for key in self.bits:
            value = value + self.swap(value, *key)
        return value

    def gather_small(self, shard):
        other = self.swap(shard, "fsdp", 0)
        first = lax.axis_index("fsdp") == 0
        return jnp.concatenate(
            [jnp.where(first, shard, other), jnp.where(first, other, shard)], axis=0
        )

    def devices(self):
        return self.sizes["dp"] * self.sizes["fsdp"]

    def place(self):
        return lax.axis_index("dp") * self.sizes["fsdp"] + lax.axis_index("fsdp")


def pick(ref, lead, spot, count, side):
    return ref.at[(lead,) + (slice(None),) * spot + (side,) + (slice(None),) * (count - spot - 1)]


def fold_product(x, dy, devices):
    total = lax.dot_general(x, dy, (((0,), (0,)), ((), ())), preferred_element_type=jnp.float32)
    rows, columns = total.shape
    total = total.reshape(devices, rows // devices, columns)
    half = columns // 2
    total = jnp.concatenate([total[:, :, :half], total[:, :, half:]], axis=1)
    return total.astype(jnp.bfloat16)


def reduce_kernel(links, plan, count, *refs):
    stages, chunks = len(links.bits), len(plan)
    sources, (out_ref, ring_ref, x_ref, y_ref) = refs[:count], refs[count : count + 4]
    rest = refs[count + 4 :]
    sums, (send_sem, recv_sem, load_sem) = rest[:stages], rest[stages:]
    halvings = []
    for order in links.orders():
        left = list(reversed(links.bits))
        halving = []
        for key in order:
            halving.append((key, left.index(key), len(left)))
            left.remove(key)
        halvings.append(halving)
    kinds = len(halvings)

    barrier = pltpu.get_barrier_semaphore()
    for key in links.bits:
        pl.semaphore_signal(
            barrier,
            inc=1,
            device_id=links.partner(*key),
            device_id_type=pl.DeviceIdType.MESH,
        )
    pl.semaphore_wait(barrier, stages)

    def source(stage, chunk, kind, away):
        key, spot, width = halvings[kind][stage]
        side = links.side(*key)
        ref, lead = (ring_ref, lax.rem(chunk, HOLD)) if stage == 0 else (sums[stage - 1], chunk)
        return pick(ref, lead, spot, width, 1 - side if away else side)

    def send(stage, chunk, kind):
        key, _, _ = halvings[kind][stage]
        return pltpu.make_async_remote_copy(
            src_ref=source(stage, chunk, kind, True),
            dst_ref=sums[stage].at[chunk],
            send_sem=send_sem.at[stage, chunk],
            recv_sem=recv_sem.at[stage, chunk],
            device_id=links.partner(*key),
            device_id_type=pl.DeviceIdType.MESH,
        )

    def loads(chunk):
        item = plan[chunk]
        if item[0] == "chunk":
            _, which, index = item
            return [
                pltpu.make_async_copy(
                    sources[which].at[index], ring_ref.at[chunk % HOLD], load_sem.at[chunk % 2, 0]
                )
            ]
        _, rows, *operands = item
        slot = chunk % 2
        result = []
        for place, (which, column) in enumerate(operands):
            buffer = (x_ref, y_ref)[place]
            width = buffer.shape[2]
            result.append(
                pltpu.make_async_copy(
                    sources[which].at[:, column * width : (column + 1) * width],
                    buffer.at[slot, :rows],
                    load_sem.at[slot, place],
                )
            )
        return result

    sizes = sorted({item[1] for item in plan if item[0] == "product"})

    def step(group, carry):
        for turn in range(kinds):
            now = group * kinds + turn

            for stage in range(stages):
                chunk = now - DELAY * (stage + 1)
                kind = (turn - DELAY * (stage + 1)) % kinds

                @pl.when((chunk >= 0) & (chunk < chunks))
                def _():
                    send(stage, chunk, kind).wait()
                    mine = source(stage, chunk, kind, False)[...]
                    if stage < stages - 1:
                        sums[stage][chunk] = sums[stage][chunk] + mine
                        send(stage + 1, chunk, kind).start()
                    else:
                        out_ref[chunk] = sums[stage][chunk].astype(jnp.float32) + mine.astype(
                            jnp.float32
                        )

            for chunk in range(turn, chunks, kinds):

                @pl.when(now == chunk)
                def _():
                    for load in loads(chunk):
                        load.wait()

            for rows in sizes:
                spots = [spot for spot, item in enumerate(plan) if item[:2] == ("product", rows)]

                @pl.when((now >= spots[0]) & (now <= spots[-1]))
                def _():
                    slot = lax.rem(now, 2)
                    made = fold_product(x_ref[slot, :rows], y_ref[slot, :rows], links.devices())
                    ring_ref[lax.rem(now, HOLD)] = made.reshape(ring_ref.shape[1:])

            @pl.when(now < chunks)
            def _():
                send(0, now, turn).start()

            for chunk in range((turn + 1) % kinds, chunks, kinds):

                @pl.when(now + 1 == chunk)
                def _():
                    for load in loads(chunk):
                        load.start()

        return carry

    for load in loads(0):
        load.start()
    slots = chunks + DELAY * stages
    lax.fori_loop(0, (slots + kinds - 1) // kinds, step, 0)


def reduce_chunks(links, plan, sources, shape, width, collective_id):
    stages, chunks = len(links.bits), len(plan)
    sums = [
        pltpu.VMEM((chunks,) + (2,) * (stages - 1 - stage) + shape, jnp.bfloat16)
        for stage in range(stages)
    ]
    rows = max([item[1] for item in plan if item[0] == "product"] + [16])
    return pl.pallas_call(
        functools.partial(reduce_kernel, links, plan, len(sources)),
        out_shape=jax.ShapeDtypeStruct((chunks,) + shape, jnp.float32),
        in_specs=[pl.BlockSpec(memory_space=pltpu.HBM)] * len(sources),
        out_specs=pl.BlockSpec(memory_space=pltpu.VMEM),
        scratch_shapes=[
            pltpu.VMEM((HOLD,) + (2,) * stages + shape, jnp.bfloat16),
            pltpu.VMEM((2, rows, width), jnp.bfloat16),
            pltpu.VMEM((2, rows, width), jnp.bfloat16),
        ]
        + sums
        + [
            pltpu.SemaphoreType.DMA((stages, chunks)),
            pltpu.SemaphoreType.DMA((stages, chunks)),
            pltpu.SemaphoreType.DMA((2, 2)),
        ],
        compiler_params=pltpu.CompilerParams(
            collective_id=collective_id, has_side_effects=True, vmem_limit_bytes=60 << 20
        ),
    )(*sources)


def fold_grad(grad, devices, width):
    rows, columns = grad.shape
    deep, wide = rows // width, columns // width
    r = rows // devices // deep
    grad = grad.astype(jnp.bfloat16).reshape(devices, deep, r, wide, 2, width // 2)
    return grad.transpose(1, 3, 0, 4, 2, 5).reshape(deep * wide, devices, 2 * r, width // 2)


def unfold_share(chunks, rows, columns):
    count, folded, half = chunks.shape
    deep, wide = rows * 2 // folded, columns // (2 * half)
    chunks = chunks.reshape(deep, wide, 2, folded // 2, half)
    return chunks.transpose(0, 3, 1, 2, 4).reshape(rows, columns)


def gather_kernel(links, units, count, *refs):
    shards, wholes, held = refs[:count], refs[count : 2 * count], refs[2 * count : 3 * count]
    send_sem, recv_sem, local_sem = refs[3 * count :]
    core, mesh_id = ("dp", 0), pl.DeviceIdType.MESH
    keys = [("dp", 1), ("dp", 2), core]
    orders = [[keys[0], keys[1], core], [keys[1], keys[0], core]]
    row = ("fsdp", 0)
    place = lax.axis_index("fsdp")

    barrier = pltpu.get_barrier_semaphore()
    for key in [row] + keys:
        pl.semaphore_signal(
            barrier, inc=1, device_id=links.partner(*key), device_id_type=mesh_id
        )
    pl.semaphore_wait(barrier, 1 + len(keys))

    def piece(known):
        return tuple(slice(None) if key in known else links.side(*key) for key in keys)

    def send(stage, unit):
        order = orders[unit % 2]
        number, rows, columns = units[unit]
        if stage == 0:
            key, where = row, piece([])
            src = shards[number].at[where + (rows, columns)]
        else:
            key, where = order[stage - 1], piece(order[: stage - 1])
            src = wholes[number].at[(1 - place,) + where + (rows, columns)]
        dst = wholes[number].at[
            (place if stage == 0 else 1 - place,) + where + (rows, columns)
        ]
        return pltpu.make_async_remote_copy(
            src_ref=src,
            dst_ref=dst,
            send_sem=send_sem.at[stage, unit],
            recv_sem=recv_sem.at[stage, unit],
            device_id=links.partner(*key),
            device_id_type=mesh_id,
        )

    def load(number):
        return pltpu.make_async_copy(shards[number], held[number], local_sem.at[0, number])

    def keep(number):
        return pltpu.make_async_copy(
            held[number], wholes[number].at[place], local_sem.at[1, number]
        )

    stages = 1 + len(keys)
    for unit in range(len(units)):
        send(0, unit).start()
    for number in range(count):
        load(number).start()
    for slot in range(len(units) + LAG * (stages - 1)):
        for stage in range(stages):
            unit = slot - LAG * stage
            if 0 <= unit < len(units):
                send(stage, unit).wait()
                if stage + 1 < stages:
                    send(stage + 1, unit).start()
        if slot < count:
            load(slot).wait()
            keep(slot).start()
    for number in range(count):
        keep(number).wait()


def gather_units(shards, width):
    least = min(shard.shape[0] for shard in shards)
    units = []
    for number, shard in enumerate(shards):
        deep, wide = shard.shape[0] // least, shard.shape[1] // width
        rows = shard.shape[0] // 8 // deep
        for part in range(deep):
            for column in range(wide):
                units.append(
                    (
                        number,
                        slice(part * rows, (part + 1) * rows),
                        slice(column * width, (column + 1) * width),
                    )
                )
    return units


def gather_weights(links, shards, collective_id):
    count = len(shards)
    units = gather_units(shards, shards[0].shape[1])
    split = [
        shard.reshape(2, 2, 2, shard.shape[0] // 8, shard.shape[1]) for shard in shards
    ]
    wholes = pl.pallas_call(
        functools.partial(gather_kernel, links, units, count),
        out_shape=[jax.ShapeDtypeStruct((2,) + piece.shape, piece.dtype) for piece in split],
        in_specs=[pl.BlockSpec(memory_space=pltpu.HBM)] * count,
        out_specs=[pl.BlockSpec(memory_space=pltpu.HBM)] * count,
        scratch_shapes=[pltpu.VMEM(piece.shape, piece.dtype) for piece in split]
        + [
            pltpu.SemaphoreType.DMA((4, len(units))),
            pltpu.SemaphoreType.DMA((4, len(units))),
            pltpu.SemaphoreType.DMA((2, count)),
        ],
        compiler_params=pltpu.CompilerParams(
            collective_id=collective_id, has_side_effects=True, vmem_limit_bytes=60 << 20
        ),
    )(*split)
    return [
        whole.reshape(2 * shard.shape[0], shard.shape[1]) for whole, shard in zip(wholes, shards)
    ]


def weight_kernel(deep, x_ref, dy_ref, *rest):
    out_ref = rest[-1]
    total = lax.dot_general(
        x_ref[...], dy_ref[...], (((0,), (0,)), ((), ())), preferred_element_type=jnp.float32
    )
    half = total.shape[1] // 2
    rows = out_ref.shape[2] // 2
    total = total.reshape(out_ref.shape[1], deep, rows, 2 * half)
    for part in range(deep):
        piece = total[:, part]
        piece = jnp.concatenate([piece[:, :, :half], piece[:, :, half:]], axis=1)
        out_ref[part] = piece.astype(jnp.bfloat16)


def weight_chunks(x, dy, chunks, start, count, devices, width):
    rows, deep, wide = x.shape[0], x.shape[1] // width, dy.shape[1] // width
    r = width // devices
    if deep == 1:
        specs = [
            pl.BlockSpec((rows, width), lambda w: (0, 0)),
            pl.BlockSpec((rows, width), lambda w: (0, w)),
        ]
        out_spec = pl.BlockSpec((1, devices, 2 * r, width // 2), lambda w: (start + w, 0, 0, 0))
    else:
        specs = [
            pl.BlockSpec((rows, width), lambda w: (0, w)),
            pl.BlockSpec((rows, width), lambda w: (0, 0)),
        ]
        out_spec = pl.BlockSpec(
            (deep, devices // deep, 2 * r, width // 2), lambda w: (start // deep, w, 0, 0)
        )
    extra = [] if chunks is None else [chunks]
    return pl.pallas_call(
        functools.partial(weight_kernel, deep),
        out_shape=jax.ShapeDtypeStruct((count, devices, 2 * r, width // 2), jnp.bfloat16),
        grid=(max(deep, wide),),
        in_specs=specs + [pl.BlockSpec(memory_space=pltpu.HBM)] * len(extra),
        out_specs=out_spec,
        input_output_aliases={2: 0} if extra else {},
        compiler_params=pltpu.CompilerParams(vmem_limit_bytes=40 << 20),
        cost_estimate=pl.CostEstimate(
            flops=2 * rows * x.shape[1] * dy.shape[1],
            transcendentals=0,
            bytes_accessed=2 * (x.size + dy.size + x.shape[1] * dy.shape[1]),
        ),
    )(x, dy, *extra)


class Gradients:
    def __init__(self, links, width):
        self.links, self.width = links, width
        self.products, self.scattered = {}, {}

    def add(self, name, x, dy):
        if name in OFFLOADED:
            grad = transpose_product(x, dy).astype(jnp.bfloat16)
            self.scattered[name] = lax.psum_scatter(
                grad, ("dp", "fsdp"), scatter_dimension=0, tiled=True
            )
        else:
            self.products[name] = (x, dy)

    def shares(self, collective_id, before):
        width, devices = self.width, self.links.devices()
        r = width // devices
        aligned = r % 8 == 0
        names = list(self.products)
        size = {name: self.products[name][0].shape for name in names}
        deep = {name: size[name][1] // width for name in names}
        names.sort(key=lambda name: (deep[name] == 1, size[name][0]))
        plan, sources, known = [], [], {}

        def number(array):
            if id(array) not in known:
                known[id(array)] = len(sources)
                sources.append(array)
            return known[id(array)]

        shapes = {}
        for name in names:
            x, dy = self.products[name]
            shapes[name] = (x.shape[1] // devices, dy.shape[1])
            wide = dy.shape[1] // width
            if aligned and deep[name] == 1:
                for part in range(wide):
                    plan.append(("product", x.shape[0], (number(x), 0), (number(dy), part)))
                continue
            count = deep[name] * wide
            if aligned:
                made = weight_chunks(x, dy, None, 0, count, devices, width)
            else:
                made = fold_grad(transpose_product(x, dy), devices, width)
            made = made.reshape((count,) + (2,) * len(self.links.bits) + made.shape[2:])
            for part in range(count):
                plan.append(("chunk", number(made), part))
        before, sources[0] = lax.optimization_barrier((before, sources[0]))
        shares = reduce_chunks(
            self.links, plan, sources, (2 * r, width // 2), width, collective_id
        )
        if aligned:
            scattered = list(self.scattered.values())
            result = pl.pallas_call(
                functools.partial(unfold_kernel, width, len(scattered)),
                out_shape=[jax.ShapeDtypeStruct(shape, jnp.float32) for shape in shapes.values()]
                + [jax.ShapeDtypeStruct(share.shape, jnp.float32) for share in scattered],
            )(shares, *scattered)
            return dict(zip(list(shapes) + list(self.scattered), result)), before
        result = {name: share.astype(jnp.float32) for name, share in self.scattered.items()}
        start = 0
        for name, shape in shapes.items():
            count = deep[name] * shape[1] // width
            result[name] = unfold_share(shares[start : start + count], *shape)
            start += count
        return result, before


def unfold_kernel(width, count, shares_ref, *refs):
    scattered, out_refs = refs[:count], refs[count:]
    if count:
        for scattered_ref, out_ref in zip(scattered, out_refs[-count:]):
            out_ref[...] = scattered_ref[...].astype(jnp.float32)
        out_refs = out_refs[:-count]
    chunk, r, half = 0, shares_ref.shape[1] // 2, width // 2
    for out_ref in out_refs:
        for row in range(0, out_ref.shape[0], r):
            for column in range(0, out_ref.shape[1], width):
                for part in range(2):
                    out_ref[
                        row : row + r, column + part * half : column + (part + 1) * half
                    ] = shares_ref[chunk, part * r : (part + 1) * r, :]
                chunk += 1


def body(
    links,
    enc_tokens,
    dec_tokens,
    enc_segments,
    dec_segments,
    enc_upstream,
    dec_upstream,
    encoder_query,
    encoder_keyval,
    encoder_proj,
    encoder_inner,
    encoder_outer,
    encoder_gains,
    encoder_table,
    decoder_query,
    decoder_keyval,
    decoder_proj,
    cross_query,
    cross_keyval,
    cross_proj,
    decoder_inner,
    decoder_outer,
    decoder_gains,
    decoder_table,
):
    small = jnp.concatenate(
        [encoder_gains, decoder_gains]
        + [
            jnp.concatenate([encoder_table, decoder_table], axis=0).reshape(
                encoder_gains.shape[0], -1
            )
        ],
        axis=1,
    )
    small = links.gather_small(small)
    enc_gains = small[:, 0:2].astype(jnp.float32)
    dec_gains = small[:, 2:5].astype(jnp.float32)
    tables = small[:, 5:].reshape(2, 2, NB // 2, H)
    enc_bias = band_bias(tables[:, 0].reshape(NB, H), encoder_bucket)
    dec_bias = band_bias(tables[:, 1].reshape(NB, H), decoder_bucket)

    shards = [
        encoder_query,
        encoder_keyval,
        encoder_proj,
        encoder_inner,
        encoder_outer,
        decoder_query,
        decoder_keyval,
        decoder_proj,
        cross_query,
        cross_keyval,
        cross_proj,
        decoder_inner,
        decoder_outer,
    ]
    shards = dict(zip(NAMES, shards))
    later = [shards.pop(name) for name in LATER]
    weights = dict(zip(shards, gather_weights(links, list(shards.values()), 1)))
    weights["equery"], *later = lax.optimization_barrier((weights["equery"], *later))
    for name, shard in zip(LATER, later):
        weights[name] = lax.all_gather(shard, "fsdp", axis=0, tiled=True)
    grads = Gradients(links, encoder_query.shape[1])

    enc_layout = (enc_segments, enc_segments, enc_bias, False)
    dec_layout = (dec_segments, dec_segments, dec_bias, True)
    cross_layout = (dec_segments, enc_segments, None, False)

    enc_stream = enc_tokens.astype(jnp.float32)
    enc_middle, enc_self = attention_forward(
        enc_stream, enc_gains[:, 0], weights["equery"], weights["ekeyval"], weights["eproj"], enc_layout, None
    )
    enc_final, enc_ffn = feed_forward(enc_middle, enc_gains[:, 1], weights["einner"], weights["eouter"])
    memory = enc_final.astype(jnp.bfloat16)

    dec_stream = dec_tokens.astype(jnp.float32)
    after_self, dec_self = attention_forward(
        dec_stream, dec_gains[:, 0], weights["dquery"], weights["dkeyval"], weights["dproj"], dec_layout, None
    )
    after_cross, dec_cross = attention_forward(
        after_self, dec_gains[:, 1], weights["cquery"], weights["ckeyval"], weights["cproj"], cross_layout, memory
    )
    dec_final, dec_ffn = feed_forward(after_cross, dec_gains[:, 2], weights["dinner"], weights["douter"])


    dec_live = (dec_segments >= 0).astype(jnp.float32)[:, None]
    gradient = dec_upstream.astype(jnp.float32) * dec_live
    gradient, dgain_ffn = feed_backward(
        grads, ("dinner", "douter"), after_cross, dec_gains[:, 2], weights["dinner"], weights["douter"], dec_ffn, gradient
    )
    gradient, dgain_cross, _, memory_grad = (
        attention_backward(
            grads,
            ("cquery", "ckeyval", "cproj"),
            after_self,
            dec_gains[:, 1],
            weights["cquery"],
            weights["ckeyval"],
            weights["cproj"],
            cross_layout,
            memory,
            dec_cross,
            gradient,
        )
    )
    dec_gradient, dgain_self, dec_band, _ = (
        attention_backward(
            grads,
            ("dquery", "dkeyval", "dproj"),
            dec_stream,
            dec_gains[:, 0],
            weights["dquery"],
            weights["dkeyval"],
            weights["dproj"],
            dec_layout,
            None,
            dec_self,
            gradient,
        )
    )

    enc_live = (enc_segments >= 0).astype(jnp.float32)[:, None]
    gradient = enc_upstream.astype(jnp.float32) * enc_live + memory_grad
    gradient, egain_ffn = feed_backward(
        grads, ("einner", "eouter"), enc_middle, enc_gains[:, 1], weights["einner"], weights["eouter"], enc_ffn, gradient
    )
    enc_gradient, egain_self, enc_band, _ = (
        attention_backward(
            grads,
            ("equery", "ekeyval", "eproj"),
            enc_stream,
            enc_gains[:, 0],
            weights["equery"],
            weights["ekeyval"],
            weights["eproj"],
            enc_layout,
            None,
            enc_self,
            gradient,
        )
    )

    table_grads = [
        band_table_grad(enc_band, encoder_bucket),
        band_table_grad(dec_band, decoder_bucket),
    ]
    gain_grads = jnp.stack([egain_self, egain_ffn, dgain_self, dgain_cross, dgain_ffn])
    flat = jnp.concatenate([gain_grads.reshape(-1)] + [grad.reshape(-1) for grad in table_grads])
    flat = links.total(flat.reshape(-1, TILE)).reshape(-1)
    width = gain_grads.shape[1]
    shares, flat = grads.shares(0, flat)
    tables_grad = flat[5 * width :].reshape(2, NB, H)
    own = width // links.devices()
    gains_share = lax.dynamic_slice_in_dim(
        flat[: 5 * width].reshape(5, width), links.place() * own, own, 1
    ).T
    return (
        memory,
        dec_final.astype(jnp.bfloat16),
        enc_gradient,
        dec_gradient,
        shares["equery"],
        shares["ekeyval"],
        shares["eproj"],
        shares["einner"],
        shares["eouter"],
        gains_share[:, 0:2],
        tables_grad[0],
        shares["dquery"],
        shares["dkeyval"],
        shares["dproj"],
        shares["cquery"],
        shares["ckeyval"],
        shares["cproj"],
        shares["dinner"],
        shares["douter"],
        gains_share[:, 2:5],
        tables_grad[1],
    )


def solution(mesh):
    in_specs = (
        P(("dp", "fsdp"), None),
        P(("dp", "fsdp"), None),
        P(("dp", "fsdp")),
        P(("dp", "fsdp")),
        P(("dp", "fsdp"), None),
        P(("dp", "fsdp"), None),
        P("fsdp", None),
        P("fsdp", None),
        P("fsdp", None),
        P("fsdp", None),
        P("fsdp", None),
        P("fsdp", None),
        P("fsdp", None),
        P("fsdp", None),
        P("fsdp", None),
        P("fsdp", None),
        P("fsdp", None),
        P("fsdp", None),
        P("fsdp", None),
        P("fsdp", None),
        P("fsdp", None),
        P("fsdp", None),
        P("fsdp", None),
    )
    out_specs = (
        P(("dp", "fsdp"), None),
        P(("dp", "fsdp"), None),
        P(("dp", "fsdp"), None),
        P(("dp", "fsdp"), None),
        P(("dp", "fsdp"), None),
        P(("dp", "fsdp"), None),
        P(("dp", "fsdp"), None),
        P(("dp", "fsdp"), None),
        P(("dp", "fsdp"), None),
        P(("dp", "fsdp"), None),
        P(),
        P(("dp", "fsdp"), None),
        P(("dp", "fsdp"), None),
        P(("dp", "fsdp"), None),
        P(("dp", "fsdp"), None),
        P(("dp", "fsdp"), None),
        P(("dp", "fsdp"), None),
        P(("dp", "fsdp"), None),
        P(("dp", "fsdp"), None),
        P(("dp", "fsdp"), None),
        P(),
    )
    return jax.shard_map(
        functools.partial(body, Links(mesh)), mesh=mesh, in_specs=in_specs, out_specs=out_specs, check_vma=False)
```

```python
import functools
import math

import jax
import jax.numpy as jnp
import numpy as np
from jax import lax
from jax.experimental import pallas as pl
from jax.experimental.pallas import tpu as pltpu
from jax.sharding import PartitionSpec as P

H = 12
HD = 64
NB = 32
TILE = 128
BAND = 5
EPSILON = 1e-06
MASKED = -1e30
ENC_EDGES = (12, 16, 23, 32, 46, 64, 91)
DEC_EDGES = tuple((math.ceil(16 * 2 ** (3 * power / 16)) for power in range(1, 16)))
PADDING_LABEL = 1 << 20
SPAN = 2 * TILE
FOLD = 8
LAG = 3
DELAY = 2
HOLD = DELAY + 1
OFFLOADED = ("douter",)
LATER = ("dinner",)
NAMES = (
    "equery",
    "ekeyval",
    "eproj",
    "einner",
    "eouter",
    "dquery",
    "dkeyval",
    "dproj",
    "cquery",
    "ckeyval",
    "cproj",
    "dinner",
    "douter",
)


def encoder_bucket(distance):
    reach = np.abs(distance)
    farther = 8 + sum((reach >= threshold).astype(np.int32) for threshold in ENC_EDGES)
    return np.where(reach < 8, reach, farther) + 16 * (distance < 0).astype(np.int32)


def decoder_bucket(distance):
    ahead = np.maximum(distance, 0)
    farther = 16 + sum((ahead >= threshold).astype(np.int32) for threshold in DEC_EDGES)
    return np.where(ahead < 16, ahead, farther)


def band_distances(rows):
    step = np.arange(BAND)[:, None, None] - 2
    row = np.arange(rows)[None, :, None]
    lane = np.arange(SPAN)[None, None, :]
    lane = np.where(lane < TILE, lane, lane - SPAN)
    return step * TILE + lane - row


def bucket_onehot(bucket_of, rows, dtype):
    bucket = jnp.asarray(bucket_of(band_distances(rows)).reshape(1, -1), jnp.int32)
    return (bucket == lax.broadcasted_iota(jnp.int32, (NB, 1), 0)).astype(dtype)


def band_bias(table, bucket_of):
    onehot = bucket_onehot(bucket_of, 1, jnp.bfloat16)
    flat = lax.dot_general(
        table, onehot, (((0,), (0,)), ((), ())), preferred_element_type=jnp.float32
    )
    return flat.reshape(H, BAND, SPAN)


def band_table_grad(band, bucket_of):
    return lax.dot_general(
        bucket_onehot(bucket_of, FOLD, jnp.float32),
        band.reshape(H, BAND * FOLD * SPAN),
        (((1,), (1,)), ((), ())),
        precision=lax.Precision.HIGHEST,
        preferred_element_type=jnp.float32,
    )


def key_bounds(query_labels, key_labels, query_rows, key_rows):
    queries = jnp.where(query_labels < 0, PADDING_LABEL, query_labels).reshape(-1, query_rows)
    keys = jnp.where(key_labels < 0, PADDING_LABEL, key_labels)
    first = jnp.sum((keys[None, :] < queries[:, :1]).astype(jnp.int32), axis=1)
    last = jnp.sum((keys[None, :] <= queries[:, -1:]).astype(jnp.int32), axis=1)
    return jnp.stack([first // key_rows, (last + key_rows - 1) // key_rows])


def fold_rows(value, combine):
    rows = value.shape[0]
    while rows > 8:
        rows //= 2
        value = combine(value[:rows], value[rows:])
    return value


def head_parts(block):
    lane = lax.broadcasted_iota(jnp.int32, block.shape, 1)
    zero = jnp.zeros_like(block)
    return (jnp.where(lane < HD, block, zero), jnp.where(lane < HD, zero, block))


def flip(value):
    return value.astype(jnp.float32).T


def band_index(query_tile, key_tile):
    return jnp.clip(query_tile - key_tile, -2, 2) + 2


def spread_bias(bias_ref, tiles_ref):
    for head in range(tiles_ref.shape[0]):
        for step in range(BAND):
            row = bias_ref[head, step : step + 1, :]
            if step in (0, BAND - 1):
                tiles_ref[head, step] = jnp.broadcast_to(row[:, :TILE], (TILE, TILE))
            else:
                wide = jnp.broadcast_to(row, (TILE, SPAN))
                wide = pltpu.roll(wide, 0, 1, stride=1, stride_axis=0)
                tiles_ref[head, step] = wide[:, :TILE]


def gather_diagonals(tiles_ref, band_ref):
    for head in range(tiles_ref.shape[0]):
        for step in range(BAND):
            tile = tiles_ref[head, step]
            tile = jnp.concatenate([tile, jnp.zeros_like(tile)], axis=1)
            rows = TILE
            while rows > FOLD:
                rows //= 2
                tile = tile[:rows] + pltpu.roll(tile[rows:], SPAN - rows, 1)
            band_ref[head, step] = tile


def tile_mask(spec, key_tile, query_block, segk_ref, segq_ref):
    rows, lanes = spec["kb"], spec["qb"]
    start = pl.multiple_of(key_tile * rows, rows) if spec["skip"] else key_tile * rows
    labels = segk_ref[pl.ds(start, rows), :]
    labels = jnp.concatenate([labels] * (lanes // TILE), axis=1)
    mask = labels == segq_ref[...]
    if spec["causal"]:
        key = lax.broadcasted_iota(jnp.int32, (rows, lanes), 0) + key_tile * rows
        query = lax.broadcasted_iota(jnp.int32, (rows, lanes), 1) + query_block * lanes
        mask = mask & (key <= query)
    return mask


def tile_bias(spec, head, key_tile, query_block, bias_ref):
    rows, lanes = spec["kb"] // TILE, spec["qb"] // TILE
    return jnp.concatenate(
        [
            jnp.concatenate(
                [
                    bias_ref[
                        head, band_index(query_block * lanes + lane, key_tile * rows + row)
                    ]
                    for lane in range(lanes)
                ],
                axis=1,
            )
            for row in range(rows)
        ],
        axis=0,
    )


def dot_rows(former, latter):
    return lax.dot_general(
        former, latter, (((1,), (1,)), ((), ())), preferred_element_type=jnp.float32
    )


def dot_plain(former, latter):
    return jnp.dot(former, latter, preferred_element_type=jnp.float32)


def for_counts(spec, first, last, run):
    if not spec["skip"]:
        run(0, spec["tiles"])
        return
    for count in range(1, spec["tiles"] + 1):
        pl.when(last - first == count)(functools.partial(run, first, count))


def forward_kernel(spec, bounds_ref, q_ref, k_ref, v_ref, segq_ref, segk_ref, *rest):
    bias_ref, rest = (rest[0], rest[1:]) if spec["bias"] else (None, rest)
    o_ref, lse_ref, score_ref, vt_ref, rest = *rest[:4], rest[4:]
    tiles_ref = rest[0] if spec["bias"] else None
    kb, qb, pairs = spec["kb"], spec["qb"], spec["pairs"]
    block = pl.program_id(1)

    @pl.when(block == 0)
    def _():
        for pair in range(pairs):
            span = slice(pair * 2 * HD, (pair + 1) * 2 * HD)
            vt_ref[span, :] = flip(v_ref[:, span]).astype(jnp.bfloat16)
        if spec["bias"]:
            spread_bias(bias_ref, tiles_ref)

    def run(first, count):
        starts = [(first + tile) * kb for tile in range(count)]
        if spec["skip"]:
            starts = [pl.multiple_of(start, kb) for start in starts]
        for pair in range(pairs):
            span = slice(pair * 2 * HD, (pair + 1) * 2 * HD)
            parts = head_parts(q_ref[:, span])
            mixed, logsum = [], []
            for head in range(2):
                number = 2 * pair + head
                top = None
                for tile in range(count):
                    s = dot_rows(k_ref[pl.ds(starts[tile], kb), span], parts[head])
                    if spec["bias"]:
                        s = s + tile_bias(spec, number, first + tile, block, tiles_ref)
                    mask = tile_mask(spec, first + tile, block, segk_ref, segq_ref)
                    s = jnp.where(mask, s, MASKED)
                    score_ref[number, tile] = s
                    peak = fold_rows(s, jnp.maximum)
                    top = peak if top is None else jnp.maximum(top, peak)
                top = jnp.max(top, axis=0, keepdims=True)
                total = None
                for tile in range(count):
                    e = jnp.exp(score_ref[number, tile] - top)
                    score_ref[number, tile] = e
                    part = fold_rows(e, jnp.add)
                    total = part if total is None else total + part
                total = jnp.sum(total, axis=0, keepdims=True)
                scale = 1.0 / total
                mix = None
                for tile in range(count):
                    weights = (score_ref[number, tile] * scale).astype(jnp.bfloat16)
                    rows = slice(number * HD, (number + 1) * HD)
                    part = dot_plain(vt_ref[rows, pl.ds(starts[tile], kb)], weights)
                    mix = part if mix is None else mix + part
                mixed.append(mix)
                logsum.append(top + jnp.log(total))
            o_ref[:, span] = flip(jnp.concatenate(mixed, axis=0)).astype(jnp.bfloat16)
            lse_ref[pair] = jnp.concatenate(logsum, axis=0)

    for_counts(spec, bounds_ref[0, block], bounds_ref[1, block], run)


def backward_kernel(
    spec, bounds_ref, q_ref, k_ref, v_ref, do_ref, lse_ref, segq_ref, segk_ref, *rest
):
    bias_ref, rest = (rest[0], rest[1:]) if spec["bias"] else (None, rest)
    dq_ref, dkv_ref, rest = rest[0], rest[1], rest[2:]
    band_ref, rest = (rest[0], rest[1:]) if spec["bias"] else (None, rest)
    p_ref, dp_ref, dk_ref, dv_ref, kt_ref, rest = *rest[:5], rest[5:]
    tiles_ref, dtiles_ref = rest if spec["bias"] else (None, None)
    kb, qb, pairs = spec["kb"], spec["qb"], spec["pairs"]
    group, block = pl.program_id(0), pl.program_id(1)

    @pl.when(block == 0)
    def _():
        for pair in range(pairs):
            span = slice(pair * 2 * HD, (pair + 1) * 2 * HD)
            kt_ref[span, :] = flip(k_ref[:, span]).astype(jnp.bfloat16)
        dk_ref[...] = jnp.zeros_like(dk_ref)
        dv_ref[...] = jnp.zeros_like(dv_ref)
        if spec["bias"]:
            spread_bias(bias_ref, tiles_ref)
            dtiles_ref[...] = jnp.zeros_like(dtiles_ref)

    def run(first, count):
        starts = [(first + tile) * kb for tile in range(count)]
        if spec["skip"]:
            starts = [pl.multiple_of(start, kb) for start in starts]
        for pair in range(pairs):
            span = slice(pair * 2 * HD, (pair + 1) * 2 * HD)
            parts = head_parts(q_ref[:, span])
            dparts = head_parts(do_ref[:, span])
            lse = lse_ref[pair]
            stacked = jnp.concatenate(parts, axis=0)
            dstacked = jnp.concatenate(dparts, axis=0)
            deltas = []
            for head in range(2):
                number = 2 * pair + head
                delta = None
                for tile in range(count):
                    here = pl.ds(starts[tile], kb)
                    s = dot_rows(k_ref[here, span], parts[head])
                    if spec["bias"]:
                        s = s + tile_bias(spec, number, first + tile, block, tiles_ref)
                    mask = tile_mask(spec, first + tile, block, segk_ref, segq_ref)
                    p = jnp.exp(jnp.where(mask, s, MASKED) - lse[head : head + 1])
                    dp = dot_rows(v_ref[here, span], dparts[head])
                    p_ref[number, tile] = p
                    dp_ref[number, tile] = dp
                    part = fold_rows(p * dp, jnp.add)
                    delta = part if delta is None else delta + part
                deltas.append(jnp.sum(delta, axis=0, keepdims=True))
            dquery = [None, None]
            for tile in range(count):
                here = pl.ds(starts[tile], kb)
                weights, lows = [], []
                for head in range(2):
                    number = 2 * pair + head
                    p = p_ref[number, tile]
                    ds = p * (dp_ref[number, tile] - deltas[head])
                    if spec["bias"]:
                        rows, lanes = kb // TILE, qb // TILE
                        for row in range(rows):
                            for lane in range(lanes):
                                index = band_index(
                                    block * lanes + lane, (first + tile) * rows + row
                                )
                                dtiles_ref[number, index] += ds[
                                    row * TILE : (row + 1) * TILE,
                                    lane * TILE : (lane + 1) * TILE,
                                ]
                    low = ds.astype(jnp.bfloat16)
                    weights.append(p.astype(jnp.bfloat16))
                    lows.append(low)
                    rows = slice(number * HD, (number + 1) * HD)
                    part = dot_plain(kt_ref[rows, here], low)
                    dquery[head] = part if tile == 0 else dquery[head] + part
                dv_ref[here, span] += dot_plain(jnp.concatenate(weights, axis=1), dstacked)
                dk_ref[here, span] += dot_plain(jnp.concatenate(lows, axis=1), stacked)
            dq_ref[:, span] = flip(jnp.concatenate(dquery, axis=0)).astype(jnp.bfloat16)

    for_counts(spec, bounds_ref[0, block], bounds_ref[1, block], run)

    @pl.when(block == pl.num_programs(1) - 1)
    def _():
        width = pairs * 2 * HD
        column = pl.multiple_of(group * width, width)
        dkv_ref[:, pl.ds(column, width)] = dk_ref[...].astype(jnp.bfloat16)
        column = pl.multiple_of((pl.num_programs(0) + group) * width, width)
        dkv_ref[:, pl.ds(column, width)] = dv_ref[...].astype(jnp.bfloat16)
        if spec["bias"]:
            gather_diagonals(dtiles_ref, band_ref)


def attention_setup(queries, keyval, query_labels, key_labels, bias, causal, pairs):
    rows, keys = queries.shape[0], keyval.shape[0]
    qb, kb = min(256, rows), min(256, keys)
    skip = rows > qb
    kb = TILE if skip else kb
    pairs = pairs if skip else 2
    spec = dict(
        qb=qb,
        kb=kb,
        causal=causal,
        bias=bias is not None,
        pairs=pairs,
        tiles=keys // kb,
        skip=skip,
    )
    bounds = jnp.zeros((2, 1), jnp.int32)
    if skip:
        bounds = key_bounds(query_labels, key_labels, qb, kb)
    segq = query_labels[None, :]
    segk = jnp.broadcast_to(key_labels[:, None], (keys, TILE))
    groups = H // 2 // pairs
    width = 2 * HD * pairs
    specs = dict(
        q=pl.BlockSpec((qb, width), lambda group, block, bounds: (block, group)),
        k=pl.BlockSpec((keys, width), lambda group, block, bounds: (0, group)),
        v=pl.BlockSpec((keys, width), lambda group, block, bounds: (0, groups + group)),
        segq=pl.BlockSpec((1, qb), lambda group, block, bounds: (0, block)),
        segk=pl.BlockSpec((keys, TILE), lambda group, block, bounds: (0, 0)),
        lse=pl.BlockSpec((pairs, 2, qb), lambda group, block, bounds: (group, 0, block)),
        bias=pl.BlockSpec((2 * pairs, BAND, SPAN), lambda group, block, bounds: (group, 0, 0)),
        band=pl.BlockSpec(
            (2 * pairs, BAND, FOLD, SPAN), lambda group, block, bounds: (group, 0, 0, 0)
        ),
        whole=pl.BlockSpec((keys, 2 * H * HD), lambda group, block, bounds: (0, 0)),
    )
    scores = pltpu.VMEM((2 * pairs, keys // kb, kb, qb), jnp.float32)
    return spec, bounds, segq, segk, specs, (groups, rows // qb), scores


def attend_forward(queries, keyval, query_labels, key_labels, bias, causal):
    spec, bounds, segq, segk, specs, grid, scores = attention_setup(
        queries, keyval, query_labels, key_labels, bias, causal, 2
    )
    rows, keys = queries.shape[0], keyval.shape[0]
    work = H * rows * keys
    extra = ([specs["bias"]], [bias]) if bias is not None else ([], [])
    tiles = [pltpu.VMEM((2 * spec["pairs"], BAND, TILE, TILE), jnp.float32)] * len(extra[0])
    return pl.pallas_call(
        functools.partial(forward_kernel, spec),
        out_shape=(
            jax.ShapeDtypeStruct((rows, H * HD), jnp.bfloat16),
            jax.ShapeDtypeStruct((H // 2, 2, rows), jnp.float32),
        ),
        grid_spec=pltpu.PrefetchScalarGridSpec(
            num_scalar_prefetch=1,
            grid=grid,
            in_specs=[specs["q"], specs["k"], specs["v"], specs["segq"], specs["segk"]]
            + extra[0],
            out_specs=[specs["q"], specs["lse"]],
            scratch_shapes=[
                scores,
                pltpu.VMEM((2 * HD * spec["pairs"], keys), jnp.bfloat16),
            ]
            + tiles,
        ),
        compiler_params=pltpu.CompilerParams(vmem_limit_bytes=40 << 20),
        cost_estimate=pl.CostEstimate(
            flops=16 * HD * work, transcendentals=work, bytes_accessed=8 << 20
        ),
    )(bounds, queries, keyval, keyval, segq, segk, *extra[1])


def attend_backward(queries, keyval, query_labels, key_labels, bias, causal, lse, dmixture):
    spec, bounds, segq, segk, specs, grid, scores = attention_setup(
        queries, keyval, query_labels, key_labels, bias, causal, 1
    )
    rows, keys = queries.shape[0], keyval.shape[0]
    work = H * rows * keys
    extra = ([specs["bias"]], [bias]) if bias is not None else ([], [])
    tiles = [pltpu.VMEM((2 * spec["pairs"], BAND, TILE, TILE), jnp.float32)] * len(extra[0])
    band = (
        [jax.ShapeDtypeStruct((H, BAND, FOLD, SPAN), jnp.float32)] if bias is not None else []
    )
    out = pl.pallas_call(
        functools.partial(backward_kernel, spec),
        out_shape=[
            jax.ShapeDtypeStruct((rows, H * HD), jnp.bfloat16),
            jax.ShapeDtypeStruct((keys, 2 * H * HD), jnp.bfloat16),
        ]
        + band,
        grid_spec=pltpu.PrefetchScalarGridSpec(
            num_scalar_prefetch=1,
            grid=grid,
            in_specs=[
                specs["q"],
                specs["k"],
                specs["v"],
                specs["q"],
                specs["lse"],
                specs["segq"],
                specs["segk"],
            ]
            + extra[0],
            out_specs=[specs["q"], specs["whole"]] + [specs["band"]] * len(band),
            scratch_shapes=[
                scores,
                scores,
                pltpu.VMEM((keys, 2 * HD * spec["pairs"]), jnp.float32),
                pltpu.VMEM((keys, 2 * HD * spec["pairs"]), jnp.float32),
                pltpu.VMEM((2 * HD * spec["pairs"], keys), jnp.bfloat16),
            ]
            + tiles
            + tiles,
        ),
        compiler_params=pltpu.CompilerParams(vmem_limit_bytes=48 << 20),
        cost_estimate=pl.CostEstimate(
            flops=40 * HD * work, transcendentals=work, bytes_accessed=16 << 20
        ),
    )(bounds, queries, keyval, keyval, dmixture, lse, segq, segk, *extra[1])
    return (out[0], out[1], out[2] if bias is not None else None)


def product(former, latter):
    return jnp.dot(former, latter, preferred_element_type=jnp.float32)


def transpose_product(former, latter):
    return lax.dot_general(
        former, latter, (((0,), (0,)), ((), ())), preferred_element_type=jnp.float32
    )


def product_transposed(former, latter):
    return lax.dot_general(
        former, latter, (((1,), (1,)), ((), ())), preferred_element_type=jnp.float32
    )


def smooth_gate(value):
    return jax.nn.gelu(value, approximate=True)


def norm_forward(stream, norm_gain):
    return (
        stream * lax.rsqrt(jnp.mean(stream * stream, axis=-1, keepdims=True) + EPSILON) * norm_gain
    )


def norm_backward(stream, norm_gain, gradient):
    outcome, pullback = jax.vjp(norm_forward, stream, norm_gain)
    return pullback(gradient)


def attention_forward(stream, norm_gain, wquery, wkeyval, wproj, layout, memory):
    normed = norm_forward(stream, norm_gain).astype(jnp.bfloat16)
    queries = product(normed, wquery).astype(jnp.bfloat16)
    source = normed if memory is None else memory
    keyval = product(source, wkeyval).astype(jnp.bfloat16)
    mixture, logsum = attend_forward(queries, keyval, *layout)
    return (stream + product(mixture, wproj), (normed, queries, keyval, mixture, logsum))


def attention_backward(
    grads, names, stream, norm_gain, wquery, wkeyval, wproj, layout, memory, stored, gradient
):
    normed, queries, keyval, mixture, logsum = stored
    gradient_low = gradient.astype(jnp.bfloat16)
    grads.add(names[2], mixture, gradient_low)
    dmixture = product_transposed(gradient_low, wproj).astype(jnp.bfloat16)
    dquery_low, dkeyval_low, band = attend_backward(queries, keyval, *layout, logsum, dmixture)
    source = normed if memory is None else memory
    grads.add(names[0], normed, dquery_low)
    grads.add(names[1], source, dkeyval_low)
    dnormed = product_transposed(dquery_low, wquery)
    dsource = product_transposed(dkeyval_low, wkeyval)
    if memory is None:
        dnormed = dnormed + dsource
        dsource = None
    dstream, dgain = norm_backward(stream, norm_gain, dnormed)
    return (gradient + dstream, dgain, band, dsource)


def feed_forward(stream, norm_gain, winner, wouter):
    normed = norm_forward(stream, norm_gain).astype(jnp.bfloat16)
    before = product(normed, winner)
    hidden = smooth_gate(before).astype(jnp.bfloat16)
    return (stream + product(hidden, wouter), (normed, before, hidden))


def feed_backward_kernel(g_ref, v_ref, gain_ref, pre_ref, wi_ref, wf_ref, *outs):
    out_ref, dpre_ref, low_ref, dgain_ref = outs
    gradient = g_ref[...]
    low = gradient.astype(jnp.bfloat16)
    low_ref[...] = low
    features, hidden = wi_ref.shape
    curve, bend = math.sqrt(2 / math.pi), 0.044715
    dnormed = None
    for start in range(0, hidden, features):
        span = slice(start, start + features)
        dhidden = dot_rows(low, wf_ref[span, :])
        value = pre_ref[:, span]
        square = value * value
        bent = jnp.tanh(value * (curve + curve * bend * square))
        slope = 0.5 * (1.0 + bent) + (0.5 * value) * (1.0 - bent * bent) * (
            curve + 3 * curve * bend * square
        )
        dpre = (dhidden * slope).astype(jnp.bfloat16)
        dpre_ref[:, span] = dpre
        part = dot_rows(dpre, wi_ref[:, span])
        dnormed = part if dnormed is None else dnormed + part
    value = v_ref[...]
    scale = lax.rsqrt(jnp.mean(value * value, axis=1, keepdims=True) + EPSILON)
    pulled = dnormed * gain_ref[...]
    inner = jnp.mean(pulled * value, axis=1, keepdims=True)
    out_ref[...] = gradient + scale * pulled - value * (scale * scale * scale * inner)
    dgain = fold_rows(dnormed * value * scale, jnp.add)

    @pl.when(pl.program_id(0) == 0)
    def _():
        dgain_ref[...] = dgain

    @pl.when(pl.program_id(0) > 0)
    def _():
        dgain_ref[...] += dgain


def feed_backward(grads, names, stream, norm_gain, winner, wouter, stored, gradient):
    normed, before, hidden = stored
    rows, features = stream.shape
    wide = before.shape[1]
    block = min(256, rows)
    row = pl.BlockSpec((block, features), lambda step: (step, 0))
    row_wide = pl.BlockSpec((block, wide), lambda step: (step, 0))
    once = pl.Buffered(1)
    dstream, dbefore, low, dgain = pl.pallas_call(
        feed_backward_kernel,
        out_shape=[
            jax.ShapeDtypeStruct((rows, features), jnp.float32),
            jax.ShapeDtypeStruct((rows, wide), jnp.bfloat16),
            jax.ShapeDtypeStruct((rows, features), jnp.bfloat16),
            jax.ShapeDtypeStruct((8, features), jnp.float32),
        ],
        grid=(rows // block,),
        in_specs=[
            row,
            row,
            pl.BlockSpec((1, features), lambda step: (0, 0)),
            row_wide,
            pl.BlockSpec((features, wide), lambda step: (0, 0), pipeline_mode=once),
            pl.BlockSpec((wide, features), lambda step: (0, 0), pipeline_mode=once),
        ],
        out_specs=[row, row_wide, row, pl.BlockSpec((8, features), lambda step: (0, 0))],
        compiler_params=pltpu.CompilerParams(vmem_limit_bytes=48 << 20),
        cost_estimate=pl.CostEstimate(
            flops=4 * rows * features * wide,
            transcendentals=rows * wide,
            bytes_accessed=rows * wide * 6 + 4 * features * wide + rows * features * 14,
        ),
    )(gradient, stream, norm_gain[None, :], before, winner, wouter)
    dstream = grads.add(names[1], hidden, low, dstream)
    dstream = grads.add(names[0], normed, dbefore, dstream)
    return (dstream, jnp.sum(dgain, axis=0))


def index_bits(devices):
    return devices.bit_length() - 1


class Links:
    def __init__(self, mesh):
        self.sizes = dict(mesh.shape)
        self.bits = [("fsdp", bit) for bit in range(index_bits(self.sizes["fsdp"]))]
        self.bits += [("dp", bit) for bit in range(index_bits(self.sizes["dp"]))]

    def side(self, axis, bit):
        return lax.rem(lax.axis_index(axis) // (1 << bit), 2)

    def partner(self, axis, bit):
        return {axis: lax.axis_index(axis) + (1 - 2 * self.side(axis, bit)) * (1 << bit)}

    def orders(self):
        core, row = ("dp", 0), ("fsdp", 0)
        rest = [key for key in self.bits if key not in (core, row)]
        third = [core] + rest[1:2] + rest[:1] + [row] + rest[2:]
        return ([core] + rest[:1] + [row] + rest[1:], [core, row] + rest, third)

    def swap(self, value, axis, bit):
        pairs = [(place, place ^ (1 << bit)) for place in range(self.sizes[axis])]
        return lax.ppermute(value, axis, pairs)

    def gather_small(self, shard):
        other = self.swap(shard, "fsdp", 0)
        first = lax.axis_index("fsdp") == 0
        return jnp.concatenate(
            [jnp.where(first, shard, other), jnp.where(first, other, shard)], axis=0
        )

    def devices(self):
        return self.sizes["dp"] * self.sizes["fsdp"]

    def place(self):
        return lax.axis_index("dp") * self.sizes["fsdp"] + lax.axis_index("fsdp")


def pick(ref, lead, spot, count, side):
    return ref.at[(lead,) + (slice(None),) * spot + (side,) + (slice(None),) * (count - spot - 1)]


def fold_product(x, dy, devices):
    total = lax.dot_general(x, dy, (((0,), (0,)), ((), ())), preferred_element_type=jnp.float32)
    rows, columns = total.shape
    total = total.reshape(devices, rows // devices, columns)
    half = columns // 2
    total = jnp.concatenate([total[:, :, :half], total[:, :, half:]], axis=1)
    return total.astype(jnp.bfloat16)


def reduce_kernel(links, plan, sides, count, *refs):
    stages, chunks = len(links.bits), len(plan)
    sources, (value_ref, out_ref, total_ref) = refs[:count], refs[count : count + 3]
    ring_ref, x_ref, y_ref, part_ref, come_ref = refs[count + 3 : count + 8]
    deep_ref, side_x_ref, side_y_ref = refs[count + 8 : count + 11]
    rest = refs[count + 11 :]
    sums, rest = rest[:stages], rest[stages:]
    send_sem, recv_sem, load_sem, part_sem, come_sem, side_sem = rest
    halvings = []
    for order in links.orders():
        left = list(reversed(links.bits))
        halving = []
        for key in order:
            halving.append((key, left.index(key), len(left)))
            left.remove(key)
        halvings.append(halving)
    kinds = len(halvings)

    barrier = pltpu.get_barrier_semaphore()
    for key in links.bits:
        pl.semaphore_signal(
            barrier,
            inc=1,
            device_id=links.partner(*key),
            device_id_type=pl.DeviceIdType.MESH,
        )
    pl.semaphore_wait(barrier, stages)

    def source(stage, chunk, kind, away):
        key, spot, width = halvings[kind][stage]
        side = links.side(*key)
        ref, lead = (ring_ref, lax.rem(chunk, HOLD)) if stage == 0 else (sums[stage - 1], chunk)
        return pick(ref, lead, spot, width, 1 - side if away else side)

    def send(stage, chunk, kind):
        key, _, _ = halvings[kind][stage]
        return pltpu.make_async_remote_copy(
            src_ref=source(stage, chunk, kind, True),
            dst_ref=sums[stage].at[chunk],
            send_sem=send_sem.at[stage, chunk],
            recv_sem=recv_sem.at[stage, chunk],
            device_id=links.partner(*key),
            device_id_type=pl.DeviceIdType.MESH,
        )

    def trade(stage):
        return pltpu.make_async_remote_copy(
            src_ref=part_ref.at[stage],
            dst_ref=come_ref.at[stage],
            send_sem=part_sem.at[stage],
            recv_sem=come_sem.at[stage],
            device_id=links.partner(*links.bits[stage]),
            device_id_type=pl.DeviceIdType.MESH,
        )

    def loads(chunk):
        item = plan[chunk]
        if item[0] == "chunk":
            _, which, index = item
            return [
                pltpu.make_async_copy(
                    sources[which].at[index], ring_ref.at[chunk % HOLD], load_sem.at[chunk % 2, 0]
                )
            ]
        if item[0] == "kept":
            return [
                pltpu.make_async_copy(
                    deep_ref.at[item[1]], ring_ref.at[chunk % HOLD], load_sem.at[chunk % 2, 0]
                )
            ]
        _, rows, *operands = item
        slot = chunk % 2
        result = []
        for place, (which, column) in enumerate(operands):
            buffer = (x_ref, y_ref)[place]
            width = buffer.shape[2]
            result.append(
                pltpu.make_async_copy(
                    sources[which].at[:, column * width : (column + 1) * width],
                    buffer.at[slot, :rows],
                    load_sem.at[slot, place],
                )
            )
        return result

    def side_loads(side):
        width = x_ref.shape[2]
        return [
            pltpu.make_async_copy(
                sources[which].at[:, column * width : (column + 1) * width],
                (side_x_ref, side_y_ref)[place],
                side_sem.at[place],
            )
            for place, (which, column) in enumerate(sides[side])
        ]

    def make_side(side):
        deep = len(sides)
        total = lax.dot_general(
            side_x_ref[...],
            side_y_ref[...],
            (((0,), (0,)), ((), ())),
            preferred_element_type=jnp.float32,
        )
        rows, columns = total.shape
        half, r = columns // 2, ring_ref.shape[-2] // 2
        total = total.reshape(rows // deep // r, deep, r, columns)
        spot = tuple((side >> bit) & 1 for bit in reversed(range(index_bits(deep))))
        for part in range(deep):
            piece = total[:, part]
            piece = jnp.concatenate([piece[:, :, :half], piece[:, :, half:]], axis=1)
            target = (part,) + spot
            deep_ref[target] = piece.astype(jnp.bfloat16).reshape(
                deep_ref.shape[len(target) :]
            )

    sizes = sorted({item[1] for item in plan if item[0] == "product"})

    def step(group, carry):
        for stage in range(stages):

            @pl.when(group == stage + 1)
            def _():
                trade(stage).wait()
                total = part_ref[stage] + come_ref[stage]
                if stage < stages - 1:
                    part_ref[stage + 1] = total
                    trade(stage + 1).start()
                else:
                    total_ref[...] = total

        for turn in range(kinds):
            now = group * kinds + turn

            for stage in range(stages):
                chunk = now - DELAY * (stage + 1)
                kind = (turn - DELAY * (stage + 1)) % kinds

                @pl.when((chunk >= 0) & (chunk < chunks))
                def _():
                    send(stage, chunk, kind).wait()
                    mine = source(stage, chunk, kind, False)[...]
                    if stage < stages - 1:
                        sums[stage][chunk] = sums[stage][chunk] + mine
                        send(stage + 1, chunk, kind).start()
                    else:
                        out_ref[chunk] = sums[stage][chunk].astype(jnp.float32) + mine.astype(
                            jnp.float32
                        )

            for chunk in range(turn, chunks, kinds):

                @pl.when(now == chunk)
                def _():
                    for load in loads(chunk):
                        load.wait()

            for rows in sizes:
                spots = [spot for spot, item in enumerate(plan) if item[:2] == ("product", rows)]

                @pl.when((now >= spots[0]) & (now <= spots[-1]))
                def _():
                    slot = lax.rem(now, 2)
                    made = fold_product(x_ref[slot, :rows], y_ref[slot, :rows], links.devices())
                    ring_ref[lax.rem(now, HOLD)] = made.reshape(ring_ref.shape[1:])

            @pl.when(now < chunks)
            def _():
                send(0, now, turn).start()

            for side in range(len(sides)):
                spot = 2 * side + 2

                if (spot - 1) % kinds == turn:

                    @pl.when(now == spot - 1)
                    def _():
                        for load in side_loads(side):
                            load.start()

                if spot % kinds == turn:

                    @pl.when(now == spot)
                    def _():
                        for load in side_loads(side):
                            load.wait()
                        make_side(side)

            for chunk in range((turn + 1) % kinds, chunks, kinds):

                @pl.when(now + 1 == chunk)
                def _():
                    for load in loads(chunk):
                        load.start()

        return carry

    for load in loads(0):
        load.start()
    part_ref[0] = value_ref[...]
    trade(0).start()
    slots = chunks + DELAY * stages
    lax.fori_loop(0, (slots + kinds - 1) // kinds, step, 0)


def reduce_chunks(links, plan, sides, sources, value, shape, width, collective_id):
    stages, chunks = len(links.bits), len(plan)
    sums = [
        pltpu.VMEM((chunks,) + (2,) * (stages - 1 - stage) + shape, jnp.bfloat16)
        for stage in range(stages)
    ]
    rows = max([item[1] for item in plan if item[0] == "product"] + [16])
    return pl.pallas_call(
        functools.partial(reduce_kernel, links, plan, sides, len(sources)),
        out_shape=[
            jax.ShapeDtypeStruct((chunks,) + shape, jnp.float32),
            jax.ShapeDtypeStruct(value.shape, jnp.float32),
        ],
        in_specs=[pl.BlockSpec(memory_space=pltpu.HBM)] * len(sources)
        + [pl.BlockSpec(memory_space=pltpu.VMEM)],
        out_specs=[pl.BlockSpec(memory_space=pltpu.VMEM)] * 2,
        scratch_shapes=[
            pltpu.VMEM((HOLD,) + (2,) * stages + shape, jnp.bfloat16),
            pltpu.VMEM((2, rows, width), jnp.bfloat16),
            pltpu.VMEM((2, rows, width), jnp.bfloat16),
            pltpu.VMEM((stages,) + value.shape, jnp.float32),
            pltpu.VMEM((stages,) + value.shape, jnp.float32),
            pltpu.VMEM((max(1, len(sides)),) + (2,) * stages + shape, jnp.bfloat16),
            pltpu.VMEM((rows, width), jnp.bfloat16),
            pltpu.VMEM((rows, width), jnp.bfloat16),
        ]
        + sums
        + [
            pltpu.SemaphoreType.DMA((stages, chunks)),
            pltpu.SemaphoreType.DMA((stages, chunks)),
            pltpu.SemaphoreType.DMA((2, 2)),
            pltpu.SemaphoreType.DMA((stages,)),
            pltpu.SemaphoreType.DMA((stages,)),
            pltpu.SemaphoreType.DMA((2,)),
        ],
        compiler_params=pltpu.CompilerParams(
            collective_id=collective_id, has_side_effects=True, vmem_limit_bytes=60 << 20
        ),
    )(*sources, value)


def fold_grad(grad, devices, width):
    rows, columns = grad.shape
    deep, wide = rows // width, columns // width
    r = rows // devices // deep
    grad = grad.astype(jnp.bfloat16).reshape(devices, deep, r, wide, 2, width // 2)
    return grad.transpose(1, 3, 0, 4, 2, 5).reshape(deep * wide, devices, 2 * r, width // 2)


def unfold_share(chunks, rows, columns):
    count, folded, half = chunks.shape
    deep, wide = rows * 2 // folded, columns // (2 * half)
    chunks = chunks.reshape(deep, wide, 2, folded // 2, half)
    return chunks.transpose(0, 3, 1, 2, 4).reshape(rows, columns)


def gather_kernel(links, units, count, *refs):
    shards, wholes, held = refs[:count], refs[count : 2 * count], refs[2 * count : 3 * count]
    send_sem, recv_sem, local_sem = refs[3 * count :]
    core, mesh_id = ("dp", 0), pl.DeviceIdType.MESH
    keys = [("dp", 1), ("dp", 2), core]
    orders = [[keys[0], keys[1], core], [keys[1], keys[0], core]]
    row = ("fsdp", 0)
    place = lax.axis_index("fsdp")

    barrier = pltpu.get_barrier_semaphore()
    for key in [row] + keys:
        pl.semaphore_signal(
            barrier, inc=1, device_id=links.partner(*key), device_id_type=mesh_id
        )
    pl.semaphore_wait(barrier, 1 + len(keys))

    def piece(known):
        return tuple(slice(None) if key in known else links.side(*key) for key in keys)

    def send(stage, unit):
        order = orders[unit % 2]
        number, rows, columns = units[unit]
        if stage == 0:
            key, where = row, piece([])
            src = shards[number].at[where + (rows, columns)]
        else:
            key, where = order[stage - 1], piece(order[: stage - 1])
            src = wholes[number].at[(1 - place,) + where + (rows, columns)]
        dst = wholes[number].at[
            (place if stage == 0 else 1 - place,) + where + (rows, columns)
        ]
        return pltpu.make_async_remote_copy(
            src_ref=src,
            dst_ref=dst,
            send_sem=send_sem.at[stage, unit],
            recv_sem=recv_sem.at[stage, unit],
            device_id=links.partner(*key),
            device_id_type=mesh_id,
        )

    def load(number):
        return pltpu.make_async_copy(shards[number], held[number], local_sem.at[0, number])

    def keep(number):
        return pltpu.make_async_copy(
            held[number], wholes[number].at[place], local_sem.at[1, number]
        )

    stages = 1 + len(keys)
    for unit in range(len(units)):
        send(0, unit).start()
    for number in range(count):
        load(number).start()
    for slot in range(len(units) + LAG * (stages - 1)):
        for stage in range(stages):
            unit = slot - LAG * stage
            if 0 <= unit < len(units):
                send(stage, unit).wait()
                if stage + 1 < stages:
                    send(stage + 1, unit).start()
        if slot < count:
            load(slot).wait()
            keep(slot).start()
    for number in range(count):
        keep(number).wait()


def gather_units(shards, width):
    least = min(shard.shape[0] for shard in shards)
    units = []
    for number, shard in enumerate(shards):
        deep, wide = shard.shape[0] // least, shard.shape[1] // width
        rows = shard.shape[0] // 8 // deep
        for part in range(deep):
            for column in range(wide):
                units.append(
                    (
                        number,
                        slice(part * rows, (part + 1) * rows),
                        slice(column * width, (column + 1) * width),
                    )
                )
    return units


def gather_weights(links, shards, collective_id):
    count = len(shards)
    units = gather_units(shards, shards[0].shape[1])
    split = [
        shard.reshape(2, 2, 2, shard.shape[0] // 8, shard.shape[1]) for shard in shards
    ]
    wholes = pl.pallas_call(
        functools.partial(gather_kernel, links, units, count),
        out_shape=[jax.ShapeDtypeStruct((2,) + piece.shape, piece.dtype) for piece in split],
        in_specs=[pl.BlockSpec(memory_space=pltpu.HBM)] * count,
        out_specs=[pl.BlockSpec(memory_space=pltpu.HBM)] * count,
        scratch_shapes=[pltpu.VMEM(piece.shape, piece.dtype) for piece in split]
        + [
            pltpu.SemaphoreType.DMA((4, len(units))),
            pltpu.SemaphoreType.DMA((4, len(units))),
            pltpu.SemaphoreType.DMA((2, count)),
        ],
        compiler_params=pltpu.CompilerParams(
            collective_id=collective_id, has_side_effects=True, vmem_limit_bytes=60 << 20
        ),
    )(*split)
    return [
        whole.reshape(2 * shard.shape[0], shard.shape[1]) for whole, shard in zip(wholes, shards)
    ]


def weight_kernel(deep, x_ref, dy_ref, *rest):
    out_ref = rest[-1]
    total = lax.dot_general(
        x_ref[...], dy_ref[...], (((0,), (0,)), ((), ())), preferred_element_type=jnp.float32
    )
    half = total.shape[1] // 2
    rows = out_ref.shape[2] // 2
    total = total.reshape(out_ref.shape[1], deep, rows, 2 * half)
    for part in range(deep):
        piece = total[:, part]
        piece = jnp.concatenate([piece[:, :, :half], piece[:, :, half:]], axis=1)
        out_ref[part] = piece.astype(jnp.bfloat16)


def weight_chunks(x, dy, chunks, start, count, devices, width):
    rows, deep, wide = x.shape[0], x.shape[1] // width, dy.shape[1] // width
    r = width // devices
    if deep == 1:
        specs = [
            pl.BlockSpec((rows, width), lambda w: (0, 0)),
            pl.BlockSpec((rows, width), lambda w: (0, w)),
        ]
        out_spec = pl.BlockSpec((1, devices, 2 * r, width // 2), lambda w: (start + w, 0, 0, 0))
    else:
        specs = [
            pl.BlockSpec((rows, width), lambda w: (0, w)),
            pl.BlockSpec((rows, width), lambda w: (0, 0)),
        ]
        out_spec = pl.BlockSpec(
            (deep, devices // deep, 2 * r, width // 2), lambda w: (start // deep, w, 0, 0)
        )
    extra = [] if chunks is None else [chunks]
    return pl.pallas_call(
        functools.partial(weight_kernel, deep),
        out_shape=jax.ShapeDtypeStruct((count, devices, 2 * r, width // 2), jnp.bfloat16),
        grid=(max(deep, wide),),
        in_specs=specs + [pl.BlockSpec(memory_space=pltpu.HBM)] * len(extra),
        out_specs=out_spec,
        input_output_aliases={2: 0} if extra else {},
        compiler_params=pltpu.CompilerParams(vmem_limit_bytes=40 << 20),
        cost_estimate=pl.CostEstimate(
            flops=2 * rows * x.shape[1] * dy.shape[1],
            transcendentals=0,
            bytes_accessed=2 * (x.size + dy.size + x.shape[1] * dy.shape[1]),
        ),
    )(x, dy, *extra)


class Gradients:
    def __init__(self, links, width):
        self.links, self.width = links, width
        self.products, self.scattered = {}, {}

    def add(self, name, x, dy, carry=None):
        if name in OFFLOADED:
            grad = transpose_product(x, dy).astype(jnp.bfloat16)
            if carry is not None:
                grad, carry = lax.optimization_barrier((grad, carry))
            self.scattered[name] = lax.psum_scatter(
                grad, ("dp", "fsdp"), scatter_dimension=0, tiled=True
            )
        else:
            self.products[name] = (x, dy)
        return carry

    def shares(self, collective_id, value):
        width, devices = self.width, self.links.devices()
        r = width // devices
        aligned = r % 8 == 0
        names = list(self.products)
        size = {name: self.products[name][0].shape for name in names}
        deep = {name: size[name][1] // width for name in names}
        tallest = max(rows for rows, _ in size.values())
        split = [name for name in names if deep[name] > 1 and size[name][0] == tallest][:1]
        if not aligned or 2 * max(deep.values()) + 2 > len(names) + 4:
            split = []
        names.sort(key=lambda name: (name in split, deep[name] == 1, size[name][0]))
        sides = []
        plan, sources, known = [], [], {}

        def number(array):
            if id(array) not in known:
                known[id(array)] = len(sources)
                sources.append(array)
            return known[id(array)]

        shapes = {}
        for name in names:
            x, dy = self.products[name]
            shapes[name] = (x.shape[1] // devices, dy.shape[1])
            wide = dy.shape[1] // width
            if aligned and deep[name] == 1:
                for part in range(wide):
                    plan.append(("product", x.shape[0], (number(x), 0), (number(dy), part)))
                continue
            count = deep[name] * wide
            if name in split:
                sides += [((number(x), part), (number(dy), 0)) for part in range(count)]
                plan += [("kept", part) for part in range(count)]
                continue
            if aligned:
                made = weight_chunks(x, dy, None, 0, count, devices, width)
            else:
                made = fold_grad(transpose_product(x, dy), devices, width)
            made = made.reshape((count,) + (2,) * len(self.links.bits) + made.shape[2:])
            for part in range(count):
                plan.append(("chunk", number(made), part))
        shares, total = reduce_chunks(
            self.links, plan, sides, sources, value, (2 * r, width // 2), width, collective_id
        )
        if aligned:
            scattered = list(self.scattered.values())
            result = pl.pallas_call(
                functools.partial(unfold_kernel, width, len(scattered)),
                out_shape=[jax.ShapeDtypeStruct(shape, jnp.float32) for shape in shapes.values()]
                + [jax.ShapeDtypeStruct(share.shape, jnp.float32) for share in scattered],
            )(shares, *scattered)
            return dict(zip(list(shapes) + list(self.scattered), result)), total
        result = {name: share.astype(jnp.float32) for name, share in self.scattered.items()}
        start = 0
        for name, shape in shapes.items():
            count = deep[name] * shape[1] // width
            result[name] = unfold_share(shares[start : start + count], *shape)
            start += count
        return result, total


def unfold_kernel(width, count, shares_ref, *refs):
    scattered, out_refs = refs[:count], refs[count:]
    if count:
        for scattered_ref, out_ref in zip(scattered, out_refs[-count:]):
            out_ref[...] = scattered_ref[...].astype(jnp.float32)
        out_refs = out_refs[:-count]
    chunk, r, half = 0, shares_ref.shape[1] // 2, width // 2
    for out_ref in out_refs:
        for row in range(0, out_ref.shape[0], r):
            for column in range(0, out_ref.shape[1], width):
                for part in range(2):
                    out_ref[
                        row : row + r, column + part * half : column + (part + 1) * half
                    ] = shares_ref[chunk, part * r : (part + 1) * r, :]
                chunk += 1


def body(
    links,
    enc_tokens,
    dec_tokens,
    enc_segments,
    dec_segments,
    enc_upstream,
    dec_upstream,
    encoder_query,
    encoder_keyval,
    encoder_proj,
    encoder_inner,
    encoder_outer,
    encoder_gains,
    encoder_table,
    decoder_query,
    decoder_keyval,
    decoder_proj,
    cross_query,
    cross_keyval,
    cross_proj,
    decoder_inner,
    decoder_outer,
    decoder_gains,
    decoder_table,
):
    small = jnp.concatenate(
        [encoder_gains, decoder_gains]
        + [
            jnp.concatenate([encoder_table, decoder_table], axis=0).reshape(
                encoder_gains.shape[0], -1
            )
        ],
        axis=1,
    )
    small = links.gather_small(small)
    enc_gains = small[:, 0:2].astype(jnp.float32)
    dec_gains = small[:, 2:5].astype(jnp.float32)
    tables = small[:, 5:].reshape(2, 2, NB // 2, H)
    enc_bias = band_bias(tables[:, 0].reshape(NB, H), encoder_bucket)
    dec_bias = band_bias(tables[:, 1].reshape(NB, H), decoder_bucket)

    shards = [
        encoder_query,
        encoder_keyval,
        encoder_proj,
        encoder_inner,
        encoder_outer,
        decoder_query,
        decoder_keyval,
        decoder_proj,
        cross_query,
        cross_keyval,
        cross_proj,
        decoder_inner,
        decoder_outer,
    ]
    shards = dict(zip(NAMES, shards))
    later = [shards.pop(name) for name in LATER]
    weights = dict(zip(shards, gather_weights(links, list(shards.values()), 1)))
    weights["equery"], *later = lax.optimization_barrier((weights["equery"], *later))
    for name, shard in zip(LATER, later):
        weights[name] = lax.all_gather(shard, "fsdp", axis=0, tiled=True)
    grads = Gradients(links, encoder_query.shape[1])

    enc_layout = (enc_segments, enc_segments, enc_bias, False)
    dec_layout = (dec_segments, dec_segments, dec_bias, True)
    cross_layout = (dec_segments, enc_segments, None, False)

    enc_stream = enc_tokens.astype(jnp.float32)
    enc_middle, enc_self = attention_forward(
        enc_stream, enc_gains[:, 0], weights["equery"], weights["ekeyval"], weights["eproj"], enc_layout, None
    )
    enc_final, enc_ffn = feed_forward(enc_middle, enc_gains[:, 1], weights["einner"], weights["eouter"])
    memory = enc_final.astype(jnp.bfloat16)

    dec_stream = dec_tokens.astype(jnp.float32)
    after_self, dec_self = attention_forward(
        dec_stream, dec_gains[:, 0], weights["dquery"], weights["dkeyval"], weights["dproj"], dec_layout, None
    )
    after_cross, dec_cross = attention_forward(
        after_self, dec_gains[:, 1], weights["cquery"], weights["ckeyval"], weights["cproj"], cross_layout, memory
    )
    dec_final, dec_ffn = feed_forward(after_cross, dec_gains[:, 2], weights["dinner"], weights["douter"])


    dec_live = (dec_segments >= 0).astype(jnp.float32)[:, None]
    gradient = dec_upstream.astype(jnp.float32) * dec_live
    gradient, dgain_ffn = feed_backward(
        grads, ("dinner", "douter"), after_cross, dec_gains[:, 2], weights["dinner"], weights["douter"], dec_ffn, gradient
    )
    gradient, dgain_cross, _, memory_grad = (
        attention_backward(
            grads,
            ("cquery", "ckeyval", "cproj"),
            after_self,
            dec_gains[:, 1],
            weights["cquery"],
            weights["ckeyval"],
            weights["cproj"],
            cross_layout,
            memory,
            dec_cross,
            gradient,
        )
    )
    dec_gradient, dgain_self, dec_band, _ = (
        attention_backward(
            grads,
            ("dquery", "dkeyval", "dproj"),
            dec_stream,
            dec_gains[:, 0],
            weights["dquery"],
            weights["dkeyval"],
            weights["dproj"],
            dec_layout,
            None,
            dec_self,
            gradient,
        )
    )

    enc_live = (enc_segments >= 0).astype(jnp.float32)[:, None]
    gradient = enc_upstream.astype(jnp.float32) * enc_live + memory_grad
    gradient, egain_ffn = feed_backward(
        grads, ("einner", "eouter"), enc_middle, enc_gains[:, 1], weights["einner"], weights["eouter"], enc_ffn, gradient
    )
    enc_gradient, egain_self, enc_band, _ = (
        attention_backward(
            grads,
            ("equery", "ekeyval", "eproj"),
            enc_stream,
            enc_gains[:, 0],
            weights["equery"],
            weights["ekeyval"],
            weights["eproj"],
            enc_layout,
            None,
            enc_self,
            gradient,
        )
    )

    table_grads = [
        band_table_grad(enc_band, encoder_bucket),
        band_table_grad(dec_band, decoder_bucket),
    ]
    gain_grads = jnp.stack([egain_self, egain_ffn, dgain_self, dgain_cross, dgain_ffn])
    flat = jnp.concatenate([gain_grads.reshape(-1)] + [grad.reshape(-1) for grad in table_grads])
    count = flat.shape[0]
    flat = jnp.pad(flat, (0, -count % (8 * TILE)))
    shares, flat = grads.shares(0, flat.reshape(-1, TILE))
    flat = flat.reshape(-1)
    width = gain_grads.shape[1]
    tables_grad = flat[5 * width : count].reshape(2, NB, H)
    own = width // links.devices()
    gains_share = lax.dynamic_slice_in_dim(
        flat[: 5 * width].reshape(5, width), links.place() * own, own, 1
    ).T
    return (
        memory,
        dec_final.astype(jnp.bfloat16),
        enc_gradient,
        dec_gradient,
        shares["equery"],
        shares["ekeyval"],
        shares["eproj"],
        shares["einner"],
        shares["eouter"],
        gains_share[:, 0:2],
        tables_grad[0],
        shares["dquery"],
        shares["dkeyval"],
        shares["dproj"],
        shares["cquery"],
        shares["ckeyval"],
        shares["cproj"],
        shares["dinner"],
        shares["douter"],
        gains_share[:, 2:5],
        tables_grad[1],
    )


def solution(mesh):
    in_specs = (
        P(("dp", "fsdp"), None),
        P(("dp", "fsdp"), None),
        P(("dp", "fsdp")),
        P(("dp", "fsdp")),
        P(("dp", "fsdp"), None),
        P(("dp", "fsdp"), None),
        P("fsdp", None),
        P("fsdp", None),
        P("fsdp", None),
        P("fsdp", None),
        P("fsdp", None),
        P("fsdp", None),
        P("fsdp", None),
        P("fsdp", None),
        P("fsdp", None),
        P("fsdp", None),
        P("fsdp", None),
        P("fsdp", None),
        P("fsdp", None),
        P("fsdp", None),
        P("fsdp", None),
        P("fsdp", None),
        P("fsdp", None),
    )
    out_specs = (
        P(("dp", "fsdp"), None),
        P(("dp", "fsdp"), None),
        P(("dp", "fsdp"), None),
        P(("dp", "fsdp"), None),
        P(("dp", "fsdp"), None),
        P(("dp", "fsdp"), None),
        P(("dp", "fsdp"), None),
        P(("dp", "fsdp"), None),
        P(("dp", "fsdp"), None),
        P(("dp", "fsdp"), None),
        P(),
        P(("dp", "fsdp"), None),
        P(("dp", "fsdp"), None),
        P(("dp", "fsdp"), None),
        P(("dp", "fsdp"), None),
        P(("dp", "fsdp"), None),
        P(("dp", "fsdp"), None),
        P(("dp", "fsdp"), None),
        P(("dp", "fsdp"), None),
        P(("dp", "fsdp"), None),
        P(),
    )
    return jax.shard_map(
        functools.partial(body, Links(mesh)), mesh=mesh, in_specs=in_specs, out_specs=out_specs, check_vma=False)
```

```python
import functools
import math

import jax
import jax.numpy as jnp
import numpy as np
from jax import lax
from jax.experimental import pallas as pl
from jax.experimental.pallas import tpu as pltpu
from jax.sharding import PartitionSpec as P

H = 12
HD = 64
NB = 32
TILE = 128
BAND = 5
EPSILON = 1e-06
MASKED = -1e30
ENC_EDGES = (12, 16, 23, 32, 46, 64, 91)
DEC_EDGES = tuple((math.ceil(16 * 2 ** (3 * power / 16)) for power in range(1, 16)))
PADDING_LABEL = 1 << 20
SPAN = 2 * TILE
FOLD = 8
LAG = 3
DELAY = 2
HOLD = DELAY + 1
OFFLOADED = ("douter",)
LATER = ("dinner",)
NAMES = (
    "equery",
    "ekeyval",
    "eproj",
    "einner",
    "eouter",
    "dquery",
    "dkeyval",
    "dproj",
    "cquery",
    "ckeyval",
    "cproj",
    "dinner",
    "douter",
)


def encoder_bucket(distance):
    reach = np.abs(distance)
    farther = 8 + sum((reach >= threshold).astype(np.int32) for threshold in ENC_EDGES)
    return np.where(reach < 8, reach, farther) + 16 * (distance < 0).astype(np.int32)


def decoder_bucket(distance):
    ahead = np.maximum(distance, 0)
    farther = 16 + sum((ahead >= threshold).astype(np.int32) for threshold in DEC_EDGES)
    return np.where(ahead < 16, ahead, farther)


def band_distances(rows):
    step = np.arange(BAND)[:, None, None] - 2
    row = np.arange(rows)[None, :, None]
    lane = np.arange(SPAN)[None, None, :]
    lane = np.where(lane < TILE, lane, lane - SPAN)
    return step * TILE + lane - row


def bucket_onehot(bucket_of, rows, dtype):
    bucket = jnp.asarray(bucket_of(band_distances(rows)).reshape(1, -1), jnp.int32)
    return (bucket == lax.broadcasted_iota(jnp.int32, (NB, 1), 0)).astype(dtype)


def band_bias(table, bucket_of):
    onehot = bucket_onehot(bucket_of, 1, jnp.bfloat16)
    flat = lax.dot_general(
        table, onehot, (((0,), (0,)), ((), ())), preferred_element_type=jnp.float32
    )
    return flat.reshape(H, BAND, SPAN)


def band_table_grad(band, bucket_of):
    return lax.dot_general(
        bucket_onehot(bucket_of, FOLD, jnp.float32),
        band.reshape(H, BAND * FOLD * SPAN),
        (((1,), (1,)), ((), ())),
        precision=lax.Precision.HIGHEST,
        preferred_element_type=jnp.float32,
    )


def key_bounds(query_labels, key_labels, query_rows, key_rows):
    queries = jnp.where(query_labels < 0, PADDING_LABEL, query_labels).reshape(-1, query_rows)
    keys = jnp.where(key_labels < 0, PADDING_LABEL, key_labels)
    first = jnp.sum((keys[None, :] < queries[:, :1]).astype(jnp.int32), axis=1)
    last = jnp.sum((keys[None, :] <= queries[:, -1:]).astype(jnp.int32), axis=1)
    return jnp.stack([first // key_rows, (last + key_rows - 1) // key_rows])


def fold_rows(value, combine):
    rows = value.shape[0]
    while rows > 8:
        rows //= 2
        value = combine(value[:rows], value[rows:])
    return value


def head_parts(block):
    lane = lax.broadcasted_iota(jnp.int32, block.shape, 1)
    zero = jnp.zeros_like(block)
    return (jnp.where(lane < HD, block, zero), jnp.where(lane < HD, zero, block))


def flip(value):
    return value.astype(jnp.float32).T


def band_index(query_tile, key_tile):
    return jnp.clip(query_tile - key_tile, -2, 2) + 2


def spread_bias(bias_ref, tiles_ref):
    for head in range(tiles_ref.shape[0]):
        for step in range(BAND):
            row = bias_ref[head, step : step + 1, :]
            if step in (0, BAND - 1):
                tiles_ref[head, step] = jnp.broadcast_to(row[:, :TILE], (TILE, TILE))
            else:
                wide = jnp.broadcast_to(row, (TILE, SPAN))
                wide = pltpu.roll(wide, 0, 1, stride=1, stride_axis=0)
                tiles_ref[head, step] = wide[:, :TILE]


def gather_diagonals(tiles_ref, band_ref):
    for head in range(tiles_ref.shape[0]):
        for step in range(BAND):
            tile = tiles_ref[head, step]
            tile = jnp.concatenate([tile, jnp.zeros_like(tile)], axis=1)
            rows = TILE
            while rows > FOLD:
                rows //= 2
                tile = tile[:rows] + pltpu.roll(tile[rows:], SPAN - rows, 1)
            band_ref[head, step] = tile


def tile_mask(spec, key_tile, query_block, segk_ref, segq_ref):
    rows, lanes = spec["kb"], spec["qb"]
    start = pl.multiple_of(key_tile * rows, rows) if spec["skip"] else key_tile * rows
    labels = segk_ref[pl.ds(start, rows), :]
    labels = jnp.concatenate([labels] * (lanes // TILE), axis=1)
    mask = labels == segq_ref[...]
    if spec["causal"]:
        key = lax.broadcasted_iota(jnp.int32, (rows, lanes), 0) + key_tile * rows
        query = lax.broadcasted_iota(jnp.int32, (rows, lanes), 1) + query_block * lanes
        mask = mask & (key <= query)
    return mask


def tile_bias(spec, head, key_tile, query_block, bias_ref):
    rows, lanes = spec["kb"] // TILE, spec["qb"] // TILE
    return jnp.concatenate(
        [
            jnp.concatenate(
                [
                    bias_ref[
                        head, band_index(query_block * lanes + lane, key_tile * rows + row)
                    ]
                    for lane in range(lanes)
                ],
                axis=1,
            )
            for row in range(rows)
        ],
        axis=0,
    )


def dot_rows(former, latter):
    return lax.dot_general(
        former, latter, (((1,), (1,)), ((), ())), preferred_element_type=jnp.float32
    )


def dot_plain(former, latter):
    return jnp.dot(former, latter, preferred_element_type=jnp.float32)


def for_counts(spec, first, last, run):
    if not spec["skip"]:
        run(0, spec["tiles"])
        return
    for count in range(1, spec["tiles"] + 1):
        pl.when(last - first == count)(functools.partial(run, first, count))


def forward_kernel(spec, bounds_ref, q_ref, k_ref, v_ref, segq_ref, segk_ref, *rest):
    bias_ref, rest = (rest[0], rest[1:]) if spec["bias"] else (None, rest)
    o_ref, lse_ref, score_ref, vt_ref, rest = *rest[:4], rest[4:]
    tiles_ref = rest[0] if spec["bias"] else None
    kb, qb, pairs = spec["kb"], spec["qb"], spec["pairs"]
    block = pl.program_id(1)

    @pl.when(block == 0)
    def _():
        for pair in range(pairs):
            span = slice(pair * 2 * HD, (pair + 1) * 2 * HD)
            vt_ref[span, :] = flip(v_ref[:, span]).astype(jnp.bfloat16)
        if spec["bias"]:
            spread_bias(bias_ref, tiles_ref)

    def run(first, count):
        starts = [(first + tile) * kb for tile in range(count)]
        if spec["skip"]:
            starts = [pl.multiple_of(start, kb) for start in starts]
        for pair in range(pairs):
            span = slice(pair * 2 * HD, (pair + 1) * 2 * HD)
            parts = head_parts(q_ref[:, span])
            mixed, logsum = [], []
            for head in range(2):
                number = 2 * pair + head
                top = None
                for tile in range(count):
                    s = dot_rows(k_ref[pl.ds(starts[tile], kb), span], parts[head])
                    if spec["bias"]:
                        s = s + tile_bias(spec, number, first + tile, block, tiles_ref)
                    mask = tile_mask(spec, first + tile, block, segk_ref, segq_ref)
                    s = jnp.where(mask, s, MASKED)
                    score_ref[number, tile] = s
                    peak = fold_rows(s, jnp.maximum)
                    top = peak if top is None else jnp.maximum(top, peak)
                top = jnp.max(top, axis=0, keepdims=True)
                total = None
                for tile in range(count):
                    e = jnp.exp(score_ref[number, tile] - top)
                    score_ref[number, tile] = e
                    part = fold_rows(e, jnp.add)
                    total = part if total is None else total + part
                total = jnp.sum(total, axis=0, keepdims=True)
                scale = 1.0 / total
                mix = None
                for tile in range(count):
                    weights = (score_ref[number, tile] * scale).astype(jnp.bfloat16)
                    rows = slice(number * HD, (number + 1) * HD)
                    part = dot_plain(vt_ref[rows, pl.ds(starts[tile], kb)], weights)
                    mix = part if mix is None else mix + part
                mixed.append(mix)
                logsum.append(top + jnp.log(total))
            o_ref[:, span] = flip(jnp.concatenate(mixed, axis=0)).astype(jnp.bfloat16)
            lse_ref[pair] = jnp.concatenate(logsum, axis=0)

    for_counts(spec, bounds_ref[0, block], bounds_ref[1, block], run)


def backward_kernel(
    spec, bounds_ref, q_ref, k_ref, v_ref, do_ref, lse_ref, segq_ref, segk_ref, *rest
):
    bias_ref, rest = (rest[0], rest[1:]) if spec["bias"] else (None, rest)
    dq_ref, dkv_ref, rest = rest[0], rest[1], rest[2:]
    band_ref, rest = (rest[0], rest[1:]) if spec["bias"] else (None, rest)
    p_ref, dp_ref, dk_ref, dv_ref, kt_ref, rest = *rest[:5], rest[5:]
    tiles_ref, dtiles_ref = rest if spec["bias"] else (None, None)
    kb, qb, pairs = spec["kb"], spec["qb"], spec["pairs"]
    group, block = pl.program_id(0), pl.program_id(1)

    @pl.when(block == 0)
    def _():
        for pair in range(pairs):
            span = slice(pair * 2 * HD, (pair + 1) * 2 * HD)
            kt_ref[span, :] = flip(k_ref[:, span]).astype(jnp.bfloat16)
        dk_ref[...] = jnp.zeros_like(dk_ref)
        dv_ref[...] = jnp.zeros_like(dv_ref)
        if spec["bias"]:
            spread_bias(bias_ref, tiles_ref)
            dtiles_ref[...] = jnp.zeros_like(dtiles_ref)

    def run(first, count):
        starts = [(first + tile) * kb for tile in range(count)]
        if spec["skip"]:
            starts = [pl.multiple_of(start, kb) for start in starts]
        for pair in range(pairs):
            span = slice(pair * 2 * HD, (pair + 1) * 2 * HD)
            parts = head_parts(q_ref[:, span])
            dparts = head_parts(do_ref[:, span])
            lse = lse_ref[pair]
            stacked = jnp.concatenate(parts, axis=0)
            dstacked = jnp.concatenate(dparts, axis=0)
            deltas = []
            for head in range(2):
                number = 2 * pair + head
                delta = None
                for tile in range(count):
                    here = pl.ds(starts[tile], kb)
                    s = dot_rows(k_ref[here, span], parts[head])
                    if spec["bias"]:
                        s = s + tile_bias(spec, number, first + tile, block, tiles_ref)
                    mask = tile_mask(spec, first + tile, block, segk_ref, segq_ref)
                    p = jnp.exp(jnp.where(mask, s, MASKED) - lse[head : head + 1])
                    dp = dot_rows(v_ref[here, span], dparts[head])
                    p_ref[number, tile] = p
                    dp_ref[number, tile] = dp
                    part = fold_rows(p * dp, jnp.add)
                    delta = part if delta is None else delta + part
                deltas.append(jnp.sum(delta, axis=0, keepdims=True))
            dquery = [None, None]
            for tile in range(count):
                here = pl.ds(starts[tile], kb)
                weights, lows = [], []
                for head in range(2):
                    number = 2 * pair + head
                    p = p_ref[number, tile]
                    ds = p * (dp_ref[number, tile] - deltas[head])
                    if spec["bias"]:
                        rows, lanes = kb // TILE, qb // TILE
                        for row in range(rows):
                            for lane in range(lanes):
                                index = band_index(
                                    block * lanes + lane, (first + tile) * rows + row
                                )
                                dtiles_ref[number, index] += ds[
                                    row * TILE : (row + 1) * TILE,
                                    lane * TILE : (lane + 1) * TILE,
                                ]
                    low = ds.astype(jnp.bfloat16)
                    weights.append(p.astype(jnp.bfloat16))
                    lows.append(low)
                    rows = slice(number * HD, (number + 1) * HD)
                    part = dot_plain(kt_ref[rows, here], low)
                    dquery[head] = part if tile == 0 else dquery[head] + part
                dv_ref[here, span] += dot_plain(jnp.concatenate(weights, axis=1), dstacked)
                dk_ref[here, span] += dot_plain(jnp.concatenate(lows, axis=1), stacked)
            dq_ref[:, span] = flip(jnp.concatenate(dquery, axis=0)).astype(jnp.bfloat16)

    for_counts(spec, bounds_ref[0, block], bounds_ref[1, block], run)

    @pl.when(block == pl.num_programs(1) - 1)
    def _():
        width = pairs * 2 * HD
        column = pl.multiple_of(group * width, width)
        dkv_ref[:, pl.ds(column, width)] = dk_ref[...].astype(jnp.bfloat16)
        column = pl.multiple_of((pl.num_programs(0) + group) * width, width)
        dkv_ref[:, pl.ds(column, width)] = dv_ref[...].astype(jnp.bfloat16)
        if spec["bias"]:
            gather_diagonals(dtiles_ref, band_ref)


def attention_setup(queries, keyval, query_labels, key_labels, bias, causal, pairs):
    rows, keys = queries.shape[0], keyval.shape[0]
    qb, kb = min(256, rows), min(256, keys)
    skip = rows > qb
    kb = TILE if skip else kb
    pairs = pairs if skip else 2
    spec = dict(
        qb=qb,
        kb=kb,
        causal=causal,
        bias=bias is not None,
        pairs=pairs,
        tiles=keys // kb,
        skip=skip,
    )
    bounds = jnp.zeros((2, 1), jnp.int32)
    if skip:
        bounds = key_bounds(query_labels, key_labels, qb, kb)
    segq = query_labels[None, :]
    segk = jnp.broadcast_to(key_labels[:, None], (keys, TILE))
    groups = H // 2 // pairs
    width = 2 * HD * pairs
    specs = dict(
        q=pl.BlockSpec((qb, width), lambda group, block, bounds: (block, group)),
        k=pl.BlockSpec((keys, width), lambda group, block, bounds: (0, group)),
        v=pl.BlockSpec((keys, width), lambda group, block, bounds: (0, groups + group)),
        segq=pl.BlockSpec((1, qb), lambda group, block, bounds: (0, block)),
        segk=pl.BlockSpec((keys, TILE), lambda group, block, bounds: (0, 0)),
        lse=pl.BlockSpec((pairs, 2, qb), lambda group, block, bounds: (group, 0, block)),
        bias=pl.BlockSpec((2 * pairs, BAND, SPAN), lambda group, block, bounds: (group, 0, 0)),
        band=pl.BlockSpec(
            (2 * pairs, BAND, FOLD, SPAN), lambda group, block, bounds: (group, 0, 0, 0)
        ),
        whole=pl.BlockSpec((keys, 2 * H * HD), lambda group, block, bounds: (0, 0)),
    )
    scores = pltpu.VMEM((2 * pairs, keys // kb, kb, qb), jnp.float32)
    return spec, bounds, segq, segk, specs, (groups, rows // qb), scores


def attend_forward(queries, keyval, query_labels, key_labels, bias, causal):
    spec, bounds, segq, segk, specs, grid, scores = attention_setup(
        queries, keyval, query_labels, key_labels, bias, causal, 2
    )
    rows, keys = queries.shape[0], keyval.shape[0]
    work = H * rows * keys
    extra = ([specs["bias"]], [bias]) if bias is not None else ([], [])
    tiles = [pltpu.VMEM((2 * spec["pairs"], BAND, TILE, TILE), jnp.float32)] * len(extra[0])
    return pl.pallas_call(
        functools.partial(forward_kernel, spec),
        out_shape=(
            jax.ShapeDtypeStruct((rows, H * HD), jnp.bfloat16),
            jax.ShapeDtypeStruct((H // 2, 2, rows), jnp.float32),
        ),
        grid_spec=pltpu.PrefetchScalarGridSpec(
            num_scalar_prefetch=1,
            grid=grid,
            in_specs=[specs["q"], specs["k"], specs["v"], specs["segq"], specs["segk"]]
            + extra[0],
            out_specs=[specs["q"], specs["lse"]],
            scratch_shapes=[
                scores,
                pltpu.VMEM((2 * HD * spec["pairs"], keys), jnp.bfloat16),
            ]
            + tiles,
        ),
        compiler_params=pltpu.CompilerParams(vmem_limit_bytes=40 << 20),
        cost_estimate=pl.CostEstimate(
            flops=16 * HD * work, transcendentals=work, bytes_accessed=8 << 20
        ),
    )(bounds, queries, keyval, keyval, segq, segk, *extra[1])


def attend_backward(queries, keyval, query_labels, key_labels, bias, causal, lse, dmixture):
    spec, bounds, segq, segk, specs, grid, scores = attention_setup(
        queries, keyval, query_labels, key_labels, bias, causal, 1
    )
    rows, keys = queries.shape[0], keyval.shape[0]
    work = H * rows * keys
    extra = ([specs["bias"]], [bias]) if bias is not None else ([], [])
    tiles = [pltpu.VMEM((2 * spec["pairs"], BAND, TILE, TILE), jnp.float32)] * len(extra[0])
    band = (
        [jax.ShapeDtypeStruct((H, BAND, FOLD, SPAN), jnp.float32)] if bias is not None else []
    )
    out = pl.pallas_call(
        functools.partial(backward_kernel, spec),
        out_shape=[
            jax.ShapeDtypeStruct((rows, H * HD), jnp.bfloat16),
            jax.ShapeDtypeStruct((keys, 2 * H * HD), jnp.bfloat16),
        ]
        + band,
        grid_spec=pltpu.PrefetchScalarGridSpec(
            num_scalar_prefetch=1,
            grid=grid,
            in_specs=[
                specs["q"],
                specs["k"],
                specs["v"],
                specs["q"],
                specs["lse"],
                specs["segq"],
                specs["segk"],
            ]
            + extra[0],
            out_specs=[specs["q"], specs["whole"]] + [specs["band"]] * len(band),
            scratch_shapes=[
                scores,
                scores,
                pltpu.VMEM((keys, 2 * HD * spec["pairs"]), jnp.float32),
                pltpu.VMEM((keys, 2 * HD * spec["pairs"]), jnp.float32),
                pltpu.VMEM((2 * HD * spec["pairs"], keys), jnp.bfloat16),
            ]
            + tiles
            + tiles,
        ),
        compiler_params=pltpu.CompilerParams(vmem_limit_bytes=48 << 20),
        cost_estimate=pl.CostEstimate(
            flops=40 * HD * work, transcendentals=work, bytes_accessed=16 << 20
        ),
    )(bounds, queries, keyval, keyval, dmixture, lse, segq, segk, *extra[1])
    return (out[0], out[1], out[2] if bias is not None else None)


def product(former, latter):
    return jnp.dot(former, latter, preferred_element_type=jnp.float32)


def transpose_product(former, latter):
    return lax.dot_general(
        former, latter, (((0,), (0,)), ((), ())), preferred_element_type=jnp.float32
    )


def product_transposed(former, latter):
    return lax.dot_general(
        former, latter, (((1,), (1,)), ((), ())), preferred_element_type=jnp.float32
    )


def smooth_gate(value):
    return jax.nn.gelu(value, approximate=True)


def norm_forward(stream, norm_gain):
    return (
        stream * lax.rsqrt(jnp.mean(stream * stream, axis=-1, keepdims=True) + EPSILON) * norm_gain
    )


def attention_forward(stream, norm_gain, wquery, wkeyval, wproj, layout, memory):
    normed = norm_forward(stream, norm_gain).astype(jnp.bfloat16)
    queries = product(normed, wquery).astype(jnp.bfloat16)
    source = normed if memory is None else memory
    keyval = product(source, wkeyval).astype(jnp.bfloat16)
    mixture, logsum = attend_forward(queries, keyval, *layout)
    return (stream + product(mixture, wproj), (normed, queries, keyval, mixture, logsum))


def attention_backward(
    grads, names, stream, norm_gain, wquery, wkeyval, wproj, layout, memory, stored, gradient
):
    normed, queries, keyval, mixture, logsum = stored
    gradient_low = gradient.astype(jnp.bfloat16)
    grads.add(names[2], mixture, gradient_low)
    dmixture = product_transposed(gradient_low, wproj).astype(jnp.bfloat16)
    dquery_low, dkeyval_low, band = attend_backward(queries, keyval, *layout, logsum, dmixture)
    source = normed if memory is None else memory
    grads.add(names[0], normed, dquery_low)
    grads.add(names[1], source, dkeyval_low)
    pulls, dsource = [(dquery_low, wquery)], None
    if memory is None:
        pulls.append((dkeyval_low, wkeyval))
    else:
        dsource = product_transposed(dkeyval_low, wkeyval)
    dstream, dgain = pull_norm(stream, norm_gain, pulls, gradient)
    return (dstream, dgain, band, dsource)


def norm_pull(gradient, value, gain, dnormed):
    scale = lax.rsqrt(jnp.mean(value * value, axis=1, keepdims=True) + EPSILON)
    pulled = dnormed * gain
    inner = jnp.mean(pulled * value, axis=1, keepdims=True)
    result = gradient + scale * pulled - value * (scale * scale * scale * inner)
    return result, fold_rows(dnormed * value * scale, jnp.add)


def add_gain(dgain_ref, dgain):
    @pl.when(pl.program_id(0) == 0)
    def _():
        dgain_ref[...] = dgain

    @pl.when(pl.program_id(0) > 0)
    def _():
        dgain_ref[...] += dgain


def pull_norm_kernel(g_ref, v_ref, gain_ref, *refs):
    *pulls, out_ref, dgain_ref = refs
    dnormed = None
    for low_ref, weight_ref in zip(pulls[::2], pulls[1::2]):
        part = dot_rows(low_ref[...], weight_ref[...])
        dnormed = part if dnormed is None else dnormed + part
    out_ref[...], dgain = norm_pull(
        g_ref[...], v_ref[...].astype(jnp.float32), gain_ref[...], dnormed
    )
    add_gain(dgain_ref, dgain)


def pull_norm(stream, norm_gain, pulls, gradient):
    rows, features = stream.shape
    block = min(256, rows)
    row = pl.BlockSpec((block, features), lambda step: (step, 0))
    specs, operands = [], []
    for low, weight in pulls:
        specs.append(pl.BlockSpec((block, low.shape[1]), lambda step: (step, 0)))
        specs.append(
            pl.BlockSpec(weight.shape, lambda step: (0, 0), pipeline_mode=pl.Buffered(1))
        )
        operands += [low, weight]
    dstream, dgain = pl.pallas_call(
        pull_norm_kernel,
        out_shape=[
            jax.ShapeDtypeStruct((rows, features), jnp.float32),
            jax.ShapeDtypeStruct((8, features), jnp.float32),
        ],
        grid=(rows // block,),
        in_specs=[row, row, pl.BlockSpec((1, features), lambda step: (0, 0))] + specs,
        out_specs=[row, pl.BlockSpec((8, features), lambda step: (0, 0))],
        compiler_params=pltpu.CompilerParams(vmem_limit_bytes=40 << 20),
        cost_estimate=pl.CostEstimate(
            flops=sum(2 * rows * weight.size for _, weight in pulls),
            transcendentals=rows,
            bytes_accessed=rows * features * 12
            + sum(2 * (low.size + weight.size) for low, weight in pulls),
        ),
    )(gradient, stream, norm_gain[None, :], *operands)
    return dstream, jnp.sum(dgain, axis=0)


def feed_forward(stream, norm_gain, winner, wouter):
    normed = norm_forward(stream, norm_gain).astype(jnp.bfloat16)
    before = product(normed, winner)
    hidden = smooth_gate(before).astype(jnp.bfloat16)
    return (stream + product(hidden, wouter), (normed, before, hidden))


def feed_backward_kernel(g_ref, v_ref, gain_ref, pre_ref, wi_ref, wf_ref, *outs):
    out_ref, dpre_ref, low_ref, dgain_ref = outs
    gradient = g_ref[...]
    low = gradient.astype(jnp.bfloat16)
    low_ref[...] = low
    features, hidden = wi_ref.shape
    curve, bend = math.sqrt(2 / math.pi), 0.044715
    dnormed = None
    for start in range(0, hidden, features):
        span = slice(start, start + features)
        dhidden = dot_rows(low, wf_ref[span, :])
        value = pre_ref[:, span]
        square = value * value
        bent = jnp.tanh(value * (curve + curve * bend * square))
        slope = 0.5 * (1.0 + bent) + (0.5 * value) * (1.0 - bent * bent) * (
            curve + 3 * curve * bend * square
        )
        dpre = (dhidden * slope).astype(jnp.bfloat16)
        dpre_ref[:, span] = dpre
        part = dot_rows(dpre, wi_ref[:, span])
        dnormed = part if dnormed is None else dnormed + part
    out_ref[...], dgain = norm_pull(gradient, v_ref[...], gain_ref[...], dnormed)
    add_gain(dgain_ref, dgain)


def feed_backward(grads, names, stream, norm_gain, winner, wouter, stored, gradient):
    normed, before, hidden = stored
    rows, features = stream.shape
    wide = before.shape[1]
    block = min(256, rows)
    row = pl.BlockSpec((block, features), lambda step: (step, 0))
    row_wide = pl.BlockSpec((block, wide), lambda step: (step, 0))
    once = pl.Buffered(1)
    dstream, dbefore, low, dgain = pl.pallas_call(
        feed_backward_kernel,
        out_shape=[
            jax.ShapeDtypeStruct((rows, features), jnp.float32),
            jax.ShapeDtypeStruct((rows, wide), jnp.bfloat16),
            jax.ShapeDtypeStruct((rows, features), jnp.bfloat16),
            jax.ShapeDtypeStruct((8, features), jnp.float32),
        ],
        grid=(rows // block,),
        in_specs=[
            row,
            row,
            pl.BlockSpec((1, features), lambda step: (0, 0)),
            row_wide,
            pl.BlockSpec((features, wide), lambda step: (0, 0), pipeline_mode=once),
            pl.BlockSpec((wide, features), lambda step: (0, 0), pipeline_mode=once),
        ],
        out_specs=[row, row_wide, row, pl.BlockSpec((8, features), lambda step: (0, 0))],
        compiler_params=pltpu.CompilerParams(vmem_limit_bytes=48 << 20),
        cost_estimate=pl.CostEstimate(
            flops=4 * rows * features * wide,
            transcendentals=rows * wide,
            bytes_accessed=rows * wide * 6 + 4 * features * wide + rows * features * 14,
        ),
    )(gradient, stream, norm_gain[None, :], before, winner, wouter)
    dstream = grads.add(names[1], hidden, low, dstream)
    dstream = grads.add(names[0], normed, dbefore, dstream)
    return (dstream, jnp.sum(dgain, axis=0))


def index_bits(devices):
    return devices.bit_length() - 1


class Links:
    def __init__(self, mesh):
        self.sizes = dict(mesh.shape)
        self.bits = [("fsdp", bit) for bit in range(index_bits(self.sizes["fsdp"]))]
        self.bits += [("dp", bit) for bit in range(index_bits(self.sizes["dp"]))]

    def side(self, axis, bit):
        return lax.rem(lax.axis_index(axis) // (1 << bit), 2)

    def partner(self, axis, bit):
        return {axis: lax.axis_index(axis) + (1 - 2 * self.side(axis, bit)) * (1 << bit)}

    def orders(self):
        core, row = ("dp", 0), ("fsdp", 0)
        rest = [key for key in self.bits if key not in (core, row)]
        third = [core] + rest[1:2] + rest[:1] + [row] + rest[2:]
        return ([core] + rest[:1] + [row] + rest[1:], [core, row] + rest, third)

    def devices(self):
        return self.sizes["dp"] * self.sizes["fsdp"]

    def place(self):
        return lax.axis_index("dp") * self.sizes["fsdp"] + lax.axis_index("fsdp")


def pick(ref, lead, spot, count, side):
    return ref.at[(lead,) + (slice(None),) * spot + (side,) + (slice(None),) * (count - spot - 1)]


def fold_product(x, dy, devices):
    total = lax.dot_general(x, dy, (((0,), (0,)), ((), ())), preferred_element_type=jnp.float32)
    rows, columns = total.shape
    total = total.reshape(devices, rows // devices, columns)
    half = columns // 2
    total = jnp.concatenate([total[:, :, :half], total[:, :, half:]], axis=1)
    return total.astype(jnp.bfloat16)


def reduce_kernel(links, plan, sides, count, *refs):
    stages, chunks = len(links.bits), len(plan)
    sources, refs = refs[:count], refs[count:]
    gains_ref, tables_ref, out_ref, gains_out_ref, tables_out_ref, *refs = refs
    ring_ref, x_ref, y_ref, part_ref, come_ref, deep_ref, side_x_ref, side_y_ref, *rest = refs
    gain_rows, lanes = gains_ref.shape[0], tables_ref.shape[1]
    blocks = gains_ref.shape[1] // lanes
    sums, rest = rest[:stages], rest[stages:]
    send_sem, recv_sem, load_sem, part_sem, come_sem, side_sem = rest
    halvings = []
    for order in links.orders():
        left = list(reversed(links.bits))
        halving = []
        for key in order:
            halving.append((key, left.index(key), len(left)))
            left.remove(key)
        halvings.append(halving)
    kinds = len(halvings)

    barrier = pltpu.get_barrier_semaphore()
    for key in links.bits:
        pl.semaphore_signal(
            barrier,
            inc=1,
            device_id=links.partner(*key),
            device_id_type=pl.DeviceIdType.MESH,
        )
    pl.semaphore_wait(barrier, stages)

    def source(stage, chunk, kind, away):
        key, spot, width = halvings[kind][stage]
        side = links.side(*key)
        ref, lead = (ring_ref, lax.rem(chunk, HOLD)) if stage == 0 else (sums[stage - 1], chunk)
        return pick(ref, lead, spot, width, 1 - side if away else side)

    def send(stage, chunk, kind):
        key, _, _ = halvings[kind][stage]
        return pltpu.make_async_remote_copy(
            src_ref=source(stage, chunk, kind, True),
            dst_ref=sums[stage].at[chunk],
            send_sem=send_sem.at[stage, chunk],
            recv_sem=recv_sem.at[stage, chunk],
            device_id=links.partner(*key),
            device_id_type=pl.DeviceIdType.MESH,
        )

    def trade(stage):
        return pltpu.make_async_remote_copy(
            src_ref=part_ref.at[stage],
            dst_ref=come_ref.at[stage],
            send_sem=part_sem.at[stage],
            recv_sem=come_sem.at[stage],
            device_id=links.partner(*links.bits[stage]),
            device_id_type=pl.DeviceIdType.MESH,
        )

    def loads(chunk):
        item = plan[chunk]
        if item[0] == "chunk":
            _, which, index = item
            return [
                pltpu.make_async_copy(
                    sources[which].at[index], ring_ref.at[chunk % HOLD], load_sem.at[chunk % 2, 0]
                )
            ]
        if item[0] == "kept":
            return [
                pltpu.make_async_copy(
                    deep_ref.at[item[1]], ring_ref.at[chunk % HOLD], load_sem.at[chunk % 2, 0]
                )
            ]
        _, rows, *operands = item
        slot = chunk % 2
        result = []
        for place, (which, column) in enumerate(operands):
            buffer = (x_ref, y_ref)[place]
            width = buffer.shape[2]
            result.append(
                pltpu.make_async_copy(
                    sources[which].at[:, column * width : (column + 1) * width],
                    buffer.at[slot, :rows],
                    load_sem.at[slot, place],
                )
            )
        return result

    def side_loads(side):
        width = x_ref.shape[2]
        return [
            pltpu.make_async_copy(
                sources[which].at[:, column * width : (column + 1) * width],
                (side_x_ref, side_y_ref)[place],
                side_sem.at[place],
            )
            for place, (which, column) in enumerate(sides[side])
        ]

    def make_side(side):
        deep = len(sides)
        total = lax.dot_general(
            side_x_ref[...],
            side_y_ref[...],
            (((0,), (0,)), ((), ())),
            preferred_element_type=jnp.float32,
        )
        rows, columns = total.shape
        half, r = columns // 2, ring_ref.shape[-2] // 2
        total = total.reshape(rows // deep // r, deep, r, columns)
        spot = tuple((side >> bit) & 1 for bit in reversed(range(index_bits(deep))))
        for part in range(deep):
            piece = total[:, part]
            piece = jnp.concatenate([piece[:, :, :half], piece[:, :, half:]], axis=1)
            target = (part,) + spot
            deep_ref[target] = piece.astype(jnp.bfloat16).reshape(
                deep_ref.shape[len(target) :]
            )

    sizes = sorted({item[1] for item in plan if item[0] == "product"})

    def step(group, carry):
        for stage in range(stages):

            @pl.when(group == stage + 1)
            def _():
                trade(stage).wait()
                total = part_ref[stage] + come_ref[stage]
                if stage < stages - 1:
                    part_ref[stage + 1] = total
                    trade(stage + 1).start()
                else:
                    for block in range(blocks):
                        gains_out_ref[:, block * lanes : (block + 1) * lanes] = total[
                            block * gain_rows : (block + 1) * gain_rows
                        ]
                    tables_out_ref[...] = total[blocks * gain_rows :]

        for turn in range(kinds):
            now = group * kinds + turn

            for stage in range(stages):
                chunk = now - DELAY * (stage + 1)
                kind = (turn - DELAY * (stage + 1)) % kinds

                @pl.when((chunk >= 0) & (chunk < chunks))
                def _():
                    send(stage, chunk, kind).wait()
                    mine = source(stage, chunk, kind, False)[...]
                    if stage < stages - 1:
                        sums[stage][chunk] = sums[stage][chunk] + mine
                        send(stage + 1, chunk, kind).start()
                    else:
                        out_ref[chunk] = sums[stage][chunk].astype(jnp.float32) + mine.astype(
                            jnp.float32
                        )

            for chunk in range(turn, chunks, kinds):

                @pl.when(now == chunk)
                def _():
                    for load in loads(chunk):
                        load.wait()

            for rows in sizes:
                spots = [spot for spot, item in enumerate(plan) if item[:2] == ("product", rows)]

                @pl.when((now >= spots[0]) & (now <= spots[-1]))
                def _():
                    slot = lax.rem(now, 2)
                    made = fold_product(x_ref[slot, :rows], y_ref[slot, :rows], links.devices())
                    ring_ref[lax.rem(now, HOLD)] = made.reshape(ring_ref.shape[1:])

            @pl.when(now < chunks)
            def _():
                send(0, now, turn).start()

            for side in range(len(sides)):
                spot = 2 * side + 2

                if (spot - 1) % kinds == turn:

                    @pl.when(now == spot - 1)
                    def _():
                        for load in side_loads(side):
                            load.start()

                if spot % kinds == turn:

                    @pl.when(now == spot)
                    def _():
                        for load in side_loads(side):
                            load.wait()
                        make_side(side)

            for chunk in range((turn + 1) % kinds, chunks, kinds):

                @pl.when(now + 1 == chunk)
                def _():
                    for load in loads(chunk):
                        load.start()

        return carry

    for load in loads(0):
        load.start()
    part_ref[0] = jnp.concatenate(
        [gains_ref[:, block * lanes : (block + 1) * lanes] for block in range(blocks)]
        + [tables_ref[...]],
        axis=0,
    )
    trade(0).start()
    slots = chunks + DELAY * stages
    lax.fori_loop(0, (slots + kinds - 1) // kinds, step, 0)


def reduce_chunks(links, plan, sides, sources, small, shape, width, collective_id):
    gains, tables = small
    value = (gains.size // tables.shape[1] + tables.shape[0], tables.shape[1])
    stages, chunks = len(links.bits), len(plan)
    sums = [
        pltpu.VMEM((chunks,) + (2,) * (stages - 1 - stage) + shape, jnp.bfloat16)
        for stage in range(stages)
    ]
    rows = max([item[1] for item in plan if item[0] == "product"] + [16])
    return pl.pallas_call(
        functools.partial(reduce_kernel, links, plan, sides, len(sources)),
        out_shape=[
            jax.ShapeDtypeStruct((chunks,) + shape, jnp.float32),
            jax.ShapeDtypeStruct(gains.shape, jnp.float32),
            jax.ShapeDtypeStruct(tables.shape, jnp.float32),
        ],
        in_specs=[pl.BlockSpec(memory_space=pltpu.HBM)] * len(sources)
        + [pl.BlockSpec(memory_space=pltpu.VMEM)] * 2,
        out_specs=[pl.BlockSpec(memory_space=pltpu.VMEM)] * 3,
        scratch_shapes=[
            pltpu.VMEM((HOLD,) + (2,) * stages + shape, jnp.bfloat16),
            pltpu.VMEM((2, rows, width), jnp.bfloat16),
            pltpu.VMEM((2, rows, width), jnp.bfloat16),
            pltpu.VMEM((stages,) + value, jnp.float32),
            pltpu.VMEM((stages,) + value, jnp.float32),
            pltpu.VMEM((max(1, len(sides)),) + (2,) * stages + shape, jnp.bfloat16),
            pltpu.VMEM((rows, width), jnp.bfloat16),
            pltpu.VMEM((rows, width), jnp.bfloat16),
        ]
        + sums
        + [
            pltpu.SemaphoreType.DMA((stages, chunks)),
            pltpu.SemaphoreType.DMA((stages, chunks)),
            pltpu.SemaphoreType.DMA((2, 2)),
            pltpu.SemaphoreType.DMA((stages,)),
            pltpu.SemaphoreType.DMA((stages,)),
            pltpu.SemaphoreType.DMA((2,)),
        ],
        compiler_params=pltpu.CompilerParams(
            collective_id=collective_id, has_side_effects=True, vmem_limit_bytes=60 << 20
        ),
    )(*sources, gains, tables)


def fold_grad(grad, devices, width):
    rows, columns = grad.shape
    deep, wide = rows // width, columns // width
    r = rows // devices // deep
    grad = grad.astype(jnp.bfloat16).reshape(devices, deep, r, wide, 2, width // 2)
    return grad.transpose(1, 3, 0, 4, 2, 5).reshape(deep * wide, devices, 2 * r, width // 2)


def unfold_share(chunks, rows, columns):
    count, folded, half = chunks.shape
    deep, wide = rows * 2 // folded, columns // (2 * half)
    chunks = chunks.reshape(deep, wide, 2, folded // 2, half)
    return chunks.transpose(0, 3, 1, 2, 4).reshape(rows, columns)


def gather_kernel(links, units, count, *refs):
    shards, small_ref, refs = refs[:count], refs[count], refs[count + 1 :]
    wholes, other_ref, refs = refs[:count], refs[count], refs[count + 1 :]
    held, (send_sem, recv_sem, local_sem, small_sem) = refs[:count], refs[count:]
    core, mesh_id = ("dp", 0), pl.DeviceIdType.MESH
    keys = [("dp", 1), ("dp", 2), core]
    orders = [[keys[0], keys[1], core], [keys[1], keys[0], core]]
    row = ("fsdp", 0)
    place = lax.axis_index("fsdp")

    barrier = pltpu.get_barrier_semaphore()
    for key in [row] + keys:
        pl.semaphore_signal(
            barrier, inc=1, device_id=links.partner(*key), device_id_type=mesh_id
        )
    pl.semaphore_wait(barrier, 1 + len(keys))

    def piece(known):
        return tuple(slice(None) if key in known else links.side(*key) for key in keys)

    def send(stage, unit):
        order = orders[unit % 2]
        number, rows, columns = units[unit]
        if stage == 0:
            key, where = row, piece([])
            src = shards[number].at[where + (rows, columns)]
        else:
            key, where = order[stage - 1], piece(order[: stage - 1])
            src = wholes[number].at[(1 - place,) + where + (rows, columns)]
        dst = wholes[number].at[
            (place if stage == 0 else 1 - place,) + where + (rows, columns)
        ]
        return pltpu.make_async_remote_copy(
            src_ref=src,
            dst_ref=dst,
            send_sem=send_sem.at[stage, unit],
            recv_sem=recv_sem.at[stage, unit],
            device_id=links.partner(*key),
            device_id_type=mesh_id,
        )

    def load(number):
        return pltpu.make_async_copy(shards[number], held[number], local_sem.at[0, number])

    def keep(number):
        return pltpu.make_async_copy(
            held[number], wholes[number].at[place], local_sem.at[1, number]
        )

    trade = pltpu.make_async_remote_copy(
        src_ref=small_ref,
        dst_ref=other_ref,
        send_sem=small_sem.at[0],
        recv_sem=small_sem.at[1],
        device_id=links.partner(*row),
        device_id_type=mesh_id,
    )
    stages = 1 + len(keys)
    for unit in range(len(units)):
        send(0, unit).start()
    for number in range(count):
        load(number).start()
    trade.start()
    for slot in range(len(units) + LAG * (stages - 1)):
        for stage in range(stages):
            unit = slot - LAG * stage
            if 0 <= unit < len(units):
                send(stage, unit).wait()
                if stage + 1 < stages:
                    send(stage + 1, unit).start()
        if slot < count:
            load(slot).wait()
            keep(slot).start()
    for number in range(count):
        keep(number).wait()
    trade.wait()


def gather_units(shards, width):
    least = min(shard.shape[0] for shard in shards)
    units = []
    for number, shard in enumerate(shards):
        deep, wide = shard.shape[0] // least, shard.shape[1] // width
        rows = shard.shape[0] // 8 // deep
        for part in range(deep):
            for column in range(wide):
                units.append(
                    (
                        number,
                        slice(part * rows, (part + 1) * rows),
                        slice(column * width, (column + 1) * width),
                    )
                )
    return units


def gather_weights(links, shards, small, collective_id):
    count = len(shards)
    units = gather_units(shards, shards[0].shape[1])
    split = [
        shard.reshape(2, 2, 2, shard.shape[0] // 8, shard.shape[1]) for shard in shards
    ]
    *wholes, other = pl.pallas_call(
        functools.partial(gather_kernel, links, units, count),
        out_shape=[jax.ShapeDtypeStruct((2,) + piece.shape, piece.dtype) for piece in split]
        + [jax.ShapeDtypeStruct(small.shape, small.dtype)],
        in_specs=[pl.BlockSpec(memory_space=pltpu.HBM)] * (count + 1),
        out_specs=[pl.BlockSpec(memory_space=pltpu.HBM)] * (count + 1),
        scratch_shapes=[pltpu.VMEM(piece.shape, piece.dtype) for piece in split]
        + [
            pltpu.SemaphoreType.DMA((4, len(units))),
            pltpu.SemaphoreType.DMA((4, len(units))),
            pltpu.SemaphoreType.DMA((2, count)),
            pltpu.SemaphoreType.DMA((2,)),
        ],
        compiler_params=pltpu.CompilerParams(
            collective_id=collective_id, has_side_effects=True, vmem_limit_bytes=60 << 20
        ),
    )(*split, small)
    wholes = [
        whole.reshape(2 * shard.shape[0], shard.shape[1]) for whole, shard in zip(wholes, shards)
    ]
    first = lax.axis_index("fsdp") == 0
    small = jnp.concatenate([jnp.where(first, small, other), jnp.where(first, other, small)])
    return wholes, small


def weight_kernel(deep, x_ref, dy_ref, *rest):
    out_ref = rest[-1]
    total = lax.dot_general(
        x_ref[...], dy_ref[...], (((0,), (0,)), ((), ())), preferred_element_type=jnp.float32
    )
    half = total.shape[1] // 2
    rows = out_ref.shape[2] // 2
    total = total.reshape(out_ref.shape[1], deep, rows, 2 * half)
    for part in range(deep):
        piece = total[:, part]
        piece = jnp.concatenate([piece[:, :, :half], piece[:, :, half:]], axis=1)
        out_ref[part] = piece.astype(jnp.bfloat16)


def weight_chunks(x, dy, chunks, start, count, devices, width):
    rows, deep, wide = x.shape[0], x.shape[1] // width, dy.shape[1] // width
    r = width // devices
    if deep == 1:
        specs = [
            pl.BlockSpec((rows, width), lambda w: (0, 0)),
            pl.BlockSpec((rows, width), lambda w: (0, w)),
        ]
        out_spec = pl.BlockSpec((1, devices, 2 * r, width // 2), lambda w: (start + w, 0, 0, 0))
    else:
        specs = [
            pl.BlockSpec((rows, width), lambda w: (0, w)),
            pl.BlockSpec((rows, width), lambda w: (0, 0)),
        ]
        out_spec = pl.BlockSpec(
            (deep, devices // deep, 2 * r, width // 2), lambda w: (start // deep, w, 0, 0)
        )
    extra = [] if chunks is None else [chunks]
    return pl.pallas_call(
        functools.partial(weight_kernel, deep),
        out_shape=jax.ShapeDtypeStruct((count, devices, 2 * r, width // 2), jnp.bfloat16),
        grid=(max(deep, wide),),
        in_specs=specs + [pl.BlockSpec(memory_space=pltpu.HBM)] * len(extra),
        out_specs=out_spec,
        input_output_aliases={2: 0} if extra else {},
        compiler_params=pltpu.CompilerParams(vmem_limit_bytes=40 << 20),
        cost_estimate=pl.CostEstimate(
            flops=2 * rows * x.shape[1] * dy.shape[1],
            transcendentals=0,
            bytes_accessed=2 * (x.size + dy.size + x.shape[1] * dy.shape[1]),
        ),
    )(x, dy, *extra)


class Gradients:
    def __init__(self, links, width):
        self.links, self.width = links, width
        self.products, self.scattered = {}, {}

    def add(self, name, x, dy, carry=None):
        if name in OFFLOADED:
            grad = transpose_product(x, dy).astype(jnp.bfloat16)
            if carry is not None:
                grad, carry = lax.optimization_barrier((grad, carry))
            self.scattered[name] = lax.psum_scatter(
                grad, ("dp", "fsdp"), scatter_dimension=0, tiled=True
            )
        else:
            self.products[name] = (x, dy)
        return carry

    def shares(self, collective_id, small):
        width, devices = self.width, self.links.devices()
        r = width // devices
        aligned = r % 8 == 0
        names = list(self.products)
        size = {name: self.products[name][0].shape for name in names}
        deep = {name: size[name][1] // width for name in names}
        tallest = max(rows for rows, _ in size.values())
        split = [name for name in names if deep[name] > 1 and size[name][0] == tallest][:1]
        if not aligned or 2 * max(deep.values()) + 2 > len(names) + 4:
            split = []
        names.sort(key=lambda name: (name in split, deep[name] == 1, size[name][0]))
        sides = []
        plan, sources, known = [], [], {}

        def number(array):
            if id(array) not in known:
                known[id(array)] = len(sources)
                sources.append(array)
            return known[id(array)]

        shapes = {}
        for name in names:
            x, dy = self.products[name]
            shapes[name] = (x.shape[1] // devices, dy.shape[1])
            wide = dy.shape[1] // width
            if aligned and deep[name] == 1:
                for part in range(wide):
                    plan.append(("product", x.shape[0], (number(x), 0), (number(dy), part)))
                continue
            count = deep[name] * wide
            if name in split:
                sides += [((number(x), part), (number(dy), 0)) for part in range(count)]
                plan += [("kept", part) for part in range(count)]
                continue
            if aligned:
                made = weight_chunks(x, dy, None, 0, count, devices, width)
            else:
                made = fold_grad(transpose_product(x, dy), devices, width)
            made = made.reshape((count,) + (2,) * len(self.links.bits) + made.shape[2:])
            for part in range(count):
                plan.append(("chunk", number(made), part))
        shares, *total = reduce_chunks(
            self.links, plan, sides, sources, small, (2 * r, width // 2), width, collective_id
        )
        if aligned:
            scattered = list(self.scattered.values())
            result = pl.pallas_call(
                functools.partial(unfold_kernel, width, len(scattered)),
                out_shape=[jax.ShapeDtypeStruct(shape, jnp.float32) for shape in shapes.values()]
                + [jax.ShapeDtypeStruct(share.shape, jnp.float32) for share in scattered],
            )(shares, *scattered)
            return dict(zip(list(shapes) + list(self.scattered), result)), total
        result = {name: share.astype(jnp.float32) for name, share in self.scattered.items()}
        start = 0
        for name, shape in shapes.items():
            count = deep[name] * shape[1] // width
            result[name] = unfold_share(shares[start : start + count], *shape)
            start += count
        return result, total


def unfold_kernel(width, count, shares_ref, *refs):
    scattered, out_refs = refs[:count], refs[count:]
    if count:
        for scattered_ref, out_ref in zip(scattered, out_refs[-count:]):
            out_ref[...] = scattered_ref[...].astype(jnp.float32)
        out_refs = out_refs[:-count]
    chunk, r, half = 0, shares_ref.shape[1] // 2, width // 2
    for out_ref in out_refs:
        for row in range(0, out_ref.shape[0], r):
            for column in range(0, out_ref.shape[1], width):
                for part in range(2):
                    out_ref[
                        row : row + r, column + part * half : column + (part + 1) * half
                    ] = shares_ref[chunk, part * r : (part + 1) * r, :]
                chunk += 1


def body(
    links,
    enc_tokens,
    dec_tokens,
    enc_segments,
    dec_segments,
    enc_upstream,
    dec_upstream,
    encoder_query,
    encoder_keyval,
    encoder_proj,
    encoder_inner,
    encoder_outer,
    encoder_gains,
    encoder_table,
    decoder_query,
    decoder_keyval,
    decoder_proj,
    cross_query,
    cross_keyval,
    cross_proj,
    decoder_inner,
    decoder_outer,
    decoder_gains,
    decoder_table,
):
    small = jnp.concatenate(
        [encoder_gains, decoder_gains]
        + [
            jnp.concatenate([encoder_table, decoder_table], axis=0).reshape(
                encoder_gains.shape[0], -1
            )
        ],
        axis=1,
    )
    shards = [
        encoder_query,
        encoder_keyval,
        encoder_proj,
        encoder_inner,
        encoder_outer,
        decoder_query,
        decoder_keyval,
        decoder_proj,
        cross_query,
        cross_keyval,
        cross_proj,
        decoder_inner,
        decoder_outer,
    ]
    shards = dict(zip(NAMES, shards))
    later = [shards.pop(name) for name in LATER]
    wholes, small = gather_weights(links, list(shards.values()), small, 1)
    weights = dict(zip(shards, wholes))
    enc_gains = small[:, 0:2].astype(jnp.float32)
    dec_gains = small[:, 2:5].astype(jnp.float32)
    tables = small[:, 5:].reshape(2, 2, NB // 2, H)
    enc_bias = band_bias(tables[:, 0].reshape(NB, H), encoder_bucket)
    dec_bias = band_bias(tables[:, 1].reshape(NB, H), decoder_bucket)

    weights["equery"], *later = lax.optimization_barrier((weights["equery"], *later))
    for name, shard in zip(LATER, later):
        weights[name] = lax.all_gather(shard, "fsdp", axis=0, tiled=True)
    grads = Gradients(links, encoder_query.shape[1])

    enc_layout = (enc_segments, enc_segments, enc_bias, False)
    dec_layout = (dec_segments, dec_segments, dec_bias, True)
    cross_layout = (dec_segments, enc_segments, None, False)

    enc_stream = enc_tokens.astype(jnp.float32)
    enc_middle, enc_self = attention_forward(
        enc_stream, enc_gains[:, 0], weights["equery"], weights["ekeyval"], weights["eproj"], enc_layout, None
    )
    enc_final, enc_ffn = feed_forward(enc_middle, enc_gains[:, 1], weights["einner"], weights["eouter"])
    memory = enc_final.astype(jnp.bfloat16)

    dec_stream = dec_tokens.astype(jnp.float32)
    after_self, dec_self = attention_forward(
        dec_stream, dec_gains[:, 0], weights["dquery"], weights["dkeyval"], weights["dproj"], dec_layout, None
    )
    after_cross, dec_cross = attention_forward(
        after_self, dec_gains[:, 1], weights["cquery"], weights["ckeyval"], weights["cproj"], cross_layout, memory
    )
    dec_final, dec_ffn = feed_forward(after_cross, dec_gains[:, 2], weights["dinner"], weights["douter"])


    dec_live = (dec_segments >= 0).astype(jnp.float32)[:, None]
    gradient = dec_upstream.astype(jnp.float32) * dec_live
    gradient, dgain_ffn = feed_backward(
        grads, ("dinner", "douter"), after_cross, dec_gains[:, 2], weights["dinner"], weights["douter"], dec_ffn, gradient
    )
    gradient, dgain_cross, _, memory_grad = (
        attention_backward(
            grads,
            ("cquery", "ckeyval", "cproj"),
            after_self,
            dec_gains[:, 1],
            weights["cquery"],
            weights["ckeyval"],
            weights["cproj"],
            cross_layout,
            memory,
            dec_cross,
            gradient,
        )
    )
    dec_gradient, dgain_self, dec_band, _ = (
        attention_backward(
            grads,
            ("dquery", "dkeyval", "dproj"),
            dec_tokens,
            dec_gains[:, 0],
            weights["dquery"],
            weights["dkeyval"],
            weights["dproj"],
            dec_layout,
            None,
            dec_self,
            gradient,
        )
    )

    enc_live = (enc_segments >= 0).astype(jnp.float32)[:, None]
    gradient = enc_upstream.astype(jnp.float32) * enc_live + memory_grad
    gradient, egain_ffn = feed_backward(
        grads, ("einner", "eouter"), enc_middle, enc_gains[:, 1], weights["einner"], weights["eouter"], enc_ffn, gradient
    )
    enc_gradient, egain_self, enc_band, _ = (
        attention_backward(
            grads,
            ("equery", "ekeyval", "eproj"),
            enc_tokens,
            enc_gains[:, 0],
            weights["equery"],
            weights["ekeyval"],
            weights["eproj"],
            enc_layout,
            None,
            enc_self,
            gradient,
        )
    )

    table_grads = jnp.concatenate(
        [
            band_table_grad(enc_band, encoder_bucket),
            band_table_grad(dec_band, decoder_bucket),
        ],
        axis=0,
    )
    table_grads = jnp.pad(table_grads, ((0, 0), (0, TILE - H)))
    none = jnp.zeros_like(egain_self)
    gain_grads = jnp.stack(
        [egain_self, egain_ffn, dgain_self, dgain_cross, dgain_ffn, none, none, none]
    )
    shares, (gain_grads, table_grads) = grads.shares(0, (gain_grads, table_grads))
    own = gain_grads.shape[1] // links.devices()
    gains_share = lax.dynamic_slice_in_dim(gain_grads, links.place() * own, own, 1).T
    tables_grad = (table_grads[:NB, :H], table_grads[NB:, :H])
    return (
        memory,
        dec_final.astype(jnp.bfloat16),
        enc_gradient,
        dec_gradient,
        shares["equery"],
        shares["ekeyval"],
        shares["eproj"],
        shares["einner"],
        shares["eouter"],
        gains_share[:, 0:2],
        tables_grad[0],
        shares["dquery"],
        shares["dkeyval"],
        shares["dproj"],
        shares["cquery"],
        shares["ckeyval"],
        shares["cproj"],
        shares["dinner"],
        shares["douter"],
        gains_share[:, 2:5],
        tables_grad[1],
    )


def solution(mesh):
    in_specs = (
        P(("dp", "fsdp"), None),
        P(("dp", "fsdp"), None),
        P(("dp", "fsdp")),
        P(("dp", "fsdp")),
        P(("dp", "fsdp"), None),
        P(("dp", "fsdp"), None),
        P("fsdp", None),
        P("fsdp", None),
        P("fsdp", None),
        P("fsdp", None),
        P("fsdp", None),
        P("fsdp", None),
        P("fsdp", None),
        P("fsdp", None),
        P("fsdp", None),
        P("fsdp", None),
        P("fsdp", None),
        P("fsdp", None),
        P("fsdp", None),
        P("fsdp", None),
        P("fsdp", None),
        P("fsdp", None),
        P("fsdp", None),
    )
    out_specs = (
        P(("dp", "fsdp"), None),
        P(("dp", "fsdp"), None),
        P(("dp", "fsdp"), None),
        P(("dp", "fsdp"), None),
        P(("dp", "fsdp"), None),
        P(("dp", "fsdp"), None),
        P(("dp", "fsdp"), None),
        P(("dp", "fsdp"), None),
        P(("dp", "fsdp"), None),
        P(("dp", "fsdp"), None),
        P(),
        P(("dp", "fsdp"), None),
        P(("dp", "fsdp"), None),
        P(("dp", "fsdp"), None),
        P(("dp", "fsdp"), None),
        P(("dp", "fsdp"), None),
        P(("dp", "fsdp"), None),
        P(("dp", "fsdp"), None),
        P(("dp", "fsdp"), None),
        P(("dp", "fsdp"), None),
        P(),
    )
    return jax.shard_map(
        functools.partial(body, Links(mesh)), mesh=mesh, in_specs=in_specs, out_specs=out_specs, check_vma=False)
```
